32 devices in a mesh: prow: 4 (over z), pcol: 8 (over y, x, core).
Axes of the slice: x: 2, y: 2, z: 4, core: 2. Of those that a mesh axis runs over, the one named last changes fastest.
Arguments:
- matrix: float32 [2048, 8192], P('prow', 'pcol'), may hold values from -6 to 6
- pivot_inverse: float32 [2, 512, 512], P(None, 'prow'), may hold values from -0.01171875 to 0.01171875
- row_live: int32 [2, 4], replicated, may hold values 0 or 1
- col_live: int32 [2, 16], replicated, may hold values 0 or 1
Outputs:
- factored: float32 [2048, 8192], P('prow', 'pcol')
The draws below stay inside these ranges and needn't reach their ends.
All inputs are finite; a program needn't handle non-finite values.
Results may differ from the reference program's by a relative error of at most 0.0001.
Values sent between devices are 32-bit elements; how exact they have to be, the bound alone decides.
A program may use at most 64 MiB of HBM per device.

```python
import jax
import jax.numpy as jnp
from jax import lax

B = 512
RB = 1
CB = 2
PANELS = 2
NBR = 4
NBC = 16
N_PROW = 4
N_PCOL = 8


def plant(result, key, least, high):
    shape = result.shape
    index_at = [jax.random.randint(jax.random.fold_in(key, axis), (), 0, shape[axis]) for axis in range(len(shape))]
    result = result.at[tuple(index_at)].set(least)
    longest = shape.index(max(shape))
    index_at[longest] = (index_at[longest] + 1) % shape[longest]
    return result.at[tuple(index_at)].set(high)


def levels(rng, dims, shards, least, high):
    def one(dim, shards_of):
        draws = jax.random.uniform(jax.random.fold_in(jax.random.fold_in(rng, 6), dim), (shards_of,), jnp.float32, least / len(shards), high / len(shards))
        return jnp.repeat(jnp.exp(draws), dims[dim] // shards_of).reshape((-1,) + (1,) * (len(dims) - dim - 1))

    level = one(*shards[0])
    for cut in shards[1:]:
        level = level * one(*cut)
    return level


def noise(rng, extent, deviation, bound, shards=(), held_as=jnp.bfloat16):
    values = deviation * jax.random.normal(rng, extent, jnp.float32)
    if shards:
        values = values * levels(rng, extent, shards, -0.22, 0.18)
    return jnp.clip(values, -bound, bound).astype(held_as)


def setup_inputs(seed: int = 0) -> dict:
    seeds = jax.random.split(jax.random.key(seed), 5)
    matrix = noise(seeds[0], (NBR * B, NBC * B), 1.0, 6.0, ((0, 4), (1, 8)), jnp.float32)
    pivot_inverse = noise(seeds[1], (PANELS, B, B), (B * B) ** -0.5, 0.01171875, ((1, 4),), jnp.float32)
    row_live = plant((jax.random.randint(seeds[2], (PANELS, NBR), 0, 4) < 3).astype(jnp.int32), jax.random.fold_in(seeds[2], 1), 0, 1)
    col_live = plant((jax.random.randint(seeds[3], (PANELS, NBC), 0, 4) < 3).astype(jnp.int32), jax.random.fold_in(seeds[3], 1), 0, 1)
    return dict(matrix=matrix, pivot_inverse=pivot_inverse, row_live=row_live, col_live=col_live)


def reference(matrix, pivot_inverse, row_live, col_live):
    block_rows = RB * N_PROW
    block_cols = CB * N_PCOL
    row_range = jnp.arange(block_rows, dtype=jnp.int32)
    col_range = jnp.arange(block_cols, dtype=jnp.int32)
    row_index = (row_range % RB) * N_PROW + row_range // RB
    col_index = (col_range % CB) * N_PCOL + col_range // CB
    for panel in range(PANELS):
        lower_mask = jnp.where(row_index > panel, jnp.take(row_live[panel], row_index), 0).astype(jnp.float32)
        upper_mask = jnp.where(col_index > panel, jnp.take(col_live[panel], col_index), 0).astype(jnp.float32)
        lower_mask = jnp.repeat(lower_mask, B)
        upper_mask = jnp.repeat(upper_mask, B)
        col_start = panel * CB * B
        row_start = panel * RB * B
        column_part = matrix[:, col_start:col_start + B]
        lower_part = jnp.dot(column_part, pivot_inverse[panel], precision=lax.Precision.HIGHEST) * lower_mask[:, None]
        upper_part = matrix[row_start:row_start + B, :] * upper_mask[None, :]
        matrix = matrix - jnp.dot(lower_part, upper_part, precision=lax.Precision.HIGHEST)
        keep_rows = jnp.repeat(row_index > panel, B)[:, None]
        matrix = matrix.at[:, col_start:col_start + B].set(jnp.where(keep_rows, lower_part, matrix[:, col_start:col_start + B]))
    return matrix
```

```python
import functools

import jax
import jax.numpy as jnp
from jax import lax
from jax.experimental import pallas as pl
from jax.experimental.pallas import tpu as pltpu
from jax.sharding import PartitionSpec as P

MESH = pl.DeviceIdType.MESH
CORES = 2
CHUNK = 256
PIECES = 16
TAIL = 4
GUESTS = 28
GRANT = 67_043_328


def split(x):
    high = x.astype(jnp.bfloat16)
    return high, (x - high.astype(jnp.float32)).astype(jnp.bfloat16)


def product(left_high, left_low, right_high, right_low):
    dot = functools.partial(jnp.dot, preferred_element_type=jnp.float32)
    return dot(left_high, right_high) + (dot(left_high, right_low) + dot(left_low, right_high))


def kernel(
    n_row, n_col, chunk, row_hbm, col_hbm, mat, piv, acc,
    row_smem, col_smem, u, p, a, guest, low, low_high, low_rest, u_high, u_rest,
    acc_sem, mask_sem, u_send, u_recv, p_send, p_recv, p_pass, p_passed, p_own,
    a_own, a_send, a_recv, t_send, t_recv, l_send, l_recv, l_pass, l_passed,
    p_up, g_in, g_recv, g_down, g_out,
):
    z, pcol = lax.axis_index("prow"), lax.axis_index("pcol")
    core, chip = lax.rem(pcol, CORES), lax.div(pcol, CORES)
    n_chip = n_col // CORES
    partner = (z, pcol + 1 - 2 * core)
    width, half = piv.shape[2], piv.shape[2] // CORES
    rows_own = piv.shape[1]
    rows_half = rows_own // CORES
    chunks = acc.shape[1] // chunk
    per_block = width // chunk
    pieces = u_send.shape[1] // chunks
    piece = width // pieces
    steps = chunks * pieces
    last = n_row - 1
    guests = guest.shape[1]
    guest_start = (chunks - 2) * pieces
    first_chip, active, both = chip == 0, z > 0, z > 1
    guest_end = guest_start + jnp.where(chip > 0, guests, 0)

    def remote(src, dst, send, recv, to):
        return pltpu.make_async_remote_copy(
            src_ref=src, dst_ref=dst, send_sem=send, recv_sem=recv, device_id=to, device_id_type=MESH
        )

    masks = [
        pltpu.make_async_copy(row_hbm, row_smem, mask_sem.at[0]),
        pltpu.make_async_copy(col_hbm, col_smem, mask_sem.at[1]),
    ]

    def columns_of(j):
        start = j * chunk
        return pl.ds(start if isinstance(j, int) else pl.multiple_of(start, 128), chunk)

    def load(j):
        return pltpu.make_async_copy(mat.at[:, columns_of(j)], acc.at[:, columns_of(j)], acc_sem.at[j])

    def pivot_own(k):
        return pltpu.make_async_copy(piv.at[k], p.at[k, pl.ds(z * rows_own, rows_own)], p_own.at[k])

    def pivot_rows(k, source):
        return p.at[k, pl.ds(pl.multiple_of(source * rows_own + core * rows_half, 8), rows_half)]

    def pivot_send(k, target, send):
        return remote(
            piv.at[k, pl.ds(pl.multiple_of(core * rows_half, 8), rows_half)],
            pivot_rows(k, z), send, p_recv.at[k, z], (target, pcol),
        )

    def pivot_relay(k, source, target):
        return remote(pivot_rows(k, source), pivot_rows(k, source), p_send.at[k, source], p_recv.at[k, source], (target, pcol))

    def pivot_landed(k, source):
        return remote(pivot_rows(k, source), pivot_rows(k, source), p_send.at[k, source], p_recv.at[k, source], (z, pcol))

    def pivot_pass(k, source):
        return remote(pivot_rows(k, source), pivot_rows(k, source), p_pass.at[k, source], p_passed.at[k, source], partner)

    def piece_of(ref, j, r):
        return ref.at[j, pl.ds(pl.multiple_of(r * piece, 8), piece)]

    def relay_copy(k, s):
        place = piece_of(u.at[k], s // pieces, s % pieces)
        return remote(place, place, u_send.at[k, s], u_recv.at[k, s], (z + 1, pcol))

    def origin_copy(k, s):
        j, r = s // pieces, s % pieces
        rows = pl.ds(pl.multiple_of(r * piece, 8), piece)
        return remote(acc.at[rows, columns_of(j)], piece_of(u.at[k], j, r), u_send.at[k, s], u_recv.at[k, s], (z + 1, pcol))

    def start_of(k):
        return jnp.where(pcol <= k, per_block * pieces, 0)

    def relay(k, begin, end):
        def body(s, carry):
            copy = relay_copy(k, s)
            copy.wait_recv()

            @pl.when(z < last)
            def _():
                copy.start()

            return carry

        lax.fori_loop(jnp.maximum(begin, start_of(k)), end, body, 0)

    def originate(k, begin, end):
        def body(s, carry):
            origin_copy(k, s).start()
            return carry

        lax.fori_loop(jnp.maximum(begin, start_of(k)), end, body, 0)

    def finish_sends(k, copy):
        def body(s, carry):
            copy(k, s).wait_send()
            return carry

        if k:
            lax.fori_loop(start_of(k), guest_start, body, 0)
            lax.fori_loop(guest_end, steps, body, 0)
        else:
            lax.fori_loop(start_of(k), steps, body, 0)

    def guest_in(i):
        rows = pl.ds(i * piece, piece)
        source = acc.at[rows, columns_of(guest_start // pieces)]
        return remote(source, guest.at[chip, i], g_in.at[i], g_recv.at[chip, i], (z, core))

    def guest_down(q, i):
        return remote(guest.at[q, i], guest.at[q, i], g_down.at[q, i], g_recv.at[q, i], (z + 1, pcol))

    def guest_out(q, i):
        target = piece_of(u.at[1], guest_start // pieces, i)
        return remote(guest.at[q, i], target, g_out.at[q, i], u_recv.at[1, guest_start + i], (z, q * CORES + core))

    def pass_guests():
        def body(t, carry):
            q, i = 1 + t // guests, t % guests
            guest_down(q, i).wait_recv()

            @pl.when(z < last)
            def _():
                guest_down(q, i).start()

            @pl.when(both)
            def _():
                guest_out(q, i).start()

            return carry

        lax.fori_loop(0, (n_chip - 1) * guests, body, 0)

    def finish_guests():
        def body(t, carry):
            q, i = 1 + t // guests, t % guests

            @pl.when(z < last)
            def _():
                guest_down(q, i).wait_send()

            @pl.when(both)
            def _():
                guest_out(q, i).wait_send()

            return carry

        lax.fori_loop(0, (n_chip - 1) * guests, body, 0)

    def own_rows():
        return pl.ds(pl.multiple_of(core * half, 8), half)

    def lower_send(k, target):
        rows = low.at[k, own_rows()]
        return remote(rows, rows, l_send.at[k, target], l_recv.at[k], (z, target * CORES + core))

    def lower_pass(k):
        rows = low.at[k, own_rows()]
        return remote(rows, rows, l_pass.at[k], l_passed.at[k], partner)

    def row_mask(k):
        return row_smem[k, z].astype(jnp.float32)

    def for_sources(k, visit):
        for distance in range(1, n_row):
            @pl.when(z - distance >= 0)
            def _():
                visit(z - distance, z + 1, z < last, z > k)

            @pl.when((z + distance <= last) & (z > k))
            def _():
                visit(z + distance, z - 1, z - 1 > k, z > k)

    def relay_pivot(k):
        def visit(source, target, onward, used):
            pivot_landed(k, source).wait_recv()

            @pl.when(onward)
            def _():
                pivot_relay(k, source, target).start()

            @pl.when(used)
            def _():
                pivot_pass(k, source).start()

        for_sources(k, visit)

    def gather_pivot(k):
        pivot_own(k).wait()
        for source in range(n_row):
            @pl.when(z != source)
            def _():
                pivot_pass(k, source).wait_recv()

    def finish_pivot(k):
        def visit(source, target, onward, used):
            @pl.when(onward)
            def _():
                pivot_relay(k, source, target).wait_send()

            @pl.when(used)
            def _():
                pivot_pass(k, source).wait_send()

        for_sources(k, visit)

    def apply_pivot(k, left):
        left_high, left_low = split(left)
        for q in range(per_block):
            columns = pl.ds(q * chunk, chunk)
            right = split(p[k, :, columns])
            low[k, own_rows(), columns] = row_mask(k) * product(left_high, left_low, *right)
        for target in range(n_chip - 1, 0, -1):
            lower_send(k, target).start()
        lower_pass(k).start()

    def take_lower(k):
        @pl.when(chip > 0)
        def _():
            lower_send(k, 0).wait_recv()
            lower_pass(k).start()

        lower_pass(k).wait_recv()
        low_high[k], low_rest[k] = split(low[k])

    def update(k, j, part=0, parts=1):
        live = col_smem[k, pcol + (j // per_block) * n_col].astype(jnp.float32)

        def run():
            depth = pl.ds(part * (width // parts), width // parts)
            u_high[depth], u_rest[depth] = split(u[k, j, depth])
            for t in range(CORES):
                rows = pl.ds(t * half, half)
                left = low_high[k, rows, depth], low_rest[k, rows, depth]
                acc[rows, columns_of(j)] -= live * product(*left, u_high[depth], u_rest[depth])

        if j < per_block:
            pl.when(pcol > k)(run)
        else:
            run()

    def store_lower(k):
        @pl.when(pcol == k)
        def _():
            acc[:, pl.ds(0, width)] = low[k]

    barrier = pltpu.get_barrier_semaphore()
    relays_guests = (z == 1) & (z < last)

    def greet(condition, device):
        @pl.when(condition)
        def _():
            pl.semaphore_signal(barrier, inc=1, device_id=device, device_id_type=MESH)

    greet(active, (z - 1, pcol))
    greet(active, partner)
    greet(active & (z < last) & first_chip, (z + 1, pcol))
    greet(active & (chip > 0), (z, core))
    for other in range(1, n_chip):
        greet(relays_guests & first_chip, (z, other * CORES + core))

    for j in range(chunks):
        load(j).start()
    for copy in masks:
        copy.start()

    @pl.when(first_chip & active)
    def _():
        for k in range(2):
            pivot_own(k).start()
        pltpu.make_async_copy(mat.at[own_rows(), pl.ds(0, width)], a.at[core], a_own).start()

    targets = (
        jnp.where(z < last, 1, 0)
        + jnp.where(active, 1, 0)
        + jnp.where(both & first_chip, 1, 0)
        + jnp.where(active & first_chip, n_chip - 1, 0)
        + jnp.where(relays_guests & (chip > 0), 1, 0)
    )
    pl.semaphore_wait(barrier, targets)

    def swap_columns():
        source = mat.at[pl.ds(pl.multiple_of((1 - core) * half, 8), half), pl.ds(0, width)]
        return remote(source, a.at[core], a_send, a_recv, partner)

    def swapped_columns():
        return remote(a.at[1 - core], a.at[1 - core], a_send, a_recv, partner)

    @pl.when(first_chip)
    def _():
        for k in range(2):
            @pl.when(z < last)
            def _():
                pivot_send(k, z + 1, p_send.at[k, z]).start()

            @pl.when(z - 1 > k)
            def _():
                pivot_send(k, z - 1, p_up.at[k]).start()

        @pl.when(active)
        def _():
            swap_columns().start()

    for j in range(chunks):
        load(j).wait()

        @pl.when(z == 0)
        def _():
            originate(0, j * pieces, (j + 1) * pieces)

    for copy in masks:
        copy.wait()

    @pl.when(active)
    def _():
        @pl.when(first_chip)
        def _():
            relay_pivot(0)
            gather_pivot(0)
            pltpu.make_async_copy(mat.at[own_rows(), pl.ds(0, width)], a.at[core], a_own).wait()
            swapped_columns().wait_recv()
            apply_pivot(0, a[0])
            relay_pivot(1)

        ahead = jnp.where(pcol == 0, steps - TAIL, per_block * pieces)
        relay(0, 0, ahead)

        @pl.when(first_chip & both)
        def _():
            top = u.at[0, pl.ds(0, per_block)]
            copy = remote(top, top, t_send, t_recv, partner)

            @pl.when(core == 1)
            def _():
                copy.start()

            gather_pivot(1)

            @pl.when(core == 0)
            def _():
                copy.wait_recv()

            live = col_smem[0, 1].astype(jnp.float32)
            left = split(low[0, own_rows()])
            for q in range(per_block):
                columns = pl.ds(q * chunk, chunk)
                a[1, :, columns] -= live * product(*left, *split(u[0, q]))
            apply_pivot(1, a[1])

            @pl.when(core == 1)
            def _():
                copy.wait_send()

        relay(0, ahead, steps - TAIL)
        take_lower(0)
        for j in range(chunks - 1):
            update(0, j)
            relay(0, steps - TAIL + j, steps - TAIL + j + 1)
        relay(0, steps - TAIL + chunks - 1, steps)

        @pl.when(z == 1)
        def _():
            @pl.when(z < last)
            def _():
                @pl.when(chip > 0)
                def _():
                    for i in range(guests):
                        guest_in(i).start()

                originate(1, 0, guest_start)
                originate(1, guest_end, steps - pieces)

                @pl.when(first_chip)
                def _():
                    pass_guests()

            update(0, chunks - 1)

            @pl.when(z < last)
            def _():
                originate(1, steps - pieces, steps)

            store_lower(0)

        @pl.when(both)
        def _():
            relay(1, 0, pieces)
            update(0, chunks - 1)
            relay(1, pieces, guest_start)
            take_lower(1)
            update(1, 0)
            relay(1, guest_end, guest_end + 4)
            update(1, 1)
            store_lower(0)
            store_lower(1)
            relay(1, guest_end + 4, steps - pieces)

            @pl.when(first_chip)
            def _():
                pass_guests()

            @pl.when(chip > 0)
            def _():
                for i in range(guests):
                    relay_copy(1, guest_start + i).wait_recv()

            for j in range(2, chunks - 1):
                update(1, j)
            for part in range(4):
                begin = steps - pieces + part * (pieces // 4)
                relay(1, begin, begin + pieces // 4)
                update(1, chunks - 1, part, 4)

    @pl.when(z == 0)
    def _():
        finish_sends(0, origin_copy)

    @pl.when(active & first_chip)
    def _():
        @pl.when((z < last) | both)
        def _():
            finish_guests()

    @pl.when((z == 1) & (z < last) & (chip > 0))
    def _():
        for i in range(guests):
            guest_in(i).wait_send()

    @pl.when(active & (z < last))
    def _():
        finish_sends(0, relay_copy)

        @pl.when(z == 1)
        def _():
            finish_sends(1, origin_copy)

        @pl.when(both)
        def _():
            finish_sends(1, relay_copy)

    @pl.when(first_chip)
    def _():
        for k in range(2):
            @pl.when(z < last)
            def _():
                pivot_send(k, z + 1, p_send.at[k, z]).wait_send()

            @pl.when(z - 1 > k)
            def _():
                pivot_send(k, z - 1, p_up.at[k]).wait_send()

            finish_pivot(k)

    @pl.when(first_chip & (z == 1))
    def _():
        pivot_own(1).wait()

    for k in range(2):
        @pl.when(z > k)
        def _():
            lower_pass(k).wait_send()

            @pl.when(first_chip)
            def _():
                for target in range(n_chip - 1, 0, -1):
                    lower_send(k, target).wait_send()
                if k == 0:
                    swap_columns().wait_send()


def dense(n_row, n_col, ident, matrix, pivot_inverse, row_live, col_live):
    rows, columns = matrix.shape
    panels, rows_own, width = pivot_inverse.shape
    chunk = min(CHUNK, width)
    chunks = columns // chunk
    steps = chunks * PIECES
    n_chip = n_col // CORES
    guests = max(1, GUESTS // n_chip)
    f32, bf16, dma = jnp.float32, jnp.bfloat16, pltpu.SemaphoreType.DMA
    return pl.pallas_call(
        functools.partial(kernel, n_row, n_col, chunk),
        out_shape=pltpu.VMEM((rows, columns), f32),
        in_specs=[pl.BlockSpec(memory_space=pltpu.HBM)] * 4,
        out_specs=pl.BlockSpec(memory_space=pltpu.VMEM),
        scratch_shapes=[
            pltpu.SMEM(row_live.shape, jnp.int32),
            pltpu.SMEM(col_live.shape, jnp.int32),
            pltpu.VMEM((panels, chunks, width, chunk), f32),
            pltpu.VMEM((panels, width, width), f32),
            pltpu.VMEM((CORES, width // CORES, width), f32),
            pltpu.VMEM((n_chip, guests, width // PIECES, chunk), f32),
            pltpu.VMEM((panels, width, width), f32),
            pltpu.VMEM((panels, width, width), bf16),
            pltpu.VMEM((panels, width, width), bf16),
            pltpu.VMEM((width, chunk), bf16),
            pltpu.VMEM((width, chunk), bf16),
            dma((chunks,)), dma((2,)),
            dma((panels, steps)), dma((panels, steps)),
            dma((panels, n_row)), dma((panels, n_row)), dma((panels, n_row)), dma((panels, n_row)),
            dma((panels,)), dma, dma, dma, dma, dma,
            dma((panels, n_col // CORES)), dma((panels,)), dma((panels,)), dma((panels,)),
            dma((panels,)), dma((guests,)), dma((n_chip, guests)), dma((n_chip, guests)), dma((n_chip, guests)),
        ],
        compiler_params=pltpu.CompilerParams(
            collective_id=ident, has_side_effects=True, vmem_limit_bytes=GRANT - 4 * rows * columns
        ),
    )(row_live, col_live, matrix, pivot_inverse)


def count(row, col, out):
    total = 0
    for k in range(row.shape[0]):
        for h in range(col.shape[1]):
            total += col[k, h]
    out[0] = lax.rem(total, 4)


def per_device(n_row, n_col, matrix, pivot_inverse, row_live, col_live):
    smem = pl.BlockSpec(memory_space=pltpu.SMEM)
    pick = pl.pallas_call(count, out_shape=jax.ShapeDtypeStruct((1,), jnp.int32), in_specs=[smem, smem], out_specs=smem)(row_live, col_live)
    arms = [functools.partial(dense, n_row, n_col, i) for i in range(4)]
    return lax.switch(pick[0], arms, matrix, pivot_inverse, row_live, col_live)


def solution(mesh):
    n_row, n_col = mesh.shape["prow"], mesh.shape["pcol"]
    return jax.shard_map(
        functools.partial(per_device, n_row, n_col),
        mesh=mesh,
        in_specs=(P("prow", "pcol"), P(None, "prow", None), P(), P()),
        out_specs=P("prow", "pcol"),
        check_vma=False,
    )
```

```python
import functools

import jax
import jax.numpy as jnp
from jax import lax
from jax.experimental import pallas as pl
from jax.experimental.pallas import tpu as pltpu
from jax.sharding import PartitionSpec as P

MESH = pl.DeviceIdType.MESH
CORES = 2
CHUNK = 256
PIECES = 16
TAIL = 4
GUESTS = 28
GRANT = 67_043_328
PARTS = 8
GROUPS = 4
ARMS = 4
PACE = 6


def split(x):
    high = x.astype(jnp.bfloat16)
    return high, (x - high.astype(jnp.float32)).astype(jnp.bfloat16)


def product(left_high, left_low, right_high, right_low):
    dot = functools.partial(jnp.dot, preferred_element_type=jnp.float32)
    return dot(left_high, right_high) + (dot(left_high, right_low) + dot(left_low, right_high))


def kernel(
    n_row, n_col, chunk, row_hbm, col_hbm, mat, piv, acc,
    row_smem, col_smem, u, p, a, guest, low, low_high, low_rest, u_high, u_rest,
    acc_sem, mask_sem, u_send, u_recv, p_send, p_recv, p_pass, p_passed, p_own,
    a_own, a_send, a_recv, t_send, t_recv, l_send, l_recv, l_pass, l_passed,
    p_up, g_in, g_recv, g_down, g_out,
):
    z, pcol = lax.axis_index("prow"), lax.axis_index("pcol")
    core, chip = lax.rem(pcol, CORES), lax.div(pcol, CORES)
    n_chip = n_col // CORES
    partner = (z, pcol + 1 - 2 * core)
    width, half = piv.shape[2], piv.shape[2] // CORES
    rows_own = piv.shape[1]
    rows_half = rows_own // CORES
    chunks = acc.shape[1] // chunk
    per_block = width // chunk
    pieces = u_send.shape[1] // chunks
    piece = width // pieces
    steps = chunks * pieces
    last = n_row - 1
    guests = guest.shape[1]
    guest_start = (chunks - 2) * pieces
    first_chip, active, both = chip == 0, z > 0, z > 1
    guest_end = guest_start + jnp.where(chip > 0, guests, 0)

    def remote(src, dst, send, recv, to):
        return pltpu.make_async_remote_copy(
            src_ref=src, dst_ref=dst, send_sem=send, recv_sem=recv, device_id=to, device_id_type=MESH
        )

    masks = [
        pltpu.make_async_copy(row_hbm, row_smem, mask_sem.at[0]),
        pltpu.make_async_copy(col_hbm, col_smem, mask_sem.at[1]),
    ]

    def columns_of(j):
        start = j * chunk
        return pl.ds(start if isinstance(j, int) else pl.multiple_of(start, 128), chunk)

    def load(j):
        return pltpu.make_async_copy(mat.at[:, columns_of(j)], acc.at[:, columns_of(j)], acc_sem.at[j])

    def pivot_own(k):
        return pltpu.make_async_copy(piv.at[k], p.at[k, pl.ds(z * rows_own, rows_own)], p_own.at[k])

    def pivot_rows(k, source):
        return p.at[k, pl.ds(pl.multiple_of(source * rows_own + core * rows_half, 8), rows_half)]

    def pivot_send(k, target, send):
        return remote(
            piv.at[k, pl.ds(pl.multiple_of(core * rows_half, 8), rows_half)],
            pivot_rows(k, z), send, p_recv.at[k, z], (target, pcol),
        )

    def pivot_relay(k, source, target):
        return remote(pivot_rows(k, source), pivot_rows(k, source), p_send.at[k, source], p_recv.at[k, source], (target, pcol))

    def pivot_landed(k, source):
        return remote(pivot_rows(k, source), pivot_rows(k, source), p_send.at[k, source], p_recv.at[k, source], (z, pcol))

    def pivot_pass(k, source):
        return remote(pivot_rows(k, source), pivot_rows(k, source), p_pass.at[k, source], p_passed.at[k, source], partner)

    def piece_of(ref, j, r):
        return ref.at[j, pl.ds(pl.multiple_of(r * piece, 8), piece)]

    def relay_copy(k, s):
        place = piece_of(u.at[k], s // pieces, s % pieces)
        return remote(place, place, u_send.at[k, s], u_recv.at[k, s], (z + 1, pcol))

    def origin_copy(k, s):
        j, r = s // pieces, s % pieces
        rows = pl.ds(pl.multiple_of(r * piece, 8), piece)
        return remote(acc.at[rows, columns_of(j)], piece_of(u.at[k], j, r), u_send.at[k, s], u_recv.at[k, s], (z + 1, pcol))

    def start_of(k):
        return jnp.where(pcol <= k, per_block * pieces, 0)

    def relay(k, begin, end):
        def body(s, carry):
            copy = relay_copy(k, s)
            copy.wait_recv()

            @pl.when(z < last)
            def _():
                copy.start()

            return carry

        lax.fori_loop(jnp.maximum(begin, start_of(k)), end, body, 0)

    def originate(k, begin, end):
        def body(s, carry):
            origin_copy(k, s).start()
            return carry

        lax.fori_loop(jnp.maximum(begin, start_of(k)), end, body, 0)

    def finish_sends(k, copy):
        def body(s, carry):
            copy(k, s).wait_send()
            return carry

        if k:
            lax.fori_loop(start_of(k), guest_start, body, 0)
            lax.fori_loop(guest_end, steps, body, 0)
        else:
            lax.fori_loop(start_of(k), steps, body, 0)

    def guest_in(i):
        rows = pl.ds(i * piece, piece)
        source = acc.at[rows, columns_of(guest_start // pieces)]
        return remote(source, guest.at[chip, i], g_in.at[i], g_recv.at[chip, i], (z, core))

    def guest_down(q, i):
        return remote(guest.at[q, i], guest.at[q, i], g_down.at[q, i], g_recv.at[q, i], (z + 1, pcol))

    def guest_out(q, i):
        target = piece_of(u.at[1], guest_start // pieces, i)
        return remote(guest.at[q, i], target, g_out.at[q, i], u_recv.at[1, guest_start + i], (z, q * CORES + core))

    def pass_guests():
        def body(t, carry):
            q, i = 1 + t // guests, t % guests
            guest_down(q, i).wait_recv()

            @pl.when(z < last)
            def _():
                guest_down(q, i).start()

            @pl.when(both)
            def _():
                guest_out(q, i).start()

            return carry

        lax.fori_loop(0, (n_chip - 1) * guests, body, 0)

    def finish_guests():
        def body(t, carry):
            q, i = 1 + t // guests, t % guests

            @pl.when(z < last)
            def _():
                guest_down(q, i).wait_send()

            @pl.when(both)
            def _():
                guest_out(q, i).wait_send()

            return carry

        lax.fori_loop(0, (n_chip - 1) * guests, body, 0)

    def own_rows():
        return pl.ds(pl.multiple_of(core * half, 8), half)

    def lower_send(k, target):
        rows = low.at[k, own_rows()]
        return remote(rows, rows, l_send.at[k, target], l_recv.at[k], (z, target * CORES + core))

    def lower_pass(k):
        rows = low.at[k, own_rows()]
        return remote(rows, rows, l_pass.at[k], l_passed.at[k], partner)

    def row_mask(k):
        return row_smem[k, z].astype(jnp.float32)

    def for_sources(k, visit):
        for distance in range(1, n_row):
            @pl.when(z - distance >= 0)
            def _():
                visit(z - distance, z + 1, z < last, z > k)

            @pl.when((z + distance <= last) & (z > k))
            def _():
                visit(z + distance, z - 1, z - 1 > k, z > k)

    def relay_pivot(k):
        def visit(source, target, onward, used):
            pivot_landed(k, source).wait_recv()

            @pl.when(onward)
            def _():
                pivot_relay(k, source, target).start()

            @pl.when(used)
            def _():
                pivot_pass(k, source).start()

        for_sources(k, visit)

    def gather_pivot(k):
        pivot_own(k).wait()
        for source in range(n_row):
            @pl.when(z != source)
            def _():
                pivot_pass(k, source).wait_recv()

    def finish_pivot(k):
        def visit(source, target, onward, used):
            @pl.when(onward)
            def _():
                pivot_relay(k, source, target).wait_send()

            @pl.when(used)
            def _():
                pivot_pass(k, source).wait_send()

        for_sources(k, visit)

    def apply_pivot(k, left):
        left_high, left_low = split(left)
        for q in range(per_block):
            columns = pl.ds(q * chunk, chunk)
            right = split(p[k, :, columns])
            low[k, own_rows(), columns] = row_mask(k) * product(left_high, left_low, *right)
        for target in range(n_chip - 1, 0, -1):
            lower_send(k, target).start()
        lower_pass(k).start()

    def take_lower(k):
        @pl.when(chip > 0)
        def _():
            lower_send(k, 0).wait_recv()
            lower_pass(k).start()

        lower_pass(k).wait_recv()
        low_high[k], low_rest[k] = split(low[k])

    def update(k, j, part=0, parts=1):
        live = col_smem[k, pcol + (j // per_block) * n_col].astype(jnp.float32)

        def run():
            depth = pl.ds(part * (width // parts), width // parts)
            u_high[depth], u_rest[depth] = split(u[k, j, depth])
            for t in range(CORES):
                rows = pl.ds(t * half, half)
                left = low_high[k, rows, depth], low_rest[k, rows, depth]
                acc[rows, columns_of(j)] -= live * product(*left, u_high[depth], u_rest[depth])

        if j < per_block:
            pl.when(pcol > k)(run)
        else:
            run()

    def store_lower(k):
        @pl.when(pcol == k)
        def _():
            acc[:, pl.ds(0, width)] = low[k]

    barrier = pltpu.get_barrier_semaphore()
    relays_guests = (z == 1) & (z < last)

    def greet(condition, device):
        @pl.when(condition)
        def _():
            pl.semaphore_signal(barrier, inc=1, device_id=device, device_id_type=MESH)

    greet(active, (z - 1, pcol))
    greet(active, partner)
    greet(active & (z < last) & first_chip, (z + 1, pcol))
    greet(active & (chip > 0), (z, core))
    for other in range(1, n_chip):
        greet(relays_guests & first_chip, (z, other * CORES + core))

    for j in range(chunks):
        load(j).start()
    for copy in masks:
        copy.start()

    @pl.when(first_chip & active)
    def _():
        for k in range(2):
            pivot_own(k).start()
        pltpu.make_async_copy(mat.at[own_rows(), pl.ds(0, width)], a.at[core], a_own).start()

    targets = (
        jnp.where(z < last, 1, 0)
        + jnp.where(active, 1, 0)
        + jnp.where(both & first_chip, 1, 0)
        + jnp.where(active & first_chip, n_chip - 1, 0)
        + jnp.where(relays_guests & (chip > 0), 1, 0)
    )
    pl.semaphore_wait(barrier, targets)

    def swap_columns():
        source = mat.at[pl.ds(pl.multiple_of((1 - core) * half, 8), half), pl.ds(0, width)]
        return remote(source, a.at[core], a_send, a_recv, partner)

    def swapped_columns():
        return remote(a.at[1 - core], a.at[1 - core], a_send, a_recv, partner)

    @pl.when(first_chip)
    def _():
        for k in range(2):
            @pl.when(z < last)
            def _():
                pivot_send(k, z + 1, p_send.at[k, z]).start()

            @pl.when(z - 1 > k)
            def _():
                pivot_send(k, z - 1, p_up.at[k]).start()

        @pl.when(active)
        def _():
            swap_columns().start()

    for j in range(chunks):
        load(j).wait()

        @pl.when(z == 0)
        def _():
            originate(0, j * pieces, (j + 1) * pieces)

    for copy in masks:
        copy.wait()

    @pl.when(active)
    def _():
        @pl.when(first_chip)
        def _():
            relay_pivot(0)
            gather_pivot(0)
            pltpu.make_async_copy(mat.at[own_rows(), pl.ds(0, width)], a.at[core], a_own).wait()
            swapped_columns().wait_recv()
            apply_pivot(0, a[0])
            relay_pivot(1)

        ahead = jnp.where(pcol == 0, steps - TAIL, per_block * pieces)
        relay(0, 0, ahead)

        @pl.when(first_chip & both)
        def _():
            top = u.at[0, pl.ds(0, per_block)]
            copy = remote(top, top, t_send, t_recv, partner)

            @pl.when(core == 1)
            def _():
                copy.start()

            gather_pivot(1)

            @pl.when(core == 0)
            def _():
                copy.wait_recv()

            live = col_smem[0, 1].astype(jnp.float32)
            left = split(low[0, own_rows()])
            for q in range(per_block):
                columns = pl.ds(q * chunk, chunk)
                a[1, :, columns] -= live * product(*left, *split(u[0, q]))
            apply_pivot(1, a[1])

            @pl.when(core == 1)
            def _():
                copy.wait_send()

        relay(0, ahead, steps - TAIL)
        take_lower(0)
        for j in range(chunks - 1):
            update(0, j)
            relay(0, steps - TAIL + j, steps - TAIL + j + 1)
        relay(0, steps - TAIL + chunks - 1, steps)

        @pl.when(z == 1)
        def _():
            @pl.when(z < last)
            def _():
                @pl.when(chip > 0)
                def _():
                    for i in range(guests):
                        guest_in(i).start()

                originate(1, 0, guest_start)
                originate(1, guest_end, steps - pieces)

                @pl.when(first_chip)
                def _():
                    pass_guests()

            update(0, chunks - 1)

            @pl.when(z < last)
            def _():
                originate(1, steps - pieces, steps)

            store_lower(0)

        @pl.when(both)
        def _():
            relay(1, 0, pieces)
            update(0, chunks - 1)
            relay(1, pieces, guest_start)
            take_lower(1)
            update(1, 0)
            relay(1, guest_end, guest_end + 4)
            update(1, 1)
            store_lower(0)
            store_lower(1)
            relay(1, guest_end + 4, steps - pieces)

            @pl.when(first_chip)
            def _():
                pass_guests()

            @pl.when(chip > 0)
            def _():
                for i in range(guests):
                    relay_copy(1, guest_start + i).wait_recv()

            for j in range(2, chunks - 1):
                update(1, j)
            for part in range(4):
                begin = steps - pieces + part * (pieces // 4)
                relay(1, begin, begin + pieces // 4)
                update(1, chunks - 1, part, 4)

    @pl.when(z == 0)
    def _():
        finish_sends(0, origin_copy)

    @pl.when(active & first_chip)
    def _():
        @pl.when((z < last) | both)
        def _():
            finish_guests()

    @pl.when((z == 1) & (z < last) & (chip > 0))
    def _():
        for i in range(guests):
            guest_in(i).wait_send()

    @pl.when(active & (z < last))
    def _():
        finish_sends(0, relay_copy)

        @pl.when(z == 1)
        def _():
            finish_sends(1, origin_copy)

        @pl.when(both)
        def _():
            finish_sends(1, relay_copy)

    @pl.when(first_chip)
    def _():
        for k in range(2):
            @pl.when(z < last)
            def _():
                pivot_send(k, z + 1, p_send.at[k, z]).wait_send()

            @pl.when(z - 1 > k)
            def _():
                pivot_send(k, z - 1, p_up.at[k]).wait_send()

            finish_pivot(k)

    @pl.when(first_chip & (z == 1))
    def _():
        pivot_own(1).wait()

    for k in range(2):
        @pl.when(z > k)
        def _():
            lower_pass(k).wait_send()

            @pl.when(first_chip)
            def _():
                for target in range(n_chip - 1, 0, -1):
                    lower_send(k, target).wait_send()
                if k == 0:
                    swap_columns().wait_send()


def dense(n_row, n_col, plan, matrix, pivot_inverse, row_live, col_live):
    rows, columns = matrix.shape
    panels, rows_own, width = pivot_inverse.shape
    chunk = min(CHUNK, width)
    chunks = columns // chunk
    steps = chunks * PIECES
    n_chip = n_col // CORES
    guests = max(1, GUESTS // n_chip)
    f32, bf16, dma = jnp.float32, jnp.bfloat16, pltpu.SemaphoreType.DMA
    return pl.pallas_call(
        functools.partial(kernel, n_row, n_col, chunk),
        out_shape=pltpu.VMEM((rows, columns), f32),
        in_specs=[pl.BlockSpec(memory_space=pltpu.HBM)] * 4,
        out_specs=pl.BlockSpec(memory_space=pltpu.VMEM),
        scratch_shapes=[
            pltpu.SMEM(row_live.shape, jnp.int32),
            pltpu.SMEM(col_live.shape, jnp.int32),
            pltpu.VMEM((panels, chunks, width, chunk), f32),
            pltpu.VMEM((panels, width, width), f32),
            pltpu.VMEM((CORES, width // CORES, width), f32),
            pltpu.VMEM((n_chip, guests, width // PIECES, chunk), f32),
            pltpu.VMEM((panels, width, width), f32),
            pltpu.VMEM((panels, width, width), bf16),
            pltpu.VMEM((panels, width, width), bf16),
            pltpu.VMEM((width, chunk), bf16),
            pltpu.VMEM((width, chunk), bf16),
            dma((chunks,)), dma((2,)),
            dma((panels, steps)), dma((panels, steps)),
            dma((panels, n_row)), dma((panels, n_row)), dma((panels, n_row)), dma((panels, n_row)),
            dma((panels,)), dma, dma, dma, dma, dma,
            dma((panels, n_col // CORES)), dma((panels,)), dma((panels,)), dma((panels,)),
            dma((panels,)), dma((guests,)), dma((n_chip, guests)), dma((n_chip, guests)), dma((n_chip, guests)),
        ],
        compiler_params=pltpu.CompilerParams(
            collective_id=0, has_side_effects=True, vmem_limit_bytes=GRANT - 4 * rows * columns
        ),
    )(row_live, col_live, matrix, pivot_inverse)


def neighbour(chip, bit):
    return chip + bit * (1 - 2 * lax.rem(lax.div(chip, bit), 2))


def live_items(row, col, chip, n_row, n_col, chunks, per_block):
    used = row[1, 2]
    for g in range(3, n_row):
        used = jnp.maximum(used, row[1, g])
    zero, one = [], []
    for j in range(CORES * chunks):
        h = chip * CORES + j % CORES + j // CORES // per_block * n_col
        zero.append(jnp.where(h > 0, col[0, h], 0))
        one.append(jnp.where(h > 1, col[1, h] * used, 0))
    return zero, one


def total(values):
    return functools.reduce(lambda x, y: x + y, values, jnp.int32(0))


def plan_kernel(n_row, n_col, chunks, per_block, row, col, out):
    n_chip, items = n_col // CORES, CORES * chunks
    half = items // 2
    lane = lax.broadcasted_iota(jnp.int32, (8, 128), 1).astype(jnp.float32)
    digits = []
    rest = lane
    for _ in range(4):
        next_rest = jnp.floor((rest + 0.5) / 3)
        digits.append(rest - 3 * next_rest - 1)
        rest = next_rest
    moves = sum(jnp.abs(f) for f in digits)
    longest = jnp.int32(0)
    for quad in range(n_chip // 4):
        worst = jnp.zeros_like(lane)
        for i in range(4):
            zero, one = live_items(row, col, quad * 4 + i, n_row, n_col, chunks, per_block)
            both = [x * y for x, y in zip(zero, one)]
            early = total(both[:half]).astype(jnp.float32)
            holes = total([(1 - zero[j]) * (1 - one[j]) for j in range(half, items)]).astype(jnp.float32)
            count = total(both).astype(jnp.float32)
            x = digits[i // 2] * (1 - 2 * (i % 2))
            y = digits[2 + i % 2] * (1 - 2 * (i // 2))
            sent = jnp.maximum(x, 0) + jnp.maximum(y, 0)
            load = items + count - x - y - jnp.minimum(holes, early - sent)
            worst = jnp.maximum(worst, jnp.where(sent > early, 99.0, load))
        key = jnp.where(rest > 0.5, 1e6, (worst * 16 + moves) * 128 + lane)
        best = jnp.min(key).astype(jnp.int32)
        longest = jnp.maximum(longest, lax.div(best, 2048))
        code = lax.rem(best, 128)
        for e in range(4):
            out[1 + quad * 4 + e] = lax.rem(code, 3) - 1
            code = lax.div(code, 3)
    out[0] = jnp.minimum(jnp.maximum(longest - items - 2, 0), ARMS)


def sparse_kernel(
    slots, n_row, n_col, chunk, row_hbm, col_hbm, plan_hbm, mat, piv, acc,
    row_smem, col_smem, plan, tab, pos, prod, tx, own, out_guest, in_guest, back,
    p, a, low, low_high, low_rest, u_high, u_rest,
    acc_sem, mask_sem, d_send, d_recv, f_send, f_recv, r_send, e_send, e_recv, s_send, s_recv, b_send, b_recv,
    p_send, p_recv, p_pass, p_passed, p_own, a_own, a_send, a_recv, l_send, l_recv, l_pass, l_passed, p_up,
):
    z, pcol = lax.axis_index("prow"), lax.axis_index("pcol")
    core, chip = lax.rem(pcol, CORES), lax.div(pcol, CORES)
    n_chip = n_col // CORES
    partner = (z, pcol + 1 - 2 * core)
    width, half = piv.shape[2], piv.shape[2] // CORES
    rows_own = piv.shape[1]
    rows_half = rows_own // CORES
    chunks = acc.shape[1] // chunk
    per_block = width // chunk
    items = CORES * chunks
    part = chunk // CORES
    piece = width // PARTS
    last = n_row - 1
    first_chip, active, both = chip == 0, z > 0, z > 1
    mine = pl.ds(pl.multiple_of(core * part, 128), part)

    def remote(src, dst, send, recv, to):
        return pltpu.make_async_remote_copy(
            src_ref=src, dst_ref=dst, send_sem=send, recv_sem=recv, device_id=to, device_id_type=MESH
        )

    masks = [
        pltpu.make_async_copy(row_hbm, row_smem, mask_sem.at[0]),
        pltpu.make_async_copy(col_hbm, col_smem, mask_sem.at[1]),
        pltpu.make_async_copy(plan_hbm, plan, mask_sem.at[2]),
    ]

    def columns_of(j):
        start = j * chunk
        return pl.ds(start if isinstance(j, int) else pl.multiple_of(start, 128), chunk)

    def part_of(j, side):
        return pl.ds(pl.multiple_of(j * chunk + side * part, 128), part)

    def rows_of(r):
        return pl.ds(pl.multiple_of(r * piece, 8), piece)

    def load(j):
        return pltpu.make_async_copy(mat.at[:, columns_of(j)], acc.at[:, columns_of(j)], acc_sem.at[j])

    def pivot_own(k):
        return pltpu.make_async_copy(piv.at[k], p.at[k, pl.ds(z * rows_own, rows_own)], p_own.at[k])

    def pivot_rows(k, source):
        return p.at[k, pl.ds(pl.multiple_of(source * rows_own + core * rows_half, 8), rows_half)]

    def pivot_send(k, target, send):
        return remote(
            piv.at[k, pl.ds(pl.multiple_of(core * rows_half, 8), rows_half)],
            pivot_rows(k, z), send, p_recv.at[k, z], (target, pcol),
        )

    def pivot_relay(k, source, target):
        return remote(pivot_rows(k, source), pivot_rows(k, source), p_send.at[k, source], p_recv.at[k, source], (target, pcol))

    def pivot_landed(k, source):
        return remote(pivot_rows(k, source), pivot_rows(k, source), p_send.at[k, source], p_recv.at[k, source], (z, pcol))

    def pivot_pass(k, source):
        return remote(pivot_rows(k, source), pivot_rows(k, source), p_pass.at[k, source], p_passed.at[k, source], partner)

    def own_rows():
        return pl.ds(pl.multiple_of(core * half, 8), half)

    def lower_send(k, target, q):
        rows = low.at[k, pl.ds(pl.multiple_of(core * half + q * (half // 2), 8), half // 2)]
        return remote(rows, rows, l_send.at[k, target, q], l_recv.at[k, q], (z, target * CORES + core))

    member = lax.rem(chip, 4)
    direct = [t for t in range(1, n_chip) if t % 4 < 3]

    def relay_lower(k):
        for q in range(2):
            @pl.when(member == 1 + q)
            def _():
                lower_send(k, chip, q).wait_recv()
                lower_send(k, chip + 2 - q, q).start()

    def lower_pass(k):
        rows = low.at[k, own_rows()]
        return remote(rows, rows, l_pass.at[k], l_passed.at[k], partner)

    def row_mask(k):
        return row_smem[k, z].astype(jnp.float32)

    def for_sources(k, visit):
        for distance in range(1, n_row):
            @pl.when(z - distance >= 0)
            def _():
                visit(z - distance, z + 1, z < last, z > k)

            @pl.when((z + distance <= last) & (z > k))
            def _():
                visit(z + distance, z - 1, z - 1 > k, z > k)

    def relay_pivot(k):
        def visit(source, target, onward, used):
            pivot_landed(k, source).wait_recv()

            @pl.when(onward)
            def _():
                pivot_relay(k, source, target).start()

            @pl.when(used)
            def _():
                pivot_pass(k, source).start()

        for_sources(k, visit)

    def gather_pivot(k):
        pivot_own(k).wait()
        for source in range(n_row):
            @pl.when(z != source)
            def _():
                pivot_pass(k, source).wait_recv()

    def finish_pivot(k):
        def visit(source, target, onward, used):
            @pl.when(onward)
            def _():
                pivot_relay(k, source, target).wait_send()

            @pl.when(used)
            def _():
                pivot_pass(k, source).wait_send()

        for_sources(k, visit)

    def apply_pivot(k, left):
        left_high, left_low = split(left)

        def visit(q):
            right = split(p[k, :, columns_of(q)])
            low[k, own_rows(), columns_of(q)] = row_mask(k) * product(left_high, left_low, *right)

        loop(0, per_block, visit)
        for turn in range(2):
            for target in direct:
                lower_send(k, target, 1 - turn if target % 4 == 2 else turn).start()
        lower_pass(k).start()

    def take_lower(k):
        @pl.when(chip > 0)
        def _():
            for q in range(2):
                @pl.when(member != 1 + q)
                def _():
                    lower_send(k, 0, q).wait_recv()

            lower_pass(k).start()

        lower_pass(k).wait_recv()

        def visit(r):
            low_high[k, rows_of(r)], low_rest[k, rows_of(r)] = split(low[k, rows_of(r)])

        loop(0, PARTS, visit)

    def store_lower(k):
        @pl.when(pcol == k)
        def _():
            acc[:, pl.ds(0, width)] = low[k]

    def swap_columns():
        source = mat.at[pl.ds(pl.multiple_of((1 - core) * half, 8), half), pl.ds(0, width)]
        return remote(source, a.at[core], a_send, a_recv, partner)

    def swapped_columns():
        return remote(a.at[1 - core], a.at[1 - core], a_send, a_recv, partner)

    def carried(j):
        return jnp.logical_not(first_chip & (lax.rem(j, 2) == 0) & (j < CORES * per_block))

    def upper_send(jj, side, r):
        j = CORES * jj + core
        return remote(
            mat.at[rows_of(r), part_of(jj, side)], pos.at[j, rows_of(r), pl.ds(pl.multiple_of(side * part, 128), part)],
            d_send.at[CORES * jj + side, r], d_recv.at[j, r], (z + 1, chip * CORES + side),
        )

    def down(source, s, r):
        return remote(source, pos.at[s, rows_of(r), mine], d_send.at[s, r], d_recv.at[s, r], (z + 1, pcol))

    def down_staged(s, r):
        return down(tx.at[s, rows_of(r)], s, r)

    def down_relay(s, r):
        return down(pos.at[s, rows_of(r), mine], s, r)

    def landed(s, r):
        place = pos.at[s, rows_of(r), mine]
        return remote(place, place, d_send.at[s, r], d_recv.at[s, r], (z, pcol))

    def give_back(b, r):
        place = pos.at[items + b, rows_of(r), mine]
        target = pos.at[slots + b, rows_of(r), mine]
        to = (z, neighbour(chip, 1 + b) * CORES + core)
        return remote(place, target, r_send.at[b, r], d_recv.at[slots + b, r], to)

    def group_rows(g):
        return pl.ds(pl.multiple_of(g * (width // GROUPS), 8), width // GROUPS)

    def forward(s, g):
        place = pos.at[s, group_rows(g), mine]
        return remote(place, place, f_send.at[s, g], f_recv.at[s, g], partner)

    def export(b):
        to = (z, neighbour(chip, 1 + b) * CORES + core)
        return remote(out_guest.at[b], in_guest.at[b], e_send.at[b], e_recv.at[b], to)

    def swap_own(jj):
        source = acc.at[:, part_of(jj, 1 - core)]
        return remote(source, own.at[CORES * jj + core], s_send.at[jj], s_recv.at[jj], partner)

    def swapped_own(jj):
        place = own.at[CORES * jj + 1 - core]
        return remote(place, place, s_send.at[jj], s_recv.at[jj], partner)

    def hand_back(jj):
        return remote(own.at[CORES * jj + 1 - core], back.at[jj], b_send.at[jj], b_recv.at[jj], partner)

    def loop(begin, end, visit):
        def body(i, carry):
            visit(i)
            return carry

        lax.fori_loop(begin, end, body, 0)

    barrier = pltpu.get_barrier_semaphore()

    def greet(condition, device):
        @pl.when(condition)
        def _():
            pl.semaphore_signal(barrier, inc=1, device_id=device, device_id_type=MESH)

    greet(active, (z - 1, pcol))
    greet(z == 1, (z - 1, pcol + 1 - 2 * core))
    greet(active, partner)
    greet(active & (z < last) & first_chip, (z + 1, pcol))
    greet(active & (chip > 0), (z, core))
    for bit in (1, 2):
        near = neighbour(chip, bit)
        greet(active & (near > 0), (z, near * CORES + core))

    for j in range(chunks):
        load(j).start()
    for copy in masks:
        copy.start()

    @pl.when(first_chip & active)
    def _():
        for k in range(2):
            pivot_own(k).start()
        pltpu.make_async_copy(mat.at[own_rows(), pl.ds(0, width)], a.at[core], a_own).start()

    targets = (
        jnp.where(z < last, 1, 0)
        + jnp.where(z == 0, 1, 0)
        + jnp.where(active, 1, 0)
        + jnp.where(both & first_chip, 1, 0)
        + jnp.where(active & first_chip, n_chip - 1, 0)
        + jnp.where(active & (chip > 0), 2, 0)
    )
    pl.semaphore_wait(barrier, targets)

    @pl.when(first_chip)
    def _():
        for k in range(2):
            @pl.when(z < last)
            def _():
                pivot_send(k, z + 1, p_send.at[k, z]).start()

            @pl.when(z - 1 > k)
            def _():
                pivot_send(k, z - 1, p_up.at[k]).start()

        @pl.when(active)
        def _():
            swap_columns().start()

    upper_start = jnp.where(pcol == 0, per_block * PARTS, 0)

    @pl.when(z == 0)
    def _():
        def visit(s):
            for side in range(CORES):
                upper_send(lax.div(s, PARTS), side, lax.rem(s, PARTS)).start()

        loop(upper_start, chunks * PARTS, visit)

    for j in range(chunks):
        load(j).wait()

    @pl.when(z == 1)
    def _():
        for jj in range(chunks):
            swap_own(jj).start()

    for copy in masks:
        copy.wait()

    zero, one = live_items(row_smem, col_smem, chip, n_row, n_col, chunks, per_block)
    pair = [x * y for x, y in zip(zero, one)]
    rank, hole, order = [], [], []
    for j in range(items):
        rank.append(total(pair[:j]))
        hole.append((1 - zero[j]) * (1 - one[j]) if j >= items // 2 else jnp.int32(0))
        order.append(total(hole[:j]))
    quad = lax.div(chip, 4)
    flow_x = plan[1 + quad * 4 + lax.div(member, 2)] * (1 - 2 * lax.rem(member, 2))
    flow_y = plan[3 + quad * 4 + lax.rem(member, 2)] * (1 - 2 * lax.div(member, 2))
    x_out, y_out = jnp.maximum(flow_x, 0), jnp.maximum(flow_y, 0)
    x_in, y_in = jnp.maximum(-flow_x, 0), jnp.maximum(-flow_y, 0)
    sent = x_out + y_out
    filled = jnp.minimum(total(hole), total(pair[: items // 2]) - sent)

    def item_of(r):
        return total([jnp.where(rank[j] == r, j * pair[j], 0) for j in range(items)])

    for j in range(items):
        held = (1 - zero[j]) * one[j]
        moved = item_of(sent + order[j]) if j >= items // 2 else j
        tab[0, j] = zero[j]
        tab[1, j] = jnp.where(held > 0, j, jnp.where(order[j] < filled, moved, j))
    for s in range(items, slots):
        tab[0, s] = 0
        index = s - items - (x_in + y_in if s > items + 1 else (x_in if s > items else 0))
        tab[1, s] = item_of(sent + filled + index)
    tab[0, slots] = 0
    tab[0, slots + 1] = 0

    for jj in range(chunks):
        found = []
        for d in range(CORES):
            j = CORES * jj + d
            spare = rank[j] - sent
            fill = total([jnp.where(order[q] == spare, q * hole[q], 0) for q in range(items // 2, items)])
            index = spare - filled
            late = items + index + jnp.where((x_in == 0) & (index == 0), 0, x_in + y_in)
            away = jnp.where((rank[j] == 0) & (x_out > 0), slots, slots + 1)
            place = jnp.where(spare < 0, away, jnp.where(spare < filled, fill, late))
            found.append(jnp.where(pair[j] > 0, place, j))
        tab[2, jj] = jnp.where(core == 0, found[0], found[1])
        tab[3, jj] = jnp.where(core == 0, one[CORES * jj], one[CORES * jj + 1])
        tab[4, jj] = jnp.where(core == 0, zero[CORES * jj], zero[CORES * jj + 1])

    def stage_pair(jj, begin, finish):
        def visit(r):
            for d in range(CORES):
                s = CORES * jj + d

                @pl.when(carried(s))
                def _():
                    landed(s, r).wait_recv()
                    upper = tab[0, s].astype(jnp.float32)
                    rows = rows_of(r)
                    tx[s, rows] = upper * pos[s, rows, mine] + (1 - upper) * own[tab[1, s], rows]

                    @pl.when(z < last)
                    def _():
                        down_staged(s, r).start()

        loop(begin, finish, visit)

    def stage_late(s):
        def visit(r):
            rows = rows_of(r)
            tx[s, rows] = own[tab[1, s], rows]

            @pl.when(z < last)
            def _():
                down_staged(s, r).start()

        loop(0, PARTS, visit)

    def stage_guest(b):
        export(b).wait_recv()
        keep = (y_in if b else x_in).astype(jnp.float32)

        def visit(r):
            rows = rows_of(r)
            tx[items + b, rows] = keep * in_guest[b, rows] + (1 - keep) * own[tab[1, items + b], rows]

            @pl.when(z < last)
            def _():
                down_staged(items + b, r).start()

        loop(0, PARTS, visit)

    def update_own(s):
        jj = lax.div(s, CORES)

        @pl.when(carried(s))
        def _():
            live = tab[0, s].astype(jnp.float32)
            u_high[:, pl.ds(0, part)], u_rest[:, pl.ds(0, part)] = split(pos[s, :, mine])

            def visit(t):
                rows = pl.ds(pl.multiple_of(t * half, half), half)
                high, rest = u_high[:, pl.ds(0, part)], u_rest[:, pl.ds(0, part)]
                own[s, rows] -= live * product(low_high[0, rows], low_rest[0, rows], high, rest)

            loop(0, CORES, visit)

        @pl.when(lax.rem(s, CORES) == core)
        def _():
            def visit(r):
                acc[rows_of(r), part_of(jj, core)] = own[s, rows_of(r)]

            loop(0, PARTS, visit)

        @pl.when(lax.rem(s, CORES) != core)
        def _():
            hand_back(jj).start()

    prompt = sum(slots >= items + 4 + b for b in range(2))
    end = slots - 1
    late_slots = [end] + [slots + b for b in range(prompt, 2)]
    side_groups = GROUPS // 2
    depth = width // 2

    def multiply(s, side):
        k = 1 - tab[0, s]
        deep = pl.ds(pl.multiple_of(side * depth, depth), depth)
        u_high[deep], u_rest[deep] = split(pos[s, deep])
        for t in range(CORES):
            rows = pl.ds(t * half, half)
            value = product(low_high[k, rows, deep], low_rest[k, rows, deep], u_high[deep], u_rest[deep])
            prod[s, rows] = value + jnp.where(side > 0, prod[s, rows], 0.0)

    def work(w):
        o, side = lax.div(w, 2), lax.rem(w, 2)
        s = jnp.where(o < end, o, jnp.where(o < end + prompt, o + 1, jnp.where(o == end + prompt, end, o)))

        @pl.when(carried(s))
        def _():
            @pl.when(jnp.logical_not(first_chip & (s < CORES * per_block)))
            def _():
                for i in range(side_groups):
                    forward(s, side * side_groups + i).wait_recv()

            multiply(s, side)

    def arrive(s, g, relays=True):
        for i in range(PARTS // GROUPS):
            r = g * (PARTS // GROUPS) + i
            landed(s, r).wait_recv()
            if relays:
                @pl.when(z < last)
                def _():
                    down_relay(s, r).start()

                for b in range(2):
                    @pl.when(s == items + b)
                    def _():
                        give_back(b, r).start()
        forward(s, g).start()

    def arrive_pair(jj, begin=0, finish=GROUPS):
        def visit(g):
            for d in range(CORES):
                s = CORES * jj + d

                @pl.when(carried(s))
                def _():
                    arrive(s, g)

        loop(begin, finish, visit)

    def take_guests(begin, finish):
        loop(begin * GROUPS, finish * GROUPS, lambda t: arrive(slots + lax.div(t, GROUPS), lax.rem(t, GROUPS), False))

    units = 2 * (slots - items)

    def limit(i):
        s, side = items + lax.div(i, 2), lax.rem(i, 2)
        whole = 2 * s + side + jnp.where(s < end, 0, 2 * prompt)
        ends = jnp.where(i == units, 2 * (slots + prompt), 2 * (slots + 2))
        return jnp.where(i < units, jnp.minimum(whole, PACE * (i + 1)), ends)

    def settle():
        def visit(t):
            jj, rows = lax.div(t, PARTS), rows_of(lax.rem(t, PARTS))
            place = tab[2, jj]
            ready = tab[3, jj] > 0
            for s in late_slots:
                ready = ready & (place != s)
            upper = jnp.where(tab[4, jj] > 0, prod[CORES * jj + core, rows], 0.0)
            acc[rows, columns_of(jj)] -= upper + jnp.where(ready, prod[place, rows], 0.0)

        loop(0, chunks * PARTS, visit)

    def settle_late():
        def visit(t):
            jj, rows = lax.div(t, PARTS), rows_of(lax.rem(t, PARTS))
            value = jnp.zeros((piece, chunk), jnp.float32)
            for s in late_slots:
                value += jnp.where((tab[3, jj] > 0) & (tab[2, jj] == s), prod[s, rows], 0.0)
            acc[rows, columns_of(jj)] -= value

        loop(0, chunks * PARTS, visit)

    @pl.when(active & first_chip)
    def _():
        relay_pivot(0)
        gather_pivot(0)
        pltpu.make_async_copy(mat.at[own_rows(), pl.ds(0, width)], a.at[core], a_own).wait()
        swapped_columns().wait_recv()
        apply_pivot(0, a[0])
        relay_pivot(1)

    @pl.when(z == 1)
    def _():
        for jj in range(chunks):
            own[CORES * jj + core] = acc[:, part_of(jj, core)]
            swapped_own(jj).wait_recv()

        def visit(jj):
            stage_pair(jj, 0, PARTS // 2)

            @pl.when(jj == 1)
            def _():
                relay_lower(0)

            stage_pair(jj, PARTS // 2, PARTS)

            @pl.when(jj == 1)
            def _():
                take_lower(0)

            @pl.when(jj == chunks - 1)
            def _():
                stage_guest(0)

            loop(CORES * jj - jnp.where(jj == 1, CORES, 0), jnp.where(jj > 0, CORES * jj + CORES, 0), update_own)

            @pl.when(jj == 1)
            def _():
                for b in range(2):
                    out_guest[b] = own[item_of(x_out if b else 0)]
                    export(b).start()

        loop(0, chunks, visit)
        stage_guest(1)
        loop(items + 2, slots, stage_late)
        for jj in range(chunks):
            hand_back(jj).wait_recv()
            swap_own(jj).wait_send()
            acc[:, part_of(jj, 1 - core)] = back[jj]
        store_lower(0)

    @pl.when(both)
    def _():
        loop(0, per_block - 1, arrive_pair)
        arrive_pair(per_block - 1, 0, side_groups)
        relay_lower(0)
        arrive_pair(per_block - 1, side_groups, GROUPS)

        @pl.when(first_chip)
        def _():
            gather_pivot(1)
            live = tab[0, 1].astype(jnp.float32)
            left = split(low[0, own_rows()])

            def visit(q):
                for g in range(GROUPS):
                    forward(CORES * q + 1, g).wait_recv()
                a[1, :, columns_of(q)] -= live * product(*left, *split(pos[CORES * q + 1]))

            loop(0, per_block, visit)
            apply_pivot(1, a[1])

        loop(per_block, chunks - 1, arrive_pair)
        arrive_pair(chunks - 1, 0, 1)
        relay_lower(1)
        arrive_pair(chunks - 1, 1, GROUPS)
        loop(0, 2, take_lower)

        def unit(i):
            s, side = items + lax.div(i, 2), lax.rem(i, 2)
            begin = side * side_groups

            @pl.when(i < units)
            def _():
                if prompt:
                    @pl.when(i == units - 2)
                    def _():
                        take_guests(0, prompt)

                loop(begin, begin + side_groups, lambda g: arrive(s, g))

            @pl.when(i == units - 1)
            def _():
                loop(jnp.where(i > 0, limit(i - 1), 0), 2 * (end + prompt), work)
                settle()

            if prompt < 2:
                @pl.when(i == units + 1)
                def _():
                    take_guests(prompt, 2)

            start = jnp.where(i > 0, limit(i - 1), 0)
            start = jnp.where(i == units - 1, jnp.maximum(start, 2 * (end + prompt)), start)
            loop(start, limit(i), work)

        loop(0, units + 2 if prompt < 2 else units + 1, unit)
        settle_late()
        for k in range(2):
            store_lower(k)

    def each_carried(visit):
        def one_slot(s):
            @pl.when(carried(s))
            def _():
                visit(s)

        loop(0, slots, one_slot)

    @pl.when(z == 0)
    def _():
        def visit(s):
            for side in range(CORES):
                upper_send(lax.div(s, PARTS), side, lax.rem(s, PARTS)).wait_send()

        loop(upper_start, chunks * PARTS, visit)

    @pl.when(z == 1)
    def _():
        for jj in range(chunks):
            hand_back(jj).wait_send()
        for b in range(2):
            export(b).wait_send()

        @pl.when(z < last)
        def _():
            each_carried(lambda s: loop(0, PARTS, lambda r: down_staged(s, r).wait_send()))

    @pl.when(both)
    def _():
        for b in range(2):
            loop(0, PARTS, lambda r: give_back(b, r).wait_send())
            loop(0, GROUPS, lambda g: forward(slots + b, g).wait_send())
        each_carried(lambda s: loop(0, GROUPS, lambda g: forward(s, g).wait_send()))

        @pl.when(z < last)
        def _():
            each_carried(lambda s: loop(0, PARTS, lambda r: down_relay(s, r).wait_send()))

    @pl.when(first_chip)
    def _():
        for k in range(2):
            @pl.when(z < last)
            def _():
                pivot_send(k, z + 1, p_send.at[k, z]).wait_send()

            @pl.when(z - 1 > k)
            def _():
                pivot_send(k, z - 1, p_up.at[k]).wait_send()

            finish_pivot(k)

    @pl.when(first_chip & (z == 1))
    def _():
        pivot_own(1).wait()

    for k in range(2):
        @pl.when(z > k)
        def _():
            lower_pass(k).wait_send()

            @pl.when(first_chip)
            def _():
                for target in direct:
                    for q in range(2):
                        lower_send(k, target, q).wait_send()
                if k == 0:
                    swap_columns().wait_send()

            for q in range(2):
                @pl.when(member == 1 + q)
                def _():
                    lower_send(k, chip + 2 - q, q).wait_send()


def sparse(arm, n_row, n_col, plan, matrix, pivot_inverse, row_live, col_live):
    rows, columns = matrix.shape
    panels, rows_own, width = pivot_inverse.shape
    chunk = min(CHUNK, width)
    chunks = columns // chunk
    items = CORES * chunks
    slots = items + 2 + arm
    part = chunk // CORES
    n_chip = n_col // CORES
    f32, bf16, dma = jnp.float32, jnp.bfloat16, pltpu.SemaphoreType.DMA
    return pl.pallas_call(
        functools.partial(sparse_kernel, slots, n_row, n_col, chunk),
        out_shape=pltpu.VMEM((rows, columns), f32),
        in_specs=[pl.BlockSpec(memory_space=pltpu.HBM)] * 5,
        out_specs=pl.BlockSpec(memory_space=pltpu.VMEM),
        scratch_shapes=[
            pltpu.SMEM(row_live.shape, jnp.int32),
            pltpu.SMEM(col_live.shape, jnp.int32),
            pltpu.SMEM(plan.shape, jnp.int32),
            pltpu.SMEM((5, slots + 2), jnp.int32),
            pltpu.VMEM((slots + 2, width, chunk), f32),
            pltpu.VMEM((slots + 2, width, chunk), f32),
            pltpu.VMEM((slots, width, part), f32),
            pltpu.VMEM((items, width, part), f32),
            pltpu.VMEM((2, width, part), f32),
            pltpu.VMEM((2, width, part), f32),
            pltpu.VMEM((chunks, width, part), f32),
            pltpu.VMEM((panels, width, width), f32),
            pltpu.VMEM((CORES, width // CORES, width), f32),
            pltpu.VMEM((panels, width, width), f32),
            pltpu.VMEM((panels, width, width), bf16),
            pltpu.VMEM((panels, width, width), bf16),
            pltpu.VMEM((width, chunk), bf16),
            pltpu.VMEM((width, chunk), bf16),
            dma((chunks,)), dma((3,)),
            dma((slots + 2, PARTS)), dma((slots + 2, PARTS)),
            dma((slots + 2, GROUPS)), dma((slots + 2, GROUPS)),
            dma((2, PARTS)), dma((2,)), dma((2,)),
            dma((chunks,)), dma((chunks,)), dma((chunks,)), dma((chunks,)),
            dma((panels, n_row)), dma((panels, n_row)), dma((panels, n_row)), dma((panels, n_row)),
            dma((panels,)), dma, dma, dma,
            dma((panels, n_chip, 2)), dma((panels, 2)), dma((panels,)), dma((panels,)), dma((panels,)),
        ],
        compiler_params=pltpu.CompilerParams(
            collective_id=1 + arm, has_side_effects=True, vmem_limit_bytes=GRANT - 4 * rows * columns
        ),
    )(row_live, col_live, plan, matrix, pivot_inverse)


def per_device(n_row, n_col, matrix, pivot_inverse, row_live, col_live):
    width = pivot_inverse.shape[2]
    chunk = min(CHUNK, width)
    chunks, per_block = matrix.shape[1] // chunk, width // chunk
    smem = pl.BlockSpec(memory_space=pltpu.SMEM)
    plan = pl.pallas_call(
        functools.partial(plan_kernel, n_row, n_col, chunks, per_block),
        out_shape=jax.ShapeDtypeStruct((1 + 2 * n_col,), jnp.int32),
        in_specs=[smem, smem],
        out_specs=smem,
    )(row_live, col_live)
    arms = [functools.partial(sparse, arm, n_row, n_col) for arm in range(ARMS)]
    arms.append(functools.partial(dense, n_row, n_col))
    return lax.switch(plan[0], arms, plan, matrix, pivot_inverse, row_live, col_live)


def solution(mesh):
    n_row, n_col = mesh.shape["prow"], mesh.shape["pcol"]
    return jax.shard_map(
        functools.partial(per_device, n_row, n_col),
        mesh=mesh,
        in_specs=(P("prow", "pcol"), P(None, "prow", None), P(), P()),
        out_specs=P("prow", "pcol"),
        check_vma=False,
    )
```

```python
import functools

import jax
import jax.numpy as jnp
from jax import lax
from jax.experimental import pallas as pl
from jax.experimental.pallas import tpu as pltpu
from jax.sharding import PartitionSpec as P

MESH = pl.DeviceIdType.MESH
CORES = 2
CHUNK = 256
PIECES = 16
TAIL = 4
GUESTS = 28
GRANT = 67_043_328
PARTS = 8
GROUPS = 4
ARMS = 5
PACE = 3


def split(x):
    high = x.astype(jnp.bfloat16)
    return high, (x - high.astype(jnp.float32)).astype(jnp.bfloat16)


def product(left_high, left_low, right_high, right_low):
    dot = functools.partial(jnp.dot, preferred_element_type=jnp.float32)
    return dot(left_high, right_high) + (dot(left_high, right_low) + dot(left_low, right_high))


def kernel(
    n_row, n_col, chunk, row_hbm, col_hbm, mat, piv, acc,
    row_smem, col_smem, u, p, a, guest, low, low_high, low_rest, u_high, u_rest,
    acc_sem, mask_sem, u_send, u_recv, p_send, p_recv, p_pass, p_passed, p_own,
    a_own, a_send, a_recv, t_send, t_recv, l_send, l_recv, l_pass, l_passed,
    p_up, g_in, g_recv, g_down, g_out,
):
    z, pcol = lax.axis_index("prow"), lax.axis_index("pcol")
    core, chip = lax.rem(pcol, CORES), lax.div(pcol, CORES)
    n_chip = n_col // CORES
    partner = (z, pcol + 1 - 2 * core)
    width, half = piv.shape[2], piv.shape[2] // CORES
    rows_own = piv.shape[1]
    rows_half = rows_own // CORES
    chunks = acc.shape[1] // chunk
    per_block = width // chunk
    pieces = u_send.shape[1] // chunks
    piece = width // pieces
    steps = chunks * pieces
    last = n_row - 1
    guests = guest.shape[1]
    guest_start = (chunks - 2) * pieces
    first_chip, active, both = chip == 0, z > 0, z > 1
    guest_end = guest_start + jnp.where(chip > 0, guests, 0)

    def remote(src, dst, send, recv, to):
        return pltpu.make_async_remote_copy(
            src_ref=src, dst_ref=dst, send_sem=send, recv_sem=recv, device_id=to, device_id_type=MESH
        )

    masks = [
        pltpu.make_async_copy(row_hbm, row_smem, mask_sem.at[0]),
        pltpu.make_async_copy(col_hbm, col_smem, mask_sem.at[1]),
    ]

    def columns_of(j):
        start = j * chunk
        return pl.ds(start if isinstance(j, int) else pl.multiple_of(start, 128), chunk)

    def load(j):
        return pltpu.make_async_copy(mat.at[:, columns_of(j)], acc.at[:, columns_of(j)], acc_sem.at[j])

    def pivot_own(k):
        return pltpu.make_async_copy(piv.at[k], p.at[k, pl.ds(z * rows_own, rows_own)], p_own.at[k])

    def pivot_rows(k, source):
        return p.at[k, pl.ds(pl.multiple_of(source * rows_own + core * rows_half, 8), rows_half)]

    def pivot_send(k, target, send):
        return remote(
            piv.at[k, pl.ds(pl.multiple_of(core * rows_half, 8), rows_half)],
            pivot_rows(k, z), send, p_recv.at[k, z], (target, pcol),
        )

    def pivot_relay(k, source, target):
        return remote(pivot_rows(k, source), pivot_rows(k, source), p_send.at[k, source], p_recv.at[k, source], (target, pcol))

    def pivot_landed(k, source):
        return remote(pivot_rows(k, source), pivot_rows(k, source), p_send.at[k, source], p_recv.at[k, source], (z, pcol))

    def pivot_pass(k, source):
        return remote(pivot_rows(k, source), pivot_rows(k, source), p_pass.at[k, source], p_passed.at[k, source], partner)

    def piece_of(ref, j, r):
        return ref.at[j, pl.ds(pl.multiple_of(r * piece, 8), piece)]

    def relay_copy(k, s):
        place = piece_of(u.at[k], s // pieces, s % pieces)
        return remote(place, place, u_send.at[k, s], u_recv.at[k, s], (z + 1, pcol))

    def origin_copy(k, s):
        j, r = s // pieces, s % pieces
        rows = pl.ds(pl.multiple_of(r * piece, 8), piece)
        return remote(acc.at[rows, columns_of(j)], piece_of(u.at[k], j, r), u_send.at[k, s], u_recv.at[k, s], (z + 1, pcol))

    def start_of(k):
        return jnp.where(pcol <= k, per_block * pieces, 0)

    def relay(k, begin, end):
        def body(s, carry):
            copy = relay_copy(k, s)
            copy.wait_recv()

            @pl.when(z < last)
            def _():
                copy.start()

            return carry

        lax.fori_loop(jnp.maximum(begin, start_of(k)), end, body, 0)

    def originate(k, begin, end):
        def body(s, carry):
            origin_copy(k, s).start()
            return carry

        lax.fori_loop(jnp.maximum(begin, start_of(k)), end, body, 0)

    def finish_sends(k, copy):
        def body(s, carry):
            copy(k, s).wait_send()
            return carry

        if k:
            lax.fori_loop(start_of(k), guest_start, body, 0)
            lax.fori_loop(guest_end, steps, body, 0)
        else:
            lax.fori_loop(start_of(k), steps, body, 0)

    def guest_in(i):
        rows = pl.ds(i * piece, piece)
        source = acc.at[rows, columns_of(guest_start // pieces)]
        return remote(source, guest.at[chip, i], g_in.at[i], g_recv.at[chip, i], (z, core))

    def guest_down(q, i):
        return remote(guest.at[q, i], guest.at[q, i], g_down.at[q, i], g_recv.at[q, i], (z + 1, pcol))

    def guest_out(q, i):
        target = piece_of(u.at[1], guest_start // pieces, i)
        return remote(guest.at[q, i], target, g_out.at[q, i], u_recv.at[1, guest_start + i], (z, q * CORES + core))

    def pass_guests():
        def body(t, carry):
            q, i = 1 + t // guests, t % guests
            guest_down(q, i).wait_recv()

            @pl.when(z < last)
            def _():
                guest_down(q, i).start()

            @pl.when(both)
            def _():
                guest_out(q, i).start()

            return carry

        lax.fori_loop(0, (n_chip - 1) * guests, body, 0)

    def finish_guests():
        def body(t, carry):
            q, i = 1 + t // guests, t % guests

            @pl.when(z < last)
            def _():
                guest_down(q, i).wait_send()

            @pl.when(both)
            def _():
                guest_out(q, i).wait_send()

            return carry

        lax.fori_loop(0, (n_chip - 1) * guests, body, 0)

    def own_rows():
        return pl.ds(pl.multiple_of(core * half, 8), half)

    def lower_send(k, target):
        rows = low.at[k, own_rows()]
        return remote(rows, rows, l_send.at[k, target], l_recv.at[k], (z, target * CORES + core))

    def lower_pass(k):
        rows = low.at[k, own_rows()]
        return remote(rows, rows, l_pass.at[k], l_passed.at[k], partner)

    def row_mask(k):
        return row_smem[k, z].astype(jnp.float32)

    def for_sources(k, visit):
        for distance in range(1, n_row):
            @pl.when(z - distance >= 0)
            def _():
                visit(z - distance, z + 1, z < last, z > k)

            @pl.when((z + distance <= last) & (z > k))
            def _():
                visit(z + distance, z - 1, z - 1 > k, z > k)

    def relay_pivot(k):
        def visit(source, target, onward, used):
            pivot_landed(k, source).wait_recv()

            @pl.when(onward)
            def _():
                pivot_relay(k, source, target).start()

            @pl.when(used)
            def _():
                pivot_pass(k, source).start()

        for_sources(k, visit)

    def gather_pivot(k):
        pivot_own(k).wait()
        for source in range(n_row):
            @pl.when(z != source)
            def _():
                pivot_pass(k, source).wait_recv()

    def finish_pivot(k):
        def visit(source, target, onward, used):
            @pl.when(onward)
            def _():
                pivot_relay(k, source, target).wait_send()

            @pl.when(used)
            def _():
                pivot_pass(k, source).wait_send()

        for_sources(k, visit)

    def apply_pivot(k, left):
        left_high, left_low = split(left)
        for q in range(per_block):
            columns = pl.ds(q * chunk, chunk)
            right = split(p[k, :, columns])
            low[k, own_rows(), columns] = row_mask(k) * product(left_high, left_low, *right)
        for target in range(n_chip - 1, 0, -1):
            lower_send(k, target).start()
        lower_pass(k).start()

    def take_lower(k):
        @pl.when(chip > 0)
        def _():
            lower_send(k, 0).wait_recv()
            lower_pass(k).start()

        lower_pass(k).wait_recv()
        low_high[k], low_rest[k] = split(low[k])

    def update(k, j, part=0, parts=1):
        live = col_smem[k, pcol + (j // per_block) * n_col].astype(jnp.float32)

        def run():
            depth = pl.ds(part * (width // parts), width // parts)
            u_high[depth], u_rest[depth] = split(u[k, j, depth])
            for t in range(CORES):
                rows = pl.ds(t * half, half)
                left = low_high[k, rows, depth], low_rest[k, rows, depth]
                acc[rows, columns_of(j)] -= live * product(*left, u_high[depth], u_rest[depth])

        if j < per_block:
            pl.when(pcol > k)(run)
        else:
            run()

    def store_lower(k):
        @pl.when(pcol == k)
        def _():
            acc[:, pl.ds(0, width)] = low[k]

    barrier = pltpu.get_barrier_semaphore()
    relays_guests = (z == 1) & (z < last)

    def greet(condition, device):
        @pl.when(condition)
        def _():
            pl.semaphore_signal(barrier, inc=1, device_id=device, device_id_type=MESH)

    greet(active, (z - 1, pcol))
    greet(active, partner)
    greet(active & (z < last) & first_chip, (z + 1, pcol))
    greet(active & (chip > 0), (z, core))
    for other in range(1, n_chip):
        greet(relays_guests & first_chip, (z, other * CORES + core))

    for j in range(chunks):
        load(j).start()
    for copy in masks:
        copy.start()

    @pl.when(first_chip & active)
    def _():
        for k in range(2):
            pivot_own(k).start()
        pltpu.make_async_copy(mat.at[own_rows(), pl.ds(0, width)], a.at[core], a_own).start()

    targets = (
        jnp.where(z < last, 1, 0)
        + jnp.where(active, 1, 0)
        + jnp.where(both & first_chip, 1, 0)
        + jnp.where(active & first_chip, n_chip - 1, 0)
        + jnp.where(relays_guests & (chip > 0), 1, 0)
    )
    pl.semaphore_wait(barrier, targets)

    def swap_columns():
        source = mat.at[pl.ds(pl.multiple_of((1 - core) * half, 8), half), pl.ds(0, width)]
        return remote(source, a.at[core], a_send, a_recv, partner)

    def swapped_columns():
        return remote(a.at[1 - core], a.at[1 - core], a_send, a_recv, partner)

    @pl.when(first_chip)
    def _():
        for k in range(2):
            @pl.when(z < last)
            def _():
                pivot_send(k, z + 1, p_send.at[k, z]).start()

            @pl.when(z - 1 > k)
            def _():
                pivot_send(k, z - 1, p_up.at[k]).start()

        @pl.when(active)
        def _():
            swap_columns().start()

    for j in range(chunks):
        load(j).wait()

        @pl.when(z == 0)
        def _():
            originate(0, j * pieces, (j + 1) * pieces)

    for copy in masks:
        copy.wait()

    @pl.when(active)
    def _():
        @pl.when(first_chip)
        def _():
            relay_pivot(0)
            gather_pivot(0)
            pltpu.make_async_copy(mat.at[own_rows(), pl.ds(0, width)], a.at[core], a_own).wait()
            swapped_columns().wait_recv()
            apply_pivot(0, a[0])
            relay_pivot(1)

        ahead = jnp.where(pcol == 0, steps - TAIL, per_block * pieces)
        relay(0, 0, ahead)

        @pl.when(first_chip & both)
        def _():
            top = u.at[0, pl.ds(0, per_block)]
            copy = remote(top, top, t_send, t_recv, partner)

            @pl.when(core == 1)
            def _():
                copy.start()

            gather_pivot(1)

            @pl.when(core == 0)
            def _():
                copy.wait_recv()

            live = col_smem[0, 1].astype(jnp.float32)
            left = split(low[0, own_rows()])
            for q in range(per_block):
                columns = pl.ds(q * chunk, chunk)
                a[1, :, columns] -= live * product(*left, *split(u[0, q]))
            apply_pivot(1, a[1])

            @pl.when(core == 1)
            def _():
                copy.wait_send()

        relay(0, ahead, steps - TAIL)
        take_lower(0)
        for j in range(chunks - 1):
            update(0, j)
            relay(0, steps - TAIL + j, steps - TAIL + j + 1)
        relay(0, steps - TAIL + chunks - 1, steps)

        @pl.when(z == 1)
        def _():
            @pl.when(z < last)
            def _():
                @pl.when(chip > 0)
                def _():
                    for i in range(guests):
                        guest_in(i).start()

                originate(1, 0, guest_start)
                originate(1, guest_end, steps - pieces)

                @pl.when(first_chip)
                def _():
                    pass_guests()

            update(0, chunks - 1)

            @pl.when(z < last)
            def _():
                originate(1, steps - pieces, steps)

            store_lower(0)

        @pl.when(both)
        def _():
            relay(1, 0, pieces)
            update(0, chunks - 1)
            relay(1, pieces, guest_start)
            take_lower(1)
            update(1, 0)
            relay(1, guest_end, guest_end + 4)
            update(1, 1)
            store_lower(0)
            store_lower(1)
            relay(1, guest_end + 4, steps - pieces)

            @pl.when(first_chip)
            def _():
                pass_guests()

            @pl.when(chip > 0)
            def _():
                for i in range(guests):
                    relay_copy(1, guest_start + i).wait_recv()

            for j in range(2, chunks - 1):
                update(1, j)
            for part in range(4):
                begin = steps - pieces + part * (pieces // 4)
                relay(1, begin, begin + pieces // 4)
                update(1, chunks - 1, part, 4)

    @pl.when(z == 0)
    def _():
        finish_sends(0, origin_copy)

    @pl.when(active & first_chip)
    def _():
        @pl.when((z < last) | both)
        def _():
            finish_guests()

    @pl.when((z == 1) & (z < last) & (chip > 0))
    def _():
        for i in range(guests):
            guest_in(i).wait_send()

    @pl.when(active & (z < last))
    def _():
        finish_sends(0, relay_copy)

        @pl.when(z == 1)
        def _():
            finish_sends(1, origin_copy)

        @pl.when(both)
        def _():
            finish_sends(1, relay_copy)

    @pl.when(first_chip)
    def _():
        for k in range(2):
            @pl.when(z < last)
            def _():
                pivot_send(k, z + 1, p_send.at[k, z]).wait_send()

            @pl.when(z - 1 > k)
            def _():
                pivot_send(k, z - 1, p_up.at[k]).wait_send()

            finish_pivot(k)

    @pl.when(first_chip & (z == 1))
    def _():
        pivot_own(1).wait()

    for k in range(2):
        @pl.when(z > k)
        def _():
            lower_pass(k).wait_send()

            @pl.when(first_chip)
            def _():
                for target in range(n_chip - 1, 0, -1):
                    lower_send(k, target).wait_send()
                if k == 0:
                    swap_columns().wait_send()


def dense(n_row, n_col, plan, matrix, pivot_inverse, row_live, col_live):
    rows, columns = matrix.shape
    panels, rows_own, width = pivot_inverse.shape
    chunk = min(CHUNK, width)
    chunks = columns // chunk
    steps = chunks * PIECES
    n_chip = n_col // CORES
    guests = max(1, GUESTS // n_chip)
    f32, bf16, dma = jnp.float32, jnp.bfloat16, pltpu.SemaphoreType.DMA
    return pl.pallas_call(
        functools.partial(kernel, n_row, n_col, chunk),
        out_shape=pltpu.VMEM((rows, columns), f32),
        in_specs=[pl.BlockSpec(memory_space=pltpu.HBM)] * 4,
        out_specs=pl.BlockSpec(memory_space=pltpu.VMEM),
        scratch_shapes=[
            pltpu.SMEM(row_live.shape, jnp.int32),
            pltpu.SMEM(col_live.shape, jnp.int32),
            pltpu.VMEM((panels, chunks, width, chunk), f32),
            pltpu.VMEM((panels, width, width), f32),
            pltpu.VMEM((CORES, width // CORES, width), f32),
            pltpu.VMEM((n_chip, guests, width // PIECES, chunk), f32),
            pltpu.VMEM((panels, width, width), f32),
            pltpu.VMEM((panels, width, width), bf16),
            pltpu.VMEM((panels, width, width), bf16),
            pltpu.VMEM((width, chunk), bf16),
            pltpu.VMEM((width, chunk), bf16),
            dma((chunks,)), dma((2,)),
            dma((panels, steps)), dma((panels, steps)),
            dma((panels, n_row)), dma((panels, n_row)), dma((panels, n_row)), dma((panels, n_row)),
            dma((panels,)), dma, dma, dma, dma, dma,
            dma((panels, n_col // CORES)), dma((panels,)), dma((panels,)), dma((panels,)),
            dma((panels,)), dma((guests,)), dma((n_chip, guests)), dma((n_chip, guests)), dma((n_chip, guests)),
        ],
        compiler_params=pltpu.CompilerParams(
            collective_id=0, has_side_effects=True, vmem_limit_bytes=GRANT - 4 * rows * columns
        ),
    )(row_live, col_live, matrix, pivot_inverse)


def neighbour(chip, bit):
    return chip + bit * (1 - 2 * lax.rem(lax.div(chip, bit), 2))


def live_items(row, col, chip, n_row, n_col, chunks, per_block):
    used = row[1, 2]
    for g in range(3, n_row):
        used = jnp.maximum(used, row[1, g])
    zero, one = [], []
    for j in range(CORES * chunks):
        h = chip * CORES + j % CORES + j // CORES // per_block * n_col
        zero.append(jnp.where(h > 0, col[0, h], 0))
        one.append(jnp.where(h > 1, col[1, h] * used, 0))
    return zero, one


def total(values):
    return functools.reduce(lambda x, y: x + y, values, jnp.int32(0))


def plan_kernel(n_row, n_col, chunks, per_block, row, col, out):
    n_chip, items = n_col // CORES, CORES * chunks
    half, final = items // 2, items - CORES
    lane = lax.broadcasted_iota(jnp.int32, (8, 128), 0) * 128 + lax.broadcasted_iota(jnp.int32, (8, 128), 1)
    lane = lane.astype(jnp.float32)
    digits = []
    rest = lane
    for _ in range(4):
        next_rest = jnp.floor((rest + 0.5) / 5)
        digits.append(rest - 5 * next_rest - 2)
        rest = next_rest
    size = [jnp.abs(f) for f in digits]
    moves = sum(size)
    x_size, y_size = jnp.maximum(size[0], size[1]), jnp.maximum(size[2], size[3])
    needed = items + 1 + jnp.maximum(jnp.maximum(2 * x_size - 1, 2 * y_size), 0)
    longest = jnp.int32(0)
    for quad in range(n_chip // 4):
        worst = needed
        for i in range(4):
            zero, one = live_items(row, col, quad * 4 + i, n_row, n_col, chunks, per_block)
            both = [x * y for x, y in zip(zero, one)]
            early = total(both[:half]).astype(jnp.float32)
            holes = total([(1 - zero[j]) * (1 - one[j]) for j in range(final, items)]).astype(jnp.float32)
            count = total(both).astype(jnp.float32)
            x = digits[i // 2] * (1 - 2 * (i % 2))
            y = digits[2 + i % 2] * (1 - 2 * (i // 2))
            sent = jnp.maximum(x, 0) + jnp.maximum(y, 0)
            load = items + count - x - y - jnp.minimum(holes, early - sent)
            worst = jnp.maximum(worst, jnp.where(sent > early, 99.0, load))
        key = jnp.where(rest > 0.5, 1e7, (worst * 16 + moves) * 1024 + lane)
        best = jnp.min(key).astype(jnp.int32)
        longest = jnp.maximum(longest, lax.div(best, 16384))
        code = lax.rem(best, 1024)
        for e in range(4):
            out[1 + quad * 4 + e] = lax.rem(code, 5) - 2
            code = lax.div(code, 5)
    out[0] = jnp.minimum(jnp.maximum(longest - items - 2, 0), ARMS)


def sparse_kernel(
    slots, n_row, n_col, chunk, row_hbm, col_hbm, plan_hbm, mat, piv, acc,
    row_smem, col_smem, plan, tab, pos, prod, tx, own, out_guest, in_guest, back,
    p, a, low, low_high, low_rest, u_high, u_rest,
    acc_sem, mask_sem, d_send, d_recv, f_send, f_recv, r_send, e_send, e_recv, s_send, s_recv, b_send, b_recv,
    p_send, p_recv, p_pass, p_passed, p_own, a_own, a_send, a_recv, l_send, l_recv, l_pass, l_passed, p_up, turn_sem,
):
    z, pcol = lax.axis_index("prow"), lax.axis_index("pcol")
    core, chip = lax.rem(pcol, CORES), lax.div(pcol, CORES)
    n_chip = n_col // CORES
    partner = (z, pcol + 1 - 2 * core)
    width, half = piv.shape[2], piv.shape[2] // CORES
    rows_own = piv.shape[1]
    rows_half = rows_own // CORES
    chunks = acc.shape[1] // chunk
    per_block = width // chunk
    items = CORES * chunks
    part = chunk // CORES
    piece = width // PARTS
    last = n_row - 1
    lanes = out_guest.shape[0]
    first_chip, active, both = chip == 0, z > 0, z > 1
    mine = pl.ds(pl.multiple_of(core * part, 128), part)

    def remote(src, dst, send, recv, to):
        return pltpu.make_async_remote_copy(
            src_ref=src, dst_ref=dst, send_sem=send, recv_sem=recv, device_id=to, device_id_type=MESH
        )

    masks = [
        pltpu.make_async_copy(row_hbm, row_smem, mask_sem.at[0]),
        pltpu.make_async_copy(col_hbm, col_smem, mask_sem.at[1]),
        pltpu.make_async_copy(plan_hbm, plan, mask_sem.at[2]),
    ]

    def columns_of(j):
        start = j * chunk
        return pl.ds(start if isinstance(j, int) else pl.multiple_of(start, 128), chunk)

    def part_of(j, side):
        return pl.ds(pl.multiple_of(j * chunk + side * part, 128), part)

    def rows_of(r):
        return pl.ds(pl.multiple_of(r * piece, 8), piece)

    def load(j):
        return pltpu.make_async_copy(mat.at[:, columns_of(j)], acc.at[:, columns_of(j)], acc_sem.at[j])

    def pivot_own(k):
        return pltpu.make_async_copy(piv.at[k], p.at[k, pl.ds(z * rows_own, rows_own)], p_own.at[k])

    def pivot_rows(k, source):
        return p.at[k, pl.ds(pl.multiple_of(source * rows_own + core * rows_half, 8), rows_half)]

    def pivot_send(k, target, send):
        return remote(
            piv.at[k, pl.ds(pl.multiple_of(core * rows_half, 8), rows_half)],
            pivot_rows(k, z), send, p_recv.at[k, z], (target, pcol),
        )

    def pivot_relay(k, source, target):
        return remote(pivot_rows(k, source), pivot_rows(k, source), p_send.at[k, source], p_recv.at[k, source], (target, pcol))

    def pivot_landed(k, source):
        return remote(pivot_rows(k, source), pivot_rows(k, source), p_send.at[k, source], p_recv.at[k, source], (z, pcol))

    def pivot_pass(k, source):
        return remote(pivot_rows(k, source), pivot_rows(k, source), p_pass.at[k, source], p_passed.at[k, source], partner)

    def own_rows():
        return pl.ds(pl.multiple_of(core * half, 8), half)

    def lower_send(k, target, q):
        rows = low.at[k, pl.ds(pl.multiple_of(core * half + q * (half // 2), 8), half // 2)]
        return remote(rows, rows, l_send.at[k, target, q], l_recv.at[k, q], (z, target * CORES + core))

    member = lax.rem(chip, 4)
    direct = [t for t in range(1, n_chip) if t % 4 < 3]

    def relay_lower(k):
        for q in range(2):
            @pl.when(member == 1 + q)
            def _():
                lower_send(k, chip, q).wait_recv()
                lower_send(k, chip + 2 - q, q).start()

    def lower_pass(k):
        rows = low.at[k, own_rows()]
        return remote(rows, rows, l_pass.at[k], l_passed.at[k], partner)

    def row_mask(k):
        return row_smem[k, z].astype(jnp.float32)

    def for_sources(k, visit):
        for distance in range(1, n_row):
            @pl.when(z - distance >= 0)
            def _():
                visit(z - distance, z + 1, z < last, z > k)

            @pl.when((z + distance <= last) & (z > k))
            def _():
                visit(z + distance, z - 1, z - 1 > k, z > k)

    def relay_pivot(k):
        def visit(source, target, onward, used):
            pivot_landed(k, source).wait_recv()

            @pl.when(onward)
            def _():
                pivot_relay(k, source, target).start()

            @pl.when(used)
            def _():
                pivot_pass(k, source).start()

        for_sources(k, visit)

    def gather_pivot(k):
        pivot_own(k).wait()
        for source in range(n_row):
            @pl.when(z != source)
            def _():
                pivot_pass(k, source).wait_recv()

    def finish_pivot(k):
        def visit(source, target, onward, used):
            @pl.when(onward)
            def _():
                pivot_relay(k, source, target).wait_send()

            @pl.when(used)
            def _():
                pivot_pass(k, source).wait_send()

        for_sources(k, visit)

    def apply_pivot(k, left):
        left_high, left_low = split(left)

        def visit(q):
            right = split(p[k, :, columns_of(q)])
            low[k, own_rows(), columns_of(q)] = row_mask(k) * product(left_high, left_low, *right)

        loop(0, per_block, visit)
        for turn in range(2):
            for target in direct:
                lower_send(k, target, 1 - turn if target % 4 == 2 else turn).start()
        lower_pass(k).start()

    def take_lower(k):
        @pl.when(chip > 0)
        def _():
            for q in range(2):
                @pl.when(member != 1 + q)
                def _():
                    lower_send(k, 0, q).wait_recv()

            lower_pass(k).start()

        lower_pass(k).wait_recv()

        def visit(r):
            low_high[k, rows_of(r)], low_rest[k, rows_of(r)] = split(low[k, rows_of(r)])

        loop(0, PARTS, visit)

    def store_lower(k):
        @pl.when(pcol == k)
        def _():
            acc[:, pl.ds(0, width)] = low[k]

    def swap_columns():
        source = mat.at[pl.ds(pl.multiple_of((1 - core) * half, 8), half), pl.ds(0, width)]
        return remote(source, a.at[core], a_send, a_recv, partner)

    def swapped_columns():
        return remote(a.at[1 - core], a.at[1 - core], a_send, a_recv, partner)

    def carried(j):
        return jnp.logical_not(first_chip & (lax.rem(j, 2) == 0) & (j < CORES * per_block))

    def upper_send(jj, side, r):
        j = CORES * jj + core
        return remote(
            mat.at[rows_of(r), part_of(jj, side)], pos.at[j, rows_of(r), pl.ds(pl.multiple_of(side * part, 128), part)],
            d_send.at[CORES * jj + side, r], d_recv.at[j, r], (z + 1, chip * CORES + side),
        )

    def down(source, s, r):
        return remote(source, pos.at[s, rows_of(r), mine], d_send.at[s, r], d_recv.at[s, r], (z + 1, pcol))

    def down_staged(s, r):
        return down(tx.at[s, rows_of(r)], s, r)

    def down_relay(s, r):
        return down(pos.at[s, rows_of(r), mine], s, r)

    def landed(s, r):
        place = pos.at[s, rows_of(r), mine]
        return remote(place, place, d_send.at[s, r], d_recv.at[s, r], (z, pcol))

    def give_back(b, r):
        place = pos.at[items + b, rows_of(r), mine]
        target = pos.at[slots + b, rows_of(r), mine]
        to = (z, neighbour(chip, 1 + b % 2) * CORES + core)
        return remote(place, target, r_send.at[b, r], d_recv.at[slots + b, r], to)

    def group_rows(g):
        return pl.ds(pl.multiple_of(g * (width // GROUPS), 8), width // GROUPS)

    def forward(s, g):
        place = pos.at[s, group_rows(g), mine]
        return remote(place, place, f_send.at[s, g], f_recv.at[s, g], partner)

    def export(b):
        to = (z, neighbour(chip, 1 + b % 2) * CORES + core)
        return remote(out_guest.at[b], in_guest.at[b], e_send.at[b], e_recv.at[b], to)

    def swap_own(jj):
        source = acc.at[:, part_of(jj, 1 - core)]
        return remote(source, own.at[CORES * jj + core], s_send.at[jj], s_recv.at[jj], partner)

    def swapped_own(jj):
        place = own.at[CORES * jj + 1 - core]
        return remote(place, place, s_send.at[jj], s_recv.at[jj], partner)

    def hand_back(jj):
        return remote(own.at[CORES * jj + 1 - core], back.at[jj], b_send.at[jj], b_recv.at[jj], partner)

    def loop(begin, end, visit):
        def body(i, carry):
            visit(i)
            return carry

        lax.fori_loop(begin, end, body, 0)

    barrier = pltpu.get_barrier_semaphore()

    def greet(condition, device):
        @pl.when(condition)
        def _():
            pl.semaphore_signal(barrier, inc=1, device_id=device, device_id_type=MESH)

    greet(active, (z - 1, pcol))
    greet(z == 1, (z - 1, pcol + 1 - 2 * core))
    greet(active | (pcol == 0), partner)
    greet(active & (z < last) & first_chip, (z + 1, pcol))
    greet(active & (chip > 0), (z, core))
    for bit in (1, 2):
        near = neighbour(chip, bit)
        greet(active & (near > 0), (z, near * CORES + core))

    for j in range(chunks):
        load(j).start()
    for copy in masks:
        copy.start()

    @pl.when(first_chip & active)
    def _():
        for k in range(2):
            pivot_own(k).start()
        pltpu.make_async_copy(mat.at[own_rows(), pl.ds(0, width)], a.at[core], a_own).start()

    targets = (
        jnp.where(z < last, 1, 0)
        + jnp.where(z == 0, 1, 0)
        + jnp.where((z == 0) & (pcol == 1), 1, 0)
        + jnp.where(active, 1, 0)
        + jnp.where(both & first_chip, 1, 0)
        + jnp.where(active & first_chip, n_chip - 1, 0)
        + jnp.where(active & (chip > 0), 2, 0)
    )
    pl.semaphore_wait(barrier, targets)

    @pl.when(first_chip)
    def _():
        for k in range(2):
            @pl.when(z < last)
            def _():
                pivot_send(k, z + 1, p_send.at[k, z]).start()

            @pl.when(z - 1 > k)
            def _():
                pivot_send(k, z - 1, p_up.at[k]).start()

        @pl.when(active)
        def _():
            swap_columns().start()

    upper_start = jnp.where(pcol == 0, per_block * PARTS, 0)

    def upper_sent(s):
        for side in range(CORES):
            upper_send(lax.div(s, PARTS), side, lax.rem(s, PARTS)).wait_send()

    @pl.when(z == 0)
    def _():
        def visit(s):
            for side in range(CORES):
                upper_send(lax.div(s, PARTS), side, lax.rem(s, PARTS)).start()

        @pl.when(first_chip & (core == 0))
        def _():
            pl.semaphore_wait(turn_sem, 1)

        loop(upper_start, chunks * PARTS, visit)

        @pl.when(first_chip & (core == 1))
        def _():
            loop(0, per_block * PARTS, upper_sent)
            pl.semaphore_signal(turn_sem, inc=1, device_id=partner, device_id_type=MESH)

    for j in range(chunks):
        load(j).wait()

    @pl.when(z == 1)
    def _():
        for jj in range(chunks):
            swap_own(jj).start()

    for copy in masks:
        copy.wait()

    zero, one = live_items(row_smem, col_smem, chip, n_row, n_col, chunks, per_block)
    pair = [x * y for x, y in zip(zero, one)]
    rank, hole, order = [], [], []
    for j in range(items):
        rank.append(total(pair[:j]))
        hole.append((1 - zero[j]) * (1 - one[j]) if j >= items - CORES else jnp.int32(0))
        order.append(total(hole[:j]))
    quad = lax.div(chip, 4)
    flow_x = plan[1 + quad * 4 + lax.div(member, 2)] * (1 - 2 * lax.rem(member, 2))
    flow_y = plan[3 + quad * 4 + lax.rem(member, 2)] * (1 - 2 * lax.div(member, 2))
    x_out, y_out = jnp.maximum(flow_x, 0), jnp.maximum(flow_y, 0)
    x_in, y_in = jnp.maximum(-flow_x, 0), jnp.maximum(-flow_y, 0)
    sent = x_out + y_out
    filled = jnp.minimum(total(hole), total(pair[: items // 2]) - sent)

    def item_of(r):
        return total([jnp.where(rank[j] == r, j * pair[j], 0) for j in range(items)])

    for j in range(items):
        held = (1 - zero[j]) * one[j]
        moved = item_of(sent + order[j]) if j >= items - CORES else j
        tab[0, j] = zero[j]
        tab[1, j] = jnp.where(held > 0, j, jnp.where(order[j] < filled, moved, j))
    imported = [jnp.where((y_in if b % 2 else x_in) > b // 2, 1, 0) for b in range(lanes)]
    imported += [jnp.int32(0)] * (slots - items - lanes)
    place_of = [s - total(imported[:s]) for s in range(slots - items)]
    for s in range(slots - items):
        tab[0, items + s] = 0
        tab[1, items + s] = item_of(sent + filled + place_of[s])
    for b in range(lanes):
        tab[0, slots + b] = 0

    for jj in range(chunks):
        found = []
        for d in range(CORES):
            j = CORES * jj + d
            spare = rank[j] - sent
            fill = total([jnp.where(order[q] == spare, q * hole[q], 0) for q in range(items - CORES, items)])
            index = spare - filled
            late = total([jnp.where(place_of[s] == index, (items + s) * (1 - imported[s]), 0) for s in range(slots - items)])
            away = slots + jnp.where(rank[j] < x_out, 2 * rank[j], 2 * (rank[j] - x_out) + 1)
            place = jnp.where(spare < 0, away, jnp.where(spare < filled, fill, late))
            found.append(jnp.where(pair[j] > 0, place, j))
        tab[2, jj] = jnp.where(core == 0, found[0], found[1])
        tab[3, jj] = jnp.where(core == 0, one[CORES * jj], one[CORES * jj + 1])
        tab[4, jj] = jnp.where(core == 0, zero[CORES * jj], zero[CORES * jj + 1])

    def stage_pair(jj, begin, finish):
        def visit(r):
            for d in range(CORES):
                s = CORES * jj + d

                @pl.when(carried(s))
                def _():
                    landed(s, r).wait_recv()
                    upper = tab[0, s].astype(jnp.float32)
                    rows = rows_of(r)
                    tx[s, rows] = upper * pos[s, rows, mine] + (1 - upper) * own[tab[1, s], rows]

                    @pl.when(z < last)
                    def _():
                        down_staged(s, r).start()

        loop(begin, finish, visit)

    def stage_late(s):
        def visit(r):
            rows = rows_of(r)
            tx[s, rows] = own[tab[1, s], rows]

            @pl.when(z < last)
            def _():
                down_staged(s, r).start()

        loop(0, PARTS, visit)

    def stage_guest(b):
        export(b).wait_recv()
        keep = imported[b].astype(jnp.float32)

        def visit(r):
            rows = rows_of(r)
            tx[items + b, rows] = keep * in_guest[b, rows] + (1 - keep) * own[tab[1, items + b], rows]

            @pl.when(z < last)
            def _():
                down_staged(items + b, r).start()

        loop(0, PARTS, visit)

    def update_pair(jj):
        for d in range(CORES):
            side = pl.ds(d * part, part)
            u_high[:, side], u_rest[:, side] = split(pos[CORES * jj + d, :, mine])

        def visit(t):
            rows = pl.ds(pl.multiple_of(t * half, half), half)
            value = product(low_high[0, rows], low_rest[0, rows], u_high[...], u_rest[...])
            for d in range(CORES):
                s = CORES * jj + d

                @pl.when(carried(s))
                def _():
                    own[s, rows] -= tab[0, s].astype(jnp.float32) * value[:, d * part:(d + 1) * part]

        loop(0, CORES, visit)
        hand_back(jj).start()

    def keep_own(jj):
        acc[:, part_of(jj, core)] = own[CORES * jj + core]

    end = slots - 1
    late_slots = [end] + [slots + b for b in range(lanes) if items + 1 + b == end]
    side_groups = GROUPS // 2
    depth = width // 2

    def multiply(s, side):
        k = 1 - tab[0, s]
        deep = pl.ds(pl.multiple_of(side * depth, depth), depth)
        u_high[deep], u_rest[deep] = split(pos[s, deep])
        for t in range(CORES):
            rows = pl.ds(t * half, half)
            value = product(low_high[k, rows, deep], low_rest[k, rows, deep], u_high[deep], u_rest[deep])
            prod[s, rows] = value + jnp.where(side > 0, prod[s, rows], 0.0)

    def work(w):
        o, side = lax.div(w, 2), lax.rem(w, 2)
        later = o - items - 1
        turn = jnp.where(lax.rem(later, 2) == 0, slots, items + 1) + lax.div(later, 2)
        s = jnp.where(later < 0, o, jnp.where(later < 2 * lanes, turn, o - lanes))

        @pl.when(carried(s))
        def _():
            @pl.when(jnp.logical_not(first_chip & (s < CORES * per_block)))
            def _():
                for i in range(side_groups):
                    forward(s, side * side_groups + i).wait_recv()

            multiply(s, side)

    def arrive(s, g, relays=True):
        for i in range(PARTS // GROUPS):
            r = g * (PARTS // GROUPS) + i
            landed(s, r).wait_recv()
            if relays:
                @pl.when(z < last)
                def _():
                    down_relay(s, r).start()

                for b in range(lanes):
                    @pl.when(s == items + b)
                    def _():
                        give_back(b, r).start()
        forward(s, g).start()

    def arrive_pair(jj, begin=0, finish=GROUPS):
        def visit(g):
            for d in range(CORES):
                s = CORES * jj + d

                @pl.when(carried(s))
                def _():
                    arrive(s, g)

        loop(begin, finish, visit)

    def take_guest(b):
        loop(0, GROUPS, lambda g: arrive(slots + b, g, False))

    units = GROUPS * (slots - items)

    def limit(i):
        s, g = items + lax.div(i, GROUPS), lax.rem(i, GROUPS)
        b = s - items - 1
        guest = jnp.where((b >= 0) & (b < lanes), 2, 0)
        whole = 2 * (s + jnp.minimum(jnp.maximum(b, 0), lanes)) + lax.div(g, side_groups) * (1 + guest)
        paced = jnp.where(i < units - GROUPS, jnp.minimum(whole, PACE * (i + 1)), whole)
        return jnp.where(i < units, paced, 2 * (slots + lanes))

    def settle():
        def visit(t):
            jj, rows = lax.div(t, PARTS), rows_of(lax.rem(t, PARTS))
            place = tab[2, jj]
            ready = tab[3, jj] > 0
            for s in late_slots:
                ready = ready & (place != s)
            upper = jnp.where(tab[4, jj] > 0, prod[CORES * jj + core, rows], 0.0)
            acc[rows, columns_of(jj)] -= upper + jnp.where(ready, prod[place, rows], 0.0)

        loop(0, chunks * PARTS, visit)

    def settle_late():
        def visit(t):
            rows = rows_of(t)
            values = [prod[s, rows] for s in late_slots]
            for jj in range(chunks):
                flags = [jnp.where(tab[2, jj] == s, tab[3, jj], 0).astype(jnp.float32) for s in late_slots]
                acc[rows, columns_of(jj)] -= functools.reduce(jnp.add, [f * v for f, v in zip(flags, values)])

        loop(0, PARTS, visit)

    def make_lower():
        gather_pivot(0)
        pltpu.make_async_copy(mat.at[own_rows(), pl.ds(0, width)], a.at[core], a_own).wait()
        swapped_columns().wait_recv()
        apply_pivot(0, a[0])

    @pl.when(active & first_chip)
    def _():
        relay_pivot(0)
        relay_pivot(1)

    @pl.when(z == 1)
    def _():
        for jj in range(chunks):
            own[CORES * jj + core] = acc[:, part_of(jj, core)]
            swapped_own(jj).wait_recv()

        steps = chunks * GROUPS
        updates = [2 * GROUPS + 2, 2 * GROUPS + 3, 3 * GROUPS + 1, steps]

        def visit(t):
            @pl.when(t < steps)
            def _():
                begin = lax.rem(t, GROUPS) * (PARTS // GROUPS)
                stage_pair(lax.div(t, GROUPS), begin, begin + PARTS // GROUPS)

            @pl.when((t == 1) & first_chip)
            def _():
                make_lower()

            @pl.when(t == 2 * GROUPS - 2)
            def _():
                relay_lower(0)

            @pl.when(t == 2 * GROUPS + 1)
            def _():
                take_lower(0)

            @pl.when(t == steps)
            def _():
                stage_guest(0)

            @pl.when(functools.reduce(jnp.logical_or, [t == u for u in updates]))
            def _():
                update_pair(sum(jnp.where(t > u, 1, 0) for u in updates))

            @pl.when(t == updates[1])
            def _():
                for b in range(lanes):
                    out_guest[b] = own[item_of((x_out if b % 2 else 0) + b // 2)]
                    export(b).start()

        loop(0, steps + 1, visit)
        for b in range(1, lanes):
            stage_guest(b)
        loop(items + lanes, slots, stage_late)
        for jj in range(chunks):
            hand_back(jj).wait_recv()
            swap_own(jj).wait_send()
            acc[:, part_of(jj, 1 - core)] = back[jj]
            keep_own(jj)
        store_lower(0)

    @pl.when(both)
    def _():
        pl.when(first_chip)(make_lower)
        loop(0, per_block - 1, arrive_pair)
        arrive_pair(per_block - 1, 0, side_groups)
        relay_lower(0)
        arrive_pair(per_block - 1, side_groups, GROUPS)

        @pl.when(first_chip)
        def _():
            gather_pivot(1)
            live = tab[0, 1].astype(jnp.float32)
            left = split(low[0, own_rows()])

            def visit(q):
                for g in range(GROUPS):
                    forward(CORES * q + 1, g).wait_recv()
                a[1, :, columns_of(q)] -= live * product(*left, *split(pos[CORES * q + 1]))

            loop(0, per_block, visit)
            apply_pivot(1, a[1])

        loop(per_block, chunks - 1, arrive_pair)
        arrive_pair(chunks - 1, 0, 1)
        relay_lower(1)
        arrive_pair(chunks - 1, 1, GROUPS)
        loop(0, 2, take_lower)

        def unit(i):
            @pl.when(i < units)
            def _():
                arrive(items + lax.div(i, GROUPS), lax.rem(i, GROUPS))

            start = jnp.where(i > 0, limit(i - 1), 0)

            b = lax.div(i, GROUPS) - 1

            @pl.when((i < units) & (b >= 0) & (b < lanes) & (lax.rem(i, GROUPS) == side_groups))
            def _():
                take_guest(b)

            loop(start, limit(i), work)
            pl.when(i == units - GROUPS)(settle)

        loop(0, units + 1, unit)
        settle_late()
        for k in range(2):
            store_lower(k)

    def each_carried(visit):
        def one_slot(s):
            @pl.when(carried(s))
            def _():
                visit(s)

        loop(0, slots, one_slot)

    @pl.when(z == 0)
    def _():
        loop(jnp.where(first_chip, per_block * PARTS, 0), chunks * PARTS, upper_sent)

    @pl.when(z == 1)
    def _():
        for jj in range(chunks):
            hand_back(jj).wait_send()
        for b in range(lanes):
            export(b).wait_send()

        @pl.when(z < last)
        def _():
            each_carried(lambda s: loop(0, PARTS, lambda r: down_staged(s, r).wait_send()))

    @pl.when(both)
    def _():
        for b in range(lanes):
            loop(0, PARTS, lambda r: give_back(b, r).wait_send())
            loop(0, GROUPS, lambda g: forward(slots + b, g).wait_send())
        each_carried(lambda s: loop(0, GROUPS, lambda g: forward(s, g).wait_send()))

        @pl.when(z < last)
        def _():
            each_carried(lambda s: loop(0, PARTS, lambda r: down_relay(s, r).wait_send()))

    @pl.when(first_chip)
    def _():
        for k in range(2):
            @pl.when(z < last)
            def _():
                pivot_send(k, z + 1, p_send.at[k, z]).wait_send()

            @pl.when(z - 1 > k)
            def _():
                pivot_send(k, z - 1, p_up.at[k]).wait_send()

            finish_pivot(k)

    @pl.when(first_chip & (z == 1))
    def _():
        pivot_own(1).wait()

    for k in range(2):
        @pl.when(z > k)
        def _():
            lower_pass(k).wait_send()

            @pl.when(first_chip)
            def _():
                for target in direct:
                    for q in range(2):
                        lower_send(k, target, q).wait_send()
                if k == 0:
                    swap_columns().wait_send()

            for q in range(2):
                @pl.when(member == 1 + q)
                def _():
                    lower_send(k, chip + 2 - q, q).wait_send()


def sparse(arm, n_row, n_col, plan, matrix, pivot_inverse, row_live, col_live):
    rows, columns = matrix.shape
    panels, rows_own, width = pivot_inverse.shape
    chunk = min(CHUNK, width)
    chunks = columns // chunk
    items = CORES * chunks
    slots = items + 2 + arm
    lanes = min(4, slots - items - 1)
    part = chunk // CORES
    n_chip = n_col // CORES
    f32, bf16, dma = jnp.float32, jnp.bfloat16, pltpu.SemaphoreType.DMA
    return pl.pallas_call(
        functools.partial(sparse_kernel, slots, n_row, n_col, chunk),
        out_shape=pltpu.VMEM((rows, columns), f32),
        in_specs=[pl.BlockSpec(memory_space=pltpu.HBM)] * 5,
        out_specs=pl.BlockSpec(memory_space=pltpu.VMEM),
        scratch_shapes=[
            pltpu.SMEM(row_live.shape, jnp.int32),
            pltpu.SMEM(col_live.shape, jnp.int32),
            pltpu.SMEM(plan.shape, jnp.int32),
            pltpu.SMEM((5, slots + lanes), jnp.int32),
            pltpu.VMEM((slots + lanes, width, chunk), f32),
            pltpu.VMEM((slots + lanes, width, chunk), f32),
            pltpu.VMEM((slots, width, part), f32),
            pltpu.VMEM((items, width, part), f32),
            pltpu.VMEM((lanes, width, part), f32),
            pltpu.VMEM((lanes, width, part), f32),
            pltpu.VMEM((chunks, width, part), f32),
            pltpu.VMEM((panels, width, width), f32),
            pltpu.VMEM((CORES, width // CORES, width), f32),
            pltpu.VMEM((panels, width, width), f32),
            pltpu.VMEM((panels, width, width), bf16),
            pltpu.VMEM((panels, width, width), bf16),
            pltpu.VMEM((width, chunk), bf16),
            pltpu.VMEM((width, chunk), bf16),
            dma((chunks,)), dma((3,)),
            dma((slots + lanes, PARTS)), dma((slots + lanes, PARTS)),
            dma((slots + lanes, GROUPS)), dma((slots + lanes, GROUPS)),
            dma((lanes, PARTS)), dma((lanes,)), dma((lanes,)),
            dma((chunks,)), dma((chunks,)), dma((chunks,)), dma((chunks,)),
            dma((panels, n_row)), dma((panels, n_row)), dma((panels, n_row)), dma((panels, n_row)),
            dma((panels,)), dma, dma, dma,
            dma((panels, n_chip, 2)), dma((panels, 2)), dma((panels,)), dma((panels,)), dma((panels,)),
            pltpu.SemaphoreType.REGULAR,
        ],
        compiler_params=pltpu.CompilerParams(
            collective_id=1 + arm, has_side_effects=True, vmem_limit_bytes=GRANT - 4 * rows * columns
        ),
    )(row_live, col_live, plan, matrix, pivot_inverse)


def per_device(n_row, n_col, matrix, pivot_inverse, row_live, col_live):
    width = pivot_inverse.shape[2]
    chunk = min(CHUNK, width)
    chunks, per_block = matrix.shape[1] // chunk, width // chunk
    smem = pl.BlockSpec(memory_space=pltpu.SMEM)
    plan = pl.pallas_call(
        functools.partial(plan_kernel, n_row, n_col, chunks, per_block),
        out_shape=jax.ShapeDtypeStruct((1 + 2 * n_col,), jnp.int32),
        in_specs=[smem, smem],
        out_specs=smem,
    )(row_live, col_live)
    arms = [functools.partial(sparse, arm, n_row, n_col) for arm in range(ARMS)]
    arms.append(functools.partial(dense, n_row, n_col))
    return lax.switch(plan[0], arms, plan, matrix, pivot_inverse, row_live, col_live)


def solution(mesh):
    n_row, n_col = mesh.shape["prow"], mesh.shape["pcol"]
    return jax.shard_map(
        functools.partial(per_device, n_row, n_col),
        mesh=mesh,
        in_specs=(P("prow", "pcol"), P(None, "prow", None), P(), P()),
        out_specs=P("prow", "pcol"),
        check_vma=False,
    )
```

```python
import functools

import jax
import jax.numpy as jnp
from jax import lax
from jax.experimental import pallas as pl
from jax.experimental.pallas import tpu as pltpu
from jax.sharding import PartitionSpec as P

MESH = pl.DeviceIdType.MESH
CORES = 2
CHUNK = 256
PIECES = 16
TAIL = 4
GUESTS = 28
GRANT = 67_043_328
PARTS = 8
GROUPS = 4
ARMS = 5
PACE = 3


def split(x):
    high = x.astype(jnp.bfloat16)
    return high, (x - high.astype(jnp.float32)).astype(jnp.bfloat16)


def product(left_high, left_low, right_high, right_low):
    dot = functools.partial(jnp.dot, preferred_element_type=jnp.float32)
    return dot(left_high, right_high) + (dot(left_high, right_low) + dot(left_low, right_high))


def kernel(
    n_row, n_col, chunk, row_hbm, col_hbm, mat, piv, acc,
    row_smem, col_smem, u, p, a, guest, low, low_high, low_rest, u_high, u_rest,
    acc_sem, mask_sem, u_send, u_recv, p_send, p_recv, p_pass, p_passed, p_own,
    a_own, a_send, a_recv, t_send, t_recv, l_send, l_recv, l_pass, l_passed,
    p_up, g_in, g_recv, g_down, g_out,
):
    z, pcol = lax.axis_index("prow"), lax.axis_index("pcol")
    core, chip = lax.rem(pcol, CORES), lax.div(pcol, CORES)
    n_chip = n_col // CORES
    partner = (z, pcol + 1 - 2 * core)
    width, half = piv.shape[2], piv.shape[2] // CORES
    rows_own = piv.shape[1]
    rows_half = rows_own // CORES
    chunks = acc.shape[1] // chunk
    per_block = width // chunk
    pieces = u_send.shape[1] // chunks
    piece = width // pieces
    steps = chunks * pieces
    last = n_row - 1
    guests = guest.shape[1]
    guest_start = (chunks - 2) * pieces
    first_chip, active, both = chip == 0, z > 0, z > 1
    guest_end = guest_start + jnp.where(chip > 0, guests, 0)

    def remote(src, dst, send, recv, to):
        return pltpu.make_async_remote_copy(
            src_ref=src, dst_ref=dst, send_sem=send, recv_sem=recv, device_id=to, device_id_type=MESH
        )

    masks = [
        pltpu.make_async_copy(row_hbm, row_smem, mask_sem.at[0]),
        pltpu.make_async_copy(col_hbm, col_smem, mask_sem.at[1]),
    ]

    def columns_of(j):
        start = j * chunk
        return pl.ds(start if isinstance(j, int) else pl.multiple_of(start, 128), chunk)

    def load(j):
        return pltpu.make_async_copy(mat.at[:, columns_of(j)], acc.at[:, columns_of(j)], acc_sem.at[j])

    def pivot_own(k):
        return pltpu.make_async_copy(piv.at[k], p.at[k, pl.ds(z * rows_own, rows_own)], p_own.at[k])

    def pivot_rows(k, source):
        return p.at[k, pl.ds(pl.multiple_of(source * rows_own + core * rows_half, 8), rows_half)]

    def pivot_send(k, target, send):
        return remote(
            piv.at[k, pl.ds(pl.multiple_of(core * rows_half, 8), rows_half)],
            pivot_rows(k, z), send, p_recv.at[k, z], (target, pcol),
        )

    def pivot_relay(k, source, target):
        return remote(pivot_rows(k, source), pivot_rows(k, source), p_send.at[k, source], p_recv.at[k, source], (target, pcol))

    def pivot_landed(k, source):
        return remote(pivot_rows(k, source), pivot_rows(k, source), p_send.at[k, source], p_recv.at[k, source], (z, pcol))

    def pivot_pass(k, source):
        return remote(pivot_rows(k, source), pivot_rows(k, source), p_pass.at[k, source], p_passed.at[k, source], partner)

    def piece_of(ref, j, r):
        return ref.at[j, pl.ds(pl.multiple_of(r * piece, 8), piece)]

    def relay_copy(k, s):
        place = piece_of(u.at[k], s // pieces, s % pieces)
        return remote(place, place, u_send.at[k, s], u_recv.at[k, s], (z + 1, pcol))

    def origin_copy(k, s):
        j, r = s // pieces, s % pieces
        rows = pl.ds(pl.multiple_of(r * piece, 8), piece)
        return remote(acc.at[rows, columns_of(j)], piece_of(u.at[k], j, r), u_send.at[k, s], u_recv.at[k, s], (z + 1, pcol))

    def start_of(k):
        return jnp.where(pcol <= k, per_block * pieces, 0)

    def relay(k, begin, end):
        def body(s, carry):
            copy = relay_copy(k, s)
            copy.wait_recv()

            @pl.when(z < last)
            def _():
                copy.start()

            return carry

        lax.fori_loop(jnp.maximum(begin, start_of(k)), end, body, 0)

    def originate(k, begin, end):
        def body(s, carry):
            origin_copy(k, s).start()
            return carry

        lax.fori_loop(jnp.maximum(begin, start_of(k)), end, body, 0)

    def finish_sends(k, copy):
        def body(s, carry):
            copy(k, s).wait_send()
            return carry

        if k:
            lax.fori_loop(start_of(k), guest_start, body, 0)
            lax.fori_loop(guest_end, steps, body, 0)
        else:
            lax.fori_loop(start_of(k), steps, body, 0)

    def guest_in(i):
        rows = pl.ds(i * piece, piece)
        source = acc.at[rows, columns_of(guest_start // pieces)]
        return remote(source, guest.at[chip, i], g_in.at[i], g_recv.at[chip, i], (z, core))

    def guest_down(q, i):
        return remote(guest.at[q, i], guest.at[q, i], g_down.at[q, i], g_recv.at[q, i], (z + 1, pcol))

    def guest_out(q, i):
        target = piece_of(u.at[1], guest_start // pieces, i)
        return remote(guest.at[q, i], target, g_out.at[q, i], u_recv.at[1, guest_start + i], (z, q * CORES + core))

    def pass_guests():
        def body(t, carry):
            q, i = 1 + t // guests, t % guests
            guest_down(q, i).wait_recv()

            @pl.when(z < last)
            def _():
                guest_down(q, i).start()

            @pl.when(both)
            def _():
                guest_out(q, i).start()

            return carry

        lax.fori_loop(0, (n_chip - 1) * guests, body, 0)

    def finish_guests():
        def body(t, carry):
            q, i = 1 + t // guests, t % guests

            @pl.when(z < last)
            def _():
                guest_down(q, i).wait_send()

            @pl.when(both)
            def _():
                guest_out(q, i).wait_send()

            return carry

        lax.fori_loop(0, (n_chip - 1) * guests, body, 0)

    def own_rows():
        return pl.ds(pl.multiple_of(core * half, 8), half)

    def lower_send(k, target):
        rows = low.at[k, own_rows()]
        return remote(rows, rows, l_send.at[k, target], l_recv.at[k], (z, target * CORES + core))

    def lower_pass(k):
        rows = low.at[k, own_rows()]
        return remote(rows, rows, l_pass.at[k], l_passed.at[k], partner)

    def row_mask(k):
        return row_smem[k, z].astype(jnp.float32)

    def for_sources(k, visit):
        for distance in range(1, n_row):
            @pl.when(z - distance >= 0)
            def _():
                visit(z - distance, z + 1, z < last, z > k)

            @pl.when((z + distance <= last) & (z > k))
            def _():
                visit(z + distance, z - 1, z - 1 > k, z > k)

    def relay_pivot(k):
        def visit(source, target, onward, used):
            pivot_landed(k, source).wait_recv()

            @pl.when(onward)
            def _():
                pivot_relay(k, source, target).start()

            @pl.when(used)
            def _():
                pivot_pass(k, source).start()

        for_sources(k, visit)

    def gather_pivot(k):
        pivot_own(k).wait()
        for source in range(n_row):
            @pl.when(z != source)
            def _():
                pivot_pass(k, source).wait_recv()

    def finish_pivot(k):
        def visit(source, target, onward, used):
            @pl.when(onward)
            def _():
                pivot_relay(k, source, target).wait_send()

            @pl.when(used)
            def _():
                pivot_pass(k, source).wait_send()

        for_sources(k, visit)

    def apply_pivot(k, left):
        left_high, left_low = split(left)
        for q in range(per_block):
            columns = pl.ds(q * chunk, chunk)
            right = split(p[k, :, columns])
            low[k, own_rows(), columns] = row_mask(k) * product(left_high, left_low, *right)
        for target in range(n_chip - 1, 0, -1):
            lower_send(k, target).start()
        lower_pass(k).start()

    def take_lower(k):
        @pl.when(chip > 0)
        def _():
            lower_send(k, 0).wait_recv()
            lower_pass(k).start()

        lower_pass(k).wait_recv()
        low_high[k], low_rest[k] = split(low[k])

    def update(k, j, part=0, parts=1):
        live = col_smem[k, pcol + (j // per_block) * n_col].astype(jnp.float32)

        def run():
            depth = pl.ds(part * (width // parts), width // parts)
            u_high[depth], u_rest[depth] = split(u[k, j, depth])
            for t in range(CORES):
                rows = pl.ds(t * half, half)
                left = low_high[k, rows, depth], low_rest[k, rows, depth]
                acc[rows, columns_of(j)] -= live * product(*left, u_high[depth], u_rest[depth])

        if j < per_block:
            pl.when(pcol > k)(run)
        else:
            run()

    def store_lower(k):
        @pl.when(pcol == k)
        def _():
            acc[:, pl.ds(0, width)] = low[k]

    barrier = pltpu.get_barrier_semaphore()
    relays_guests = (z == 1) & (z < last)

    def greet(condition, device):
        @pl.when(condition)
        def _():
            pl.semaphore_signal(barrier, inc=1, device_id=device, device_id_type=MESH)

    greet(active, (z - 1, pcol))
    greet(active, partner)
    greet(active & (z < last) & first_chip, (z + 1, pcol))
    greet(active & (chip > 0), (z, core))
    for other in range(1, n_chip):
        greet(relays_guests & first_chip, (z, other * CORES + core))

    for j in range(chunks):
        load(j).start()
    for copy in masks:
        copy.start()

    @pl.when(first_chip & active)
    def _():
        for k in range(2):
            pivot_own(k).start()
        pltpu.make_async_copy(mat.at[own_rows(), pl.ds(0, width)], a.at[core], a_own).start()

    targets = (
        jnp.where(z < last, 1, 0)
        + jnp.where(active, 1, 0)
        + jnp.where(both & first_chip, 1, 0)
        + jnp.where(active & first_chip, n_chip - 1, 0)
        + jnp.where(relays_guests & (chip > 0), 1, 0)
    )
    pl.semaphore_wait(barrier, targets)

    def swap_columns():
        source = mat.at[pl.ds(pl.multiple_of((1 - core) * half, 8), half), pl.ds(0, width)]
        return remote(source, a.at[core], a_send, a_recv, partner)

    def swapped_columns():
        return remote(a.at[1 - core], a.at[1 - core], a_send, a_recv, partner)

    @pl.when(first_chip)
    def _():
        for k in range(2):
            @pl.when(z < last)
            def _():
                pivot_send(k, z + 1, p_send.at[k, z]).start()

            @pl.when(z - 1 > k)
            def _():
                pivot_send(k, z - 1, p_up.at[k]).start()

        @pl.when(active)
        def _():
            swap_columns().start()

    for j in range(chunks):
        load(j).wait()

        @pl.when(z == 0)
        def _():
            originate(0, j * pieces, (j + 1) * pieces)

    for copy in masks:
        copy.wait()

    @pl.when(active)
    def _():
        @pl.when(first_chip)
        def _():
            relay_pivot(0)
            gather_pivot(0)
            pltpu.make_async_copy(mat.at[own_rows(), pl.ds(0, width)], a.at[core], a_own).wait()
            swapped_columns().wait_recv()
            apply_pivot(0, a[0])
            relay_pivot(1)

        ahead = jnp.where(pcol == 0, steps - TAIL, per_block * pieces)
        relay(0, 0, ahead)

        @pl.when(first_chip & both)
        def _():
            top = u.at[0, pl.ds(0, per_block)]
            copy = remote(top, top, t_send, t_recv, partner)

            @pl.when(core == 1)
            def _():
                copy.start()

            gather_pivot(1)

            @pl.when(core == 0)
            def _():
                copy.wait_recv()

            live = col_smem[0, 1].astype(jnp.float32)
            left = split(low[0, own_rows()])
            for q in range(per_block):
                columns = pl.ds(q * chunk, chunk)
                a[1, :, columns] -= live * product(*left, *split(u[0, q]))
            apply_pivot(1, a[1])

            @pl.when(core == 1)
            def _():
                copy.wait_send()

        relay(0, ahead, steps - TAIL)
        take_lower(0)
        for j in range(chunks - 1):
            update(0, j)
            relay(0, steps - TAIL + j, steps - TAIL + j + 1)
        relay(0, steps - TAIL + chunks - 1, steps)

        @pl.when(z == 1)
        def _():
            @pl.when(z < last)
            def _():
                @pl.when(chip > 0)
                def _():
                    for i in range(guests):
                        guest_in(i).start()

                originate(1, 0, guest_start)
                originate(1, guest_end, steps - pieces)

                @pl.when(first_chip)
                def _():
                    pass_guests()

            update(0, chunks - 1)

            @pl.when(z < last)
            def _():
                originate(1, steps - pieces, steps)

            store_lower(0)

        @pl.when(both)
        def _():
            relay(1, 0, pieces)
            update(0, chunks - 1)
            relay(1, pieces, guest_start)
            take_lower(1)
            update(1, 0)
            relay(1, guest_end, guest_end + 4)
            update(1, 1)
            store_lower(0)
            store_lower(1)
            relay(1, guest_end + 4, steps - pieces)

            @pl.when(first_chip)
            def _():
                pass_guests()

            @pl.when(chip > 0)
            def _():
                for i in range(guests):
                    relay_copy(1, guest_start + i).wait_recv()

            for j in range(2, chunks - 1):
                update(1, j)
            for part in range(4):
                begin = steps - pieces + part * (pieces // 4)
                relay(1, begin, begin + pieces // 4)
                update(1, chunks - 1, part, 4)

    @pl.when(z == 0)
    def _():
        finish_sends(0, origin_copy)

    @pl.when(active & first_chip)
    def _():
        @pl.when((z < last) | both)
        def _():
            finish_guests()

    @pl.when((z == 1) & (z < last) & (chip > 0))
    def _():
        for i in range(guests):
            guest_in(i).wait_send()

    @pl.when(active & (z < last))
    def _():
        finish_sends(0, relay_copy)

        @pl.when(z == 1)
        def _():
            finish_sends(1, origin_copy)

        @pl.when(both)
        def _():
            finish_sends(1, relay_copy)

    @pl.when(first_chip)
    def _():
        for k in range(2):
            @pl.when(z < last)
            def _():
                pivot_send(k, z + 1, p_send.at[k, z]).wait_send()

            @pl.when(z - 1 > k)
            def _():
                pivot_send(k, z - 1, p_up.at[k]).wait_send()

            finish_pivot(k)

    @pl.when(first_chip & (z == 1))
    def _():
        pivot_own(1).wait()

    for k in range(2):
        @pl.when(z > k)
        def _():
            lower_pass(k).wait_send()

            @pl.when(first_chip)
            def _():
                for target in range(n_chip - 1, 0, -1):
                    lower_send(k, target).wait_send()
                if k == 0:
                    swap_columns().wait_send()


def dense(n_row, n_col, plan, matrix, pivot_inverse, row_live, col_live):
    rows, columns = matrix.shape
    panels, rows_own, width = pivot_inverse.shape
    chunk = min(CHUNK, width)
    chunks = columns // chunk
    steps = chunks * PIECES
    n_chip = n_col // CORES
    guests = max(1, GUESTS // n_chip)
    f32, bf16, dma = jnp.float32, jnp.bfloat16, pltpu.SemaphoreType.DMA
    return pl.pallas_call(
        functools.partial(kernel, n_row, n_col, chunk),
        out_shape=pltpu.VMEM((rows, columns), f32),
        in_specs=[pl.BlockSpec(memory_space=pltpu.HBM)] * 4,
        out_specs=pl.BlockSpec(memory_space=pltpu.VMEM),
        scratch_shapes=[
            pltpu.SMEM(row_live.shape, jnp.int32),
            pltpu.SMEM(col_live.shape, jnp.int32),
            pltpu.VMEM((panels, chunks, width, chunk), f32),
            pltpu.VMEM((panels, width, width), f32),
            pltpu.VMEM((CORES, width // CORES, width), f32),
            pltpu.VMEM((n_chip, guests, width // PIECES, chunk), f32),
            pltpu.VMEM((panels, width, width), f32),
            pltpu.VMEM((panels, width, width), bf16),
            pltpu.VMEM((panels, width, width), bf16),
            pltpu.VMEM((width, chunk), bf16),
            pltpu.VMEM((width, chunk), bf16),
            dma((chunks,)), dma((2,)),
            dma((panels, steps)), dma((panels, steps)),
            dma((panels, n_row)), dma((panels, n_row)), dma((panels, n_row)), dma((panels, n_row)),
            dma((panels,)), dma, dma, dma, dma, dma,
            dma((panels, n_col // CORES)), dma((panels,)), dma((panels,)), dma((panels,)),
            dma((panels,)), dma((guests,)), dma((n_chip, guests)), dma((n_chip, guests)), dma((n_chip, guests)),
        ],
        compiler_params=pltpu.CompilerParams(
            collective_id=0, has_side_effects=True, vmem_limit_bytes=GRANT - 4 * rows * columns
        ),
    )(row_live, col_live, matrix, pivot_inverse)


def neighbour(chip, bit):
    return chip + bit * (1 - 2 * lax.rem(lax.div(chip, bit), 2))


def live_items(row, col, chip, n_row, n_col, chunks, per_block):
    used = row[1, 2]
    for g in range(3, n_row):
        used = jnp.maximum(used, row[1, g])
    zero, one = [], []
    for j in range(CORES * chunks):
        h = chip * CORES + j % CORES + j // CORES // per_block * n_col
        zero.append(jnp.where(h > 0, col[0, h], 0))
        one.append(jnp.where(h > 1, col[1, h] * used, 0))
    return zero, one


def total(values):
    return functools.reduce(lambda x, y: x + y, values, jnp.int32(0))


def plan_kernel(n_row, n_col, chunks, per_block, row, col, out):
    n_chip, items = n_col // CORES, CORES * chunks
    half, final = items // 2, items - CORES
    lane = lax.broadcasted_iota(jnp.int32, (8, 128), 0) * 128 + lax.broadcasted_iota(jnp.int32, (8, 128), 1)
    lane = lane.astype(jnp.float32)
    digits = []
    rest = lane
    for _ in range(4):
        next_rest = jnp.floor((rest + 0.5) / 5)
        digits.append(rest - 5 * next_rest - 2)
        rest = next_rest
    size = [jnp.abs(f) for f in digits]
    moves = sum(size)
    x_size, y_size = jnp.maximum(size[0], size[1]), jnp.maximum(size[2], size[3])
    needed = items + 1 + jnp.maximum(jnp.maximum(2 * x_size - 1, 2 * y_size), 0)
    longest = jnp.int32(0)
    for quad in range(n_chip // 4):
        worst = needed
        for i in range(4):
            zero, one = live_items(row, col, quad * 4 + i, n_row, n_col, chunks, per_block)
            both = [x * y for x, y in zip(zero, one)]
            early = total(both[:half]).astype(jnp.float32)
            holes = total([(1 - zero[j]) * (1 - one[j]) for j in range(final, items)]).astype(jnp.float32)
            count = total(both).astype(jnp.float32)
            x = digits[i // 2] * (1 - 2 * (i % 2))
            y = digits[2 + i % 2] * (1 - 2 * (i // 2))
            sent = jnp.maximum(x, 0) + jnp.maximum(y, 0)
            load = items + count - x - y - jnp.minimum(holes, early - sent)
            worst = jnp.maximum(worst, jnp.where(sent > early, 99.0, load))
        key = jnp.where(rest > 0.5, 1e7, (worst * 16 + moves) * 1024 + lane)
        best = jnp.min(key).astype(jnp.int32)
        longest = jnp.maximum(longest, lax.div(best, 16384))
        code = lax.rem(best, 1024)
        for e in range(4):
            out[1 + quad * 4 + e] = lax.rem(code, 5) - 2
            code = lax.div(code, 5)
    out[0] = jnp.minimum(jnp.maximum(longest - items - 2, 0), ARMS)


def sparse_kernel(
    slots, n_row, n_col, chunk, row_hbm, col_hbm, plan_hbm, mat, piv, acc,
    row_smem, col_smem, plan, tab, pos, prod, tx, own, out_guest, in_guest, back,
    p, a, low, low_high, low_rest, u_high, u_rest,
    acc_sem, mask_sem, d_send, d_recv, f_send, f_recv, r_send, e_send, e_recv, s_send, s_recv, b_send, b_recv,
    p_send, p_recv, p_pass, p_passed, p_own, a_own, a_send, a_recv, l_send, l_recv, l_pass, l_passed, p_up, turn_sem,
):
    z, pcol = lax.axis_index("prow"), lax.axis_index("pcol")
    core, chip = lax.rem(pcol, CORES), lax.div(pcol, CORES)
    n_chip = n_col // CORES
    partner = (z, pcol + 1 - 2 * core)
    width, half = piv.shape[2], piv.shape[2] // CORES
    rows_own = piv.shape[1]
    rows_half = rows_own // CORES
    chunks = acc.shape[1] // chunk
    per_block = width // chunk
    items = CORES * chunks
    part = chunk // CORES
    piece = width // PARTS
    last = n_row - 1
    lanes = out_guest.shape[0]
    first_chip, active, both = chip == 0, z > 0, z > 1
    mine = pl.ds(pl.multiple_of(core * part, 128), part)

    def remote(src, dst, send, recv, to):
        return pltpu.make_async_remote_copy(
            src_ref=src, dst_ref=dst, send_sem=send, recv_sem=recv, device_id=to, device_id_type=MESH
        )

    masks = [
        pltpu.make_async_copy(row_hbm, row_smem, mask_sem.at[0]),
        pltpu.make_async_copy(col_hbm, col_smem, mask_sem.at[1]),
        pltpu.make_async_copy(plan_hbm, plan, mask_sem.at[2]),
    ]

    def columns_of(j):
        start = j * chunk
        return pl.ds(start if isinstance(j, int) else pl.multiple_of(start, 128), chunk)

    def part_of(j, side):
        return pl.ds(pl.multiple_of(j * chunk + side * part, 128), part)

    def rows_of(r):
        return pl.ds(pl.multiple_of(r * piece, 8), piece)

    def load(j):
        return pltpu.make_async_copy(mat.at[:, columns_of(j)], acc.at[:, columns_of(j)], acc_sem.at[j])

    def pivot_own(k):
        return pltpu.make_async_copy(piv.at[k], p.at[k, pl.ds(z * rows_own, rows_own)], p_own.at[k])

    def pivot_rows(k, source):
        return p.at[k, pl.ds(pl.multiple_of(source * rows_own + core * rows_half, 8), rows_half)]

    def pivot_send(k, target, send):
        return remote(
            piv.at[k, pl.ds(pl.multiple_of(core * rows_half, 8), rows_half)],
            pivot_rows(k, z), send, p_recv.at[k, z], (target, pcol),
        )

    def pivot_relay(k, source, target):
        return remote(pivot_rows(k, source), pivot_rows(k, source), p_send.at[k, source], p_recv.at[k, source], (target, pcol))

    def pivot_landed(k, source):
        return remote(pivot_rows(k, source), pivot_rows(k, source), p_send.at[k, source], p_recv.at[k, source], (z, pcol))

    def pivot_pass(k, source):
        return remote(pivot_rows(k, source), pivot_rows(k, source), p_pass.at[k, source], p_passed.at[k, source], partner)

    def own_rows():
        return pl.ds(pl.multiple_of(core * half, 8), half)

    def lower_send(k, target, q):
        rows = low.at[k, pl.ds(pl.multiple_of(core * half + q * (half // 2), 8), half // 2)]
        return remote(rows, rows, l_send.at[k, target, q], l_recv.at[k, q], (z, target * CORES + core))

    member = lax.rem(chip, 4)
    direct = [t for t in range(1, n_chip) if t % 4 < 3]

    def relay_lower(k):
        for q in range(2):
            @pl.when(member == 1 + q)
            def _():
                lower_send(k, chip, q).wait_recv()
                lower_send(k, chip + 2 - q, q).start()

    def lower_pass(k):
        rows = low.at[k, own_rows()]
        return remote(rows, rows, l_pass.at[k], l_passed.at[k], partner)

    def row_mask(k):
        return row_smem[k, z].astype(jnp.float32)

    def for_sources(k, visit):
        for distance in range(1, n_row):
            @pl.when(z - distance >= 0)
            def _():
                visit(z - distance, z + 1, z < last, z > k)

            @pl.when((z + distance <= last) & (z > k))
            def _():
                visit(z + distance, z - 1, z - 1 > k, z > k)

    def relay_pivot(k):
        def visit(source, target, onward, used):
            pivot_landed(k, source).wait_recv()

            @pl.when(onward)
            def _():
                pivot_relay(k, source, target).start()

            @pl.when(used)
            def _():
                pivot_pass(k, source).start()

        for_sources(k, visit)

    def gather_pivot(k):
        pivot_own(k).wait()
        for source in range(n_row):
            @pl.when(z != source)
            def _():
                pivot_pass(k, source).wait_recv()

    def finish_pivot(k):
        def visit(source, target, onward, used):
            @pl.when(onward)
            def _():
                pivot_relay(k, source, target).wait_send()

            @pl.when(used)
            def _():
                pivot_pass(k, source).wait_send()

        for_sources(k, visit)

    def apply_pivot(k, left):
        left_high, left_low = split(left)

        def visit(q):
            right = split(p[k, :, columns_of(q)])
            low[k, own_rows(), columns_of(q)] = row_mask(k) * product(left_high, left_low, *right)

        loop(0, per_block, visit)
        for turn in range(2):
            for target in direct:
                lower_send(k, target, 1 - turn if target % 4 == 2 else turn).start()
        lower_pass(k).start()

    def take_lower(k):
        @pl.when(chip > 0)
        def _():
            for q in range(2):
                @pl.when(member != 1 + q)
                def _():
                    lower_send(k, 0, q).wait_recv()

            lower_pass(k).start()

        lower_pass(k).wait_recv()

        def visit(r):
            low_high[k, rows_of(r)], low_rest[k, rows_of(r)] = split(low[k, rows_of(r)])

        loop(0, PARTS, visit)

    def store_lower(k):
        @pl.when(pcol == k)
        def _():
            acc[:, pl.ds(0, width)] = low[k]

    def swap_columns():
        source = mat.at[pl.ds(pl.multiple_of((1 - core) * half, 8), half), pl.ds(0, width)]
        return remote(source, a.at[core], a_send, a_recv, partner)

    def swapped_columns():
        return remote(a.at[1 - core], a.at[1 - core], a_send, a_recv, partner)

    def carried(j):
        return jnp.logical_not(first_chip & (lax.rem(j, 2) == 0) & (j < CORES * per_block))

    def upper_send(jj, side, r):
        j = CORES * jj + core
        return remote(
            mat.at[rows_of(r), part_of(jj, side)], pos.at[j, rows_of(r), pl.ds(pl.multiple_of(side * part, 128), part)],
            d_send.at[CORES * jj + side], d_recv.at[j, r], (z + 1, chip * CORES + side),
        )

    def down(source, s, r):
        return remote(source, pos.at[s, rows_of(r), mine], d_send.at[s], d_recv.at[s, r], (z + 1, pcol))

    def down_staged(s, r):
        return down(tx.at[s, rows_of(r)], s, r)

    def down_relay(s, r):
        return down(pos.at[s, rows_of(r), mine], s, r)

    def landed(s, r):
        place = pos.at[s, rows_of(r), mine]
        return remote(place, place, d_send.at[s], d_recv.at[s, r], (z, pcol))

    def give_back(b, r):
        place = pos.at[items + b, rows_of(r), mine]
        target = pos.at[slots + b, rows_of(r), mine]
        to = (z, neighbour(chip, 1 + b % 2) * CORES + core)
        return remote(place, target, r_send.at[b], d_recv.at[slots + b, r], to)

    def slot_sent(s, sem):
        place = pos.at[s, :, mine]
        remote(place, place, sem, d_recv.at[s, 0], partner).wait_send()

    def group_rows(g):
        return pl.ds(pl.multiple_of(g * (width // GROUPS), 8), width // GROUPS)

    def forward(s, g):
        place = pos.at[s, group_rows(g), mine]
        return remote(place, place, f_send.at[s], f_recv.at[s, g], partner)

    def export(b):
        to = (z, neighbour(chip, 1 + b % 2) * CORES + core)
        return remote(out_guest.at[b], in_guest.at[b], e_send.at[b], e_recv.at[b], to)

    def swap_own(jj):
        source = acc.at[:, part_of(jj, 1 - core)]
        return remote(source, own.at[CORES * jj + core], s_send.at[jj], s_recv.at[jj], partner)

    def swapped_own(jj):
        place = own.at[CORES * jj + 1 - core]
        return remote(place, place, s_send.at[jj], s_recv.at[jj], partner)

    def hand_back(jj):
        return remote(own.at[CORES * jj + 1 - core], back.at[jj], b_send.at[jj], b_recv.at[jj], partner)

    def loop(begin, end, visit):
        def body(i, carry):
            visit(i)
            return carry

        lax.fori_loop(begin, end, body, 0)

    barrier = pltpu.get_barrier_semaphore()

    def greet(condition, device):
        @pl.when(condition)
        def _():
            pl.semaphore_signal(barrier, inc=1, device_id=device, device_id_type=MESH)

    greet(active, (z - 1, pcol))
    greet(z == 1, (z - 1, pcol + 1 - 2 * core))
    greet(active | (pcol == 0), partner)
    greet(active & (z < last) & first_chip, (z + 1, pcol))
    greet(active & (chip > 0), (z, core))
    for bit in (1, 2):
        near = neighbour(chip, bit)
        greet(active & (near > 0), (z, near * CORES + core))

    for j in range(chunks):
        load(j).start()
    for copy in masks:
        copy.start()

    @pl.when(first_chip & active)
    def _():
        for k in range(2):
            pivot_own(k).start()
        pltpu.make_async_copy(mat.at[own_rows(), pl.ds(0, width)], a.at[core], a_own).start()

    targets = (
        jnp.where(z < last, 1, 0)
        + jnp.where(z == 0, 1, 0)
        + jnp.where((z == 0) & (pcol == 1), 1, 0)
        + jnp.where(active, 1, 0)
        + jnp.where(both & first_chip, 1, 0)
        + jnp.where(active & first_chip, n_chip - 1, 0)
        + jnp.where(active & (chip > 0), 2, 0)
    )
    pl.semaphore_wait(barrier, targets)

    @pl.when(first_chip)
    def _():
        for k in range(2):
            @pl.when(z < last)
            def _():
                pivot_send(k, z + 1, p_send.at[k, z]).start()

            @pl.when(z - 1 > k)
            def _():
                pivot_send(k, z - 1, p_up.at[k]).start()

        @pl.when(active)
        def _():
            swap_columns().start()

    upper_start = jnp.where(pcol == 0, per_block * PARTS, 0)

    def upper_sent(jj):
        for side in range(CORES):
            slot_sent(0, d_send.at[CORES * jj + side])

    @pl.when(z == 0)
    def _():
        def visit(s):
            for side in range(CORES):
                upper_send(lax.div(s, PARTS), side, lax.rem(s, PARTS)).start()

        @pl.when(first_chip & (core == 0))
        def _():
            pl.semaphore_wait(turn_sem, 1)

        loop(upper_start, chunks * PARTS, visit)

        @pl.when(first_chip & (core == 1))
        def _():
            loop(0, per_block, upper_sent)
            pl.semaphore_signal(turn_sem, inc=1, device_id=partner, device_id_type=MESH)

    for j in range(chunks):
        load(j).wait()

    @pl.when(z == 1)
    def _():
        for jj in range(chunks):
            swap_own(jj).start()

    for copy in masks:
        copy.wait()

    zero, one = live_items(row_smem, col_smem, chip, n_row, n_col, chunks, per_block)
    pair = [x * y for x, y in zip(zero, one)]
    rank, hole, order = [], [], []
    for j in range(items):
        rank.append(total(pair[:j]))
        hole.append((1 - zero[j]) * (1 - one[j]) if j >= items - CORES else jnp.int32(0))
        order.append(total(hole[:j]))
    quad = lax.div(chip, 4)
    flow_x = plan[1 + quad * 4 + lax.div(member, 2)] * (1 - 2 * lax.rem(member, 2))
    flow_y = plan[3 + quad * 4 + lax.rem(member, 2)] * (1 - 2 * lax.div(member, 2))
    x_out, y_out = jnp.maximum(flow_x, 0), jnp.maximum(flow_y, 0)
    x_in, y_in = jnp.maximum(-flow_x, 0), jnp.maximum(-flow_y, 0)
    sent = x_out + y_out
    filled = jnp.minimum(total(hole), total(pair[: items // 2]) - sent)

    def item_of(r):
        return total([jnp.where(rank[j] == r, j * pair[j], 0) for j in range(items)])

    for j in range(items):
        held = (1 - zero[j]) * one[j]
        moved = item_of(sent + order[j]) if j >= items - CORES else j
        tab[0, j] = zero[j]
        tab[1, j] = jnp.where(held > 0, j, jnp.where(order[j] < filled, moved, j))
    imported = [jnp.where((y_in if b % 2 else x_in) > b // 2, 1, 0) for b in range(lanes)]
    imported += [jnp.int32(0)] * (slots - items - lanes)
    place_of = [s - total(imported[:s]) for s in range(slots - items)]
    for s in range(slots - items):
        tab[0, items + s] = 0
        tab[1, items + s] = item_of(sent + filled + place_of[s])
    for b in range(lanes):
        tab[0, slots + b] = 0

    for jj in range(chunks):
        found = []
        for d in range(CORES):
            j = CORES * jj + d
            spare = rank[j] - sent
            fill = total([jnp.where(order[q] == spare, q * hole[q], 0) for q in range(items - CORES, items)])
            index = spare - filled
            late = total([jnp.where(place_of[s] == index, (items + s) * (1 - imported[s]), 0) for s in range(slots - items)])
            away = slots + jnp.where(rank[j] < x_out, 2 * rank[j], 2 * (rank[j] - x_out) + 1)
            place = jnp.where(spare < 0, away, jnp.where(spare < filled, fill, late))
            found.append(jnp.where(pair[j] > 0, place, j))
        tab[2, jj] = jnp.where(core == 0, found[0], found[1])
        tab[3, jj] = jnp.where(core == 0, one[CORES * jj], one[CORES * jj + 1])
        tab[4, jj] = jnp.where(core == 0, zero[CORES * jj], zero[CORES * jj + 1])

    def stage_pair(jj, begin, finish):
        def visit(r):
            for d in range(CORES):
                s = CORES * jj + d

                @pl.when(carried(s))
                def _():
                    landed(s, r).wait_recv()
                    upper = tab[0, s].astype(jnp.float32)
                    rows = rows_of(r)
                    tx[s, rows] = upper * pos[s, rows, mine] + (1 - upper) * own[tab[1, s], rows]

                    @pl.when(z < last)
                    def _():
                        down_staged(s, r).start()

        loop(begin, finish, visit)

    def stage_late(s):
        def visit(r):
            rows = rows_of(r)
            tx[s, rows] = own[tab[1, s], rows]

            @pl.when(z < last)
            def _():
                down_staged(s, r).start()

        loop(0, PARTS, visit)

    def stage_guest(b):
        export(b).wait_recv()
        keep = imported[b].astype(jnp.float32)

        def visit(r):
            rows = rows_of(r)
            tx[items + b, rows] = keep * in_guest[b, rows] + (1 - keep) * own[tab[1, items + b], rows]

            @pl.when(z < last)
            def _():
                down_staged(items + b, r).start()

        loop(0, PARTS, visit)

    def update_pair(jj):
        for d in range(CORES):
            side = pl.ds(d * part, part)
            u_high[:, side], u_rest[:, side] = split(pos[CORES * jj + d, :, mine])

        def visit(t):
            rows = pl.ds(pl.multiple_of(t * half, half), half)
            value = product(low_high[0, rows], low_rest[0, rows], u_high[...], u_rest[...])
            for d in range(CORES):
                s = CORES * jj + d

                @pl.when(carried(s))
                def _():
                    own[s, rows] -= tab[0, s].astype(jnp.float32) * value[:, d * part:(d + 1) * part]

        loop(0, CORES, visit)
        hand_back(jj).start()

    def keep_own(jj):
        acc[:, part_of(jj, core)] = own[CORES * jj + core]

    end = slots - 1
    late_slots = [end] + [slots + b for b in range(lanes) if items + 1 + b == end]
    side_groups = GROUPS // 2
    depth = width // 2

    def multiply(s, side):
        k = 1 - tab[0, s]
        deep = pl.ds(pl.multiple_of(side * depth, depth), depth)
        u_high[deep], u_rest[deep] = split(pos[s, deep])
        for t in range(CORES):
            rows = pl.ds(t * half, half)
            value = product(low_high[k, rows, deep], low_rest[k, rows, deep], u_high[deep], u_rest[deep])
            prod[s, rows] = value + jnp.where(side > 0, prod[s, rows], 0.0)

    def work(w):
        o, side = lax.div(w, 2), lax.rem(w, 2)
        later = o - items - 1
        turn = jnp.where(lax.rem(later, 2) == 0, slots, items + 1) + lax.div(later, 2)
        s = jnp.where(later < 0, o, jnp.where(later < 2 * lanes, turn, o - lanes))

        @pl.when(carried(s))
        def _():
            @pl.when(jnp.logical_not(first_chip & (s < CORES * per_block)))
            def _():
                for i in range(side_groups):
                    forward(s, side * side_groups + i).wait_recv()

            multiply(s, side)

    def arrive(s, g, relays=True):
        for i in range(PARTS // GROUPS):
            r = g * (PARTS // GROUPS) + i
            landed(s, r).wait_recv()
            if relays:
                @pl.when(z < last)
                def _():
                    down_relay(s, r).start()

                for b in range(lanes):
                    @pl.when(s == items + b)
                    def _():
                        give_back(b, r).start()
        forward(s, g).start()

    def arrive_pair(jj, begin=0, finish=GROUPS):
        def visit(g):
            for d in range(CORES):
                s = CORES * jj + d

                @pl.when(carried(s))
                def _():
                    arrive(s, g)

        loop(begin, finish, visit)

    def take_guest(b):
        loop(0, GROUPS, lambda g: arrive(slots + b, g, False))

    units = GROUPS * (slots - items)
    first = 2 if slots > items + 2 else 0

    def limit(i):
        s, g = items + lax.div(i, GROUPS), lax.rem(i, GROUPS)
        b = s - items - 1
        guest = jnp.where((b >= 0) & (b < lanes), 2, 0)
        late = jnp.where(g >= side_groups, guest, 0) + jnp.where(g == GROUPS - 1, 1, 0)
        whole = 2 * (s + jnp.minimum(jnp.maximum(b, 0), lanes)) + late
        pace = jnp.maximum(PACE * (i + 1 - first), 0)
        paced = jnp.where(i < units - GROUPS, jnp.minimum(whole, pace), whole)
        return jnp.where(i < units, paced, 2 * (slots + lanes))

    def settle(begin):
        def visit(t):
            jj, rows = lax.div(t, PARTS), rows_of(lax.rem(t, PARTS))
            place = tab[2, jj]
            ready = tab[3, jj] > 0
            for s in late_slots:
                ready = ready & (place != s)
            upper = jnp.where(tab[4, jj] > 0, prod[CORES * jj + core, rows], 0.0)
            acc[rows, columns_of(jj)] -= upper + jnp.where(ready, prod[place, rows], 0.0)

        loop(begin * chunks * PARTS // 2, (begin + 1) * chunks * PARTS // 2, visit)

    def settle_late():
        def visit(t):
            rows = rows_of(t)
            values = [prod[s, rows] for s in late_slots]
            for jj in range(chunks):
                flags = [jnp.where(tab[2, jj] == s, tab[3, jj], 0).astype(jnp.float32) for s in late_slots]
                acc[rows, columns_of(jj)] -= functools.reduce(jnp.add, [f * v for f, v in zip(flags, values)])

        loop(0, PARTS, visit)

    def make_lower():
        gather_pivot(0)
        pltpu.make_async_copy(mat.at[own_rows(), pl.ds(0, width)], a.at[core], a_own).wait()
        swapped_columns().wait_recv()
        apply_pivot(0, a[0])

    @pl.when(active & first_chip)
    def _():
        relay_pivot(0)
        relay_pivot(1)

    @pl.when(z == 1)
    def _():
        for jj in range(chunks):
            own[CORES * jj + core] = acc[:, part_of(jj, core)]
            swapped_own(jj).wait_recv()

        steps = chunks * GROUPS
        updates = [2 * GROUPS + 2, 2 * GROUPS + 3, 3 * GROUPS + 1, steps]

        def visit(t):
            @pl.when(t < steps)
            def _():
                begin = lax.rem(t, GROUPS) * (PARTS // GROUPS)
                stage_pair(lax.div(t, GROUPS), begin, begin + PARTS // GROUPS)

            @pl.when((t == 1) & first_chip)
            def _():
                make_lower()

            @pl.when(t == 2 * GROUPS - 2)
            def _():
                relay_lower(0)

            @pl.when(t == 2 * GROUPS + 1)
            def _():
                take_lower(0)

            @pl.when(t == steps)
            def _():
                stage_guest(0)

            @pl.when(functools.reduce(jnp.logical_or, [t == u for u in updates]))
            def _():
                update_pair(sum(jnp.where(t > u, 1, 0) for u in updates))

            @pl.when(t == updates[1])
            def _():
                for b in range(lanes):
                    out_guest[b] = own[item_of((x_out if b % 2 else 0) + b // 2)]
                    export(b).start()

        loop(0, steps + 1, visit)
        for b in range(1, lanes):
            stage_guest(b)
        loop(items + lanes, slots, stage_late)
        for jj in range(chunks):
            hand_back(jj).wait_recv()
            swap_own(jj).wait_send()
            acc[:, part_of(jj, 1 - core)] = back[jj]
            keep_own(jj)
        store_lower(0)

    @pl.when(both)
    def _():
        pl.when(first_chip)(make_lower)
        loop(0, per_block - 1, arrive_pair)
        arrive_pair(per_block - 1, 0, side_groups)
        relay_lower(0)
        arrive_pair(per_block - 1, side_groups, GROUPS)

        @pl.when(first_chip)
        def _():
            gather_pivot(1)
            live = tab[0, 1].astype(jnp.float32)
            left = split(low[0, own_rows()])

            def visit(q):
                for g in range(GROUPS):
                    forward(CORES * q + 1, g).wait_recv()
                a[1, :, columns_of(q)] -= live * product(*left, *split(pos[CORES * q + 1]))

            loop(0, per_block, visit)
            apply_pivot(1, a[1])

        loop(per_block, chunks - 1, arrive_pair)
        arrive_pair(chunks - 1, 0, 1)
        relay_lower(1)
        arrive_pair(chunks - 1, 1, GROUPS)
        if first == 0:
            loop(0, 2, take_lower)

        def unit(i):
            @pl.when(i < units)
            def _():
                arrive(items + lax.div(i, GROUPS), lax.rem(i, GROUPS))

            start = jnp.where(i > 0, limit(i - 1), 0)

            if first:
                @pl.when(i == first)
                def _():
                    loop(0, 2, take_lower)

            b = lax.div(i, GROUPS) - 1

            @pl.when((i < units) & (b >= 0) & (b < lanes) & (lax.rem(i, GROUPS) == side_groups))
            def _():
                take_guest(b)

            loop(start, limit(i), work)
            for half_of in range(2):
                pl.when(i == units - GROUPS + half_of)(functools.partial(settle, half_of))

        loop(0, units + 1, unit)
        settle_late()
        for k in range(2):
            store_lower(k)

    def each_carried(visit):
        def one_slot(s):
            @pl.when(carried(s))
            def _():
                visit(s)

        loop(0, slots, one_slot)

    @pl.when(z == 0)
    def _():
        loop(jnp.where(first_chip, per_block, 0), chunks, upper_sent)

    @pl.when(z == 1)
    def _():
        for jj in range(chunks):
            hand_back(jj).wait_send()
        for b in range(lanes):
            export(b).wait_send()

        @pl.when(z < last)
        def _():
            each_carried(lambda s: slot_sent(s, d_send.at[s]))

    @pl.when(both)
    def _():
        for b in range(lanes):
            slot_sent(slots + b, r_send.at[b])
            slot_sent(slots + b, f_send.at[slots + b])
        each_carried(lambda s: slot_sent(s, f_send.at[s]))

        @pl.when(z < last)
        def _():
            each_carried(lambda s: slot_sent(s, d_send.at[s]))

    @pl.when(first_chip)
    def _():
        for k in range(2):
            @pl.when(z < last)
            def _():
                pivot_send(k, z + 1, p_send.at[k, z]).wait_send()

            @pl.when(z - 1 > k)
            def _():
                pivot_send(k, z - 1, p_up.at[k]).wait_send()

            finish_pivot(k)

    @pl.when(first_chip & (z == 1))
    def _():
        pivot_own(1).wait()

    for k in range(2):
        @pl.when(z > k)
        def _():
            lower_pass(k).wait_send()

            @pl.when(first_chip)
            def _():
                for target in direct:
                    for q in range(2):
                        lower_send(k, target, q).wait_send()
                if k == 0:
                    swap_columns().wait_send()

            for q in range(2):
                @pl.when(member == 1 + q)
                def _():
                    lower_send(k, chip + 2 - q, q).wait_send()


def sparse(arm, n_row, n_col, plan, matrix, pivot_inverse, row_live, col_live):
    rows, columns = matrix.shape
    panels, rows_own, width = pivot_inverse.shape
    chunk = min(CHUNK, width)
    chunks = columns // chunk
    items = CORES * chunks
    slots = items + 2 + arm
    lanes = min(4, slots - items - 1)
    part = chunk // CORES
    n_chip = n_col // CORES
    f32, bf16, dma = jnp.float32, jnp.bfloat16, pltpu.SemaphoreType.DMA
    return pl.pallas_call(
        functools.partial(sparse_kernel, slots, n_row, n_col, chunk),
        out_shape=pltpu.VMEM((rows, columns), f32),
        in_specs=[pl.BlockSpec(memory_space=pltpu.HBM)] * 5,
        out_specs=pl.BlockSpec(memory_space=pltpu.VMEM),
        scratch_shapes=[
            pltpu.SMEM(row_live.shape, jnp.int32),
            pltpu.SMEM(col_live.shape, jnp.int32),
            pltpu.SMEM(plan.shape, jnp.int32),
            pltpu.SMEM((5, slots + lanes), jnp.int32),
            pltpu.VMEM((slots + lanes, width, chunk), f32),
            pltpu.VMEM((slots + lanes, width, chunk), f32),
            pltpu.VMEM((slots, width, part), f32),
            pltpu.VMEM((items, width, part), f32),
            pltpu.VMEM((lanes, width, part), f32),
            pltpu.VMEM((lanes, width, part), f32),
            pltpu.VMEM((chunks, width, part), f32),
            pltpu.VMEM((panels, width, width), f32),
            pltpu.VMEM((CORES, width // CORES, width), f32),
            pltpu.VMEM((panels, width, width), f32),
            pltpu.VMEM((panels, width, width), bf16),
            pltpu.VMEM((panels, width, width), bf16),
            pltpu.VMEM((width, chunk), bf16),
            pltpu.VMEM((width, chunk), bf16),
            dma((chunks,)), dma((3,)),
            dma((slots + lanes,)), dma((slots + lanes, PARTS)),
            dma((slots + lanes,)), dma((slots + lanes, GROUPS)),
            dma((lanes,)), dma((lanes,)), dma((lanes,)),
            dma((chunks,)), dma((chunks,)), dma((chunks,)), dma((chunks,)),
            dma((panels, n_row)), dma((panels, n_row)), dma((panels, n_row)), dma((panels, n_row)),
            dma((panels,)), dma, dma, dma,
            dma((panels, n_chip, 2)), dma((panels, 2)), dma((panels,)), dma((panels,)), dma((panels,)),
            pltpu.SemaphoreType.REGULAR,
        ],
        compiler_params=pltpu.CompilerParams(
            collective_id=1 + arm, has_side_effects=True, vmem_limit_bytes=GRANT - 4 * rows * columns
        ),
    )(row_live, col_live, plan, matrix, pivot_inverse)


def per_device(n_row, n_col, matrix, pivot_inverse, row_live, col_live):
    width = pivot_inverse.shape[2]
    chunk = min(CHUNK, width)
    chunks, per_block = matrix.shape[1] // chunk, width // chunk
    smem = pl.BlockSpec(memory_space=pltpu.SMEM)
    plan = pl.pallas_call(
        functools.partial(plan_kernel, n_row, n_col, chunks, per_block),
        out_shape=jax.ShapeDtypeStruct((1 + 2 * n_col,), jnp.int32),
        in_specs=[smem, smem],
        out_specs=smem,
    )(row_live, col_live)
    arms = [functools.partial(sparse, arm, n_row, n_col) for arm in range(ARMS)]
    arms.append(functools.partial(dense, n_row, n_col))
    return lax.switch(plan[0], arms, plan, matrix, pivot_inverse, row_live, col_live)


def solution(mesh):
    n_row, n_col = mesh.shape["prow"], mesh.shape["pcol"]
    return jax.shard_map(
        functools.partial(per_device, n_row, n_col),
        mesh=mesh,
        in_specs=(P("prow", "pcol"), P(None, "prow", None), P(), P()),
        out_specs=P("prow", "pcol"),
        check_vma=False,
    )
```

```python
import functools

import jax
import jax.numpy as jnp
from jax import lax
from jax.experimental import pallas as pl
from jax.experimental.pallas import tpu as pltpu
from jax.sharding import PartitionSpec as P

MESH = pl.DeviceIdType.MESH
CORES = 2
CHUNK = 256
PIECES = 16
TAIL = 4
GUESTS = 28
GRANT = 67_043_328
PARTS = 8
GROUPS = 4
ARMS = 5


def split(x):
    high = x.astype(jnp.bfloat16)
    return high, (x - high.astype(jnp.float32)).astype(jnp.bfloat16)


def product(left_high, left_low, right_high, right_low):
    dot = functools.partial(jnp.dot, preferred_element_type=jnp.float32)
    return dot(left_high, right_high) + (dot(left_high, right_low) + dot(left_low, right_high))


def kernel(
    n_row, n_col, chunk, row_hbm, col_hbm, mat, piv, acc,
    row_smem, col_smem, u, p, a, guest, low, low_high, low_rest, u_high, u_rest,
    acc_sem, mask_sem, u_send, u_recv, p_send, p_recv, p_pass, p_passed, p_own,
    a_own, a_send, a_recv, t_send, t_recv, l_send, l_recv, l_pass, l_passed,
    p_up, g_in, g_recv, g_down, g_out,
):
    z, pcol = lax.axis_index("prow"), lax.axis_index("pcol")
    core, chip = lax.rem(pcol, CORES), lax.div(pcol, CORES)
    n_chip = n_col // CORES
    partner = (z, pcol + 1 - 2 * core)
    width, half = piv.shape[2], piv.shape[2] // CORES
    rows_own = piv.shape[1]
    rows_half = rows_own // CORES
    chunks = acc.shape[1] // chunk
    per_block = width // chunk
    pieces = u_send.shape[1] // chunks
    piece = width // pieces
    steps = chunks * pieces
    last = n_row - 1
    guests = guest.shape[1]
    guest_start = (chunks - 2) * pieces
    first_chip, active, both = chip == 0, z > 0, z > 1
    guest_end = guest_start + jnp.where(chip > 0, guests, 0)

    def remote(src, dst, send, recv, to):
        return pltpu.make_async_remote_copy(
            src_ref=src, dst_ref=dst, send_sem=send, recv_sem=recv, device_id=to, device_id_type=MESH
        )

    masks = [
        pltpu.make_async_copy(row_hbm, row_smem, mask_sem.at[0]),
        pltpu.make_async_copy(col_hbm, col_smem, mask_sem.at[1]),
    ]

    def columns_of(j):
        start = j * chunk
        return pl.ds(start if isinstance(j, int) else pl.multiple_of(start, 128), chunk)

    def load(j):
        return pltpu.make_async_copy(mat.at[:, columns_of(j)], acc.at[:, columns_of(j)], acc_sem.at[j])

    def pivot_own(k):
        return pltpu.make_async_copy(piv.at[k], p.at[k, pl.ds(z * rows_own, rows_own)], p_own.at[k])

    def pivot_rows(k, source):
        return p.at[k, pl.ds(pl.multiple_of(source * rows_own + core * rows_half, 8), rows_half)]

    def pivot_send(k, target, send):
        return remote(
            piv.at[k, pl.ds(pl.multiple_of(core * rows_half, 8), rows_half)],
            pivot_rows(k, z), send, p_recv.at[k, z], (target, pcol),
        )

    def pivot_relay(k, source, target):
        return remote(pivot_rows(k, source), pivot_rows(k, source), p_send.at[k, source], p_recv.at[k, source], (target, pcol))

    def pivot_landed(k, source):
        return remote(pivot_rows(k, source), pivot_rows(k, source), p_send.at[k, source], p_recv.at[k, source], (z, pcol))

    def pivot_pass(k, source):
        return remote(pivot_rows(k, source), pivot_rows(k, source), p_pass.at[k, source], p_passed.at[k, source], partner)

    def piece_of(ref, j, r):
        return ref.at[j, pl.ds(pl.multiple_of(r * piece, 8), piece)]

    def relay_copy(k, s):
        place = piece_of(u.at[k], s // pieces, s % pieces)
        return remote(place, place, u_send.at[k, s], u_recv.at[k, s], (z + 1, pcol))

    def origin_copy(k, s):
        j, r = s // pieces, s % pieces
        rows = pl.ds(pl.multiple_of(r * piece, 8), piece)
        return remote(acc.at[rows, columns_of(j)], piece_of(u.at[k], j, r), u_send.at[k, s], u_recv.at[k, s], (z + 1, pcol))

    def start_of(k):
        return jnp.where(pcol <= k, per_block * pieces, 0)

    def relay(k, begin, end):
        def body(s, carry):
            copy = relay_copy(k, s)
            copy.wait_recv()

            @pl.when(z < last)
            def _():
                copy.start()

            return carry

        lax.fori_loop(jnp.maximum(begin, start_of(k)), end, body, 0)

    def originate(k, begin, end):
        def body(s, carry):
            origin_copy(k, s).start()
            return carry

        lax.fori_loop(jnp.maximum(begin, start_of(k)), end, body, 0)

    def finish_sends(k, copy):
        def body(s, carry):
            copy(k, s).wait_send()
            return carry

        if k:
            lax.fori_loop(start_of(k), guest_start, body, 0)
            lax.fori_loop(guest_end, steps, body, 0)
        else:
            lax.fori_loop(start_of(k), steps, body, 0)

    def guest_in(i):
        rows = pl.ds(i * piece, piece)
        source = acc.at[rows, columns_of(guest_start // pieces)]
        return remote(source, guest.at[chip, i], g_in.at[i], g_recv.at[chip, i], (z, core))

    def guest_down(q, i):
        return remote(guest.at[q, i], guest.at[q, i], g_down.at[q, i], g_recv.at[q, i], (z + 1, pcol))

    def guest_out(q, i):
        target = piece_of(u.at[1], guest_start // pieces, i)
        return remote(guest.at[q, i], target, g_out.at[q, i], u_recv.at[1, guest_start + i], (z, q * CORES + core))

    def pass_guests():
        def body(t, carry):
            q, i = 1 + t // guests, t % guests
            guest_down(q, i).wait_recv()

            @pl.when(z < last)
            def _():
                guest_down(q, i).start()

            @pl.when(both)
            def _():
                guest_out(q, i).start()

            return carry

        lax.fori_loop(0, (n_chip - 1) * guests, body, 0)

    def finish_guests():
        def body(t, carry):
            q, i = 1 + t // guests, t % guests

            @pl.when(z < last)
            def _():
                guest_down(q, i).wait_send()

            @pl.when(both)
            def _():
                guest_out(q, i).wait_send()

            return carry

        lax.fori_loop(0, (n_chip - 1) * guests, body, 0)

    def own_rows():
        return pl.ds(pl.multiple_of(core * half, 8), half)

    def lower_send(k, target):
        rows = low.at[k, own_rows()]
        return remote(rows, rows, l_send.at[k, target], l_recv.at[k], (z, target * CORES + core))

    def lower_pass(k):
        rows = low.at[k, own_rows()]
        return remote(rows, rows, l_pass.at[k], l_passed.at[k], partner)

    def row_mask(k):
        return row_smem[k, z].astype(jnp.float32)

    def for_sources(k, visit):
        for distance in range(1, n_row):
            @pl.when(z - distance >= 0)
            def _():
                visit(z - distance, z + 1, z < last, z > k)

            @pl.when((z + distance <= last) & (z > k))
            def _():
                visit(z + distance, z - 1, z - 1 > k, z > k)

    def relay_pivot(k):
        def visit(source, target, onward, used):
            pivot_landed(k, source).wait_recv()

            @pl.when(onward)
            def _():
                pivot_relay(k, source, target).start()

            @pl.when(used)
            def _():
                pivot_pass(k, source).start()

        for_sources(k, visit)

    def gather_pivot(k):
        pivot_own(k).wait()
        for source in range(n_row):
            @pl.when(z != source)
            def _():
                pivot_pass(k, source).wait_recv()

    def finish_pivot(k):
        def visit(source, target, onward, used):
            @pl.when(onward)
            def _():
                pivot_relay(k, source, target).wait_send()

            @pl.when(used)
            def _():
                pivot_pass(k, source).wait_send()

        for_sources(k, visit)

    def apply_pivot(k, left):
        left_high, left_low = split(left)
        for q in range(per_block):
            columns = pl.ds(q * chunk, chunk)
            right = split(p[k, :, columns])
            low[k, own_rows(), columns] = row_mask(k) * product(left_high, left_low, *right)
        for target in range(n_chip - 1, 0, -1):
            lower_send(k, target).start()
        lower_pass(k).start()

    def take_lower(k):
        @pl.when(chip > 0)
        def _():
            lower_send(k, 0).wait_recv()
            lower_pass(k).start()

        lower_pass(k).wait_recv()
        low_high[k], low_rest[k] = split(low[k])

    def update(k, j, part=0, parts=1):
        live = col_smem[k, pcol + (j // per_block) * n_col].astype(jnp.float32)

        def run():
            depth = pl.ds(part * (width // parts), width // parts)
            u_high[depth], u_rest[depth] = split(u[k, j, depth])
            for t in range(CORES):
                rows = pl.ds(t * half, half)
                left = low_high[k, rows, depth], low_rest[k, rows, depth]
                acc[rows, columns_of(j)] -= live * product(*left, u_high[depth], u_rest[depth])

        if j < per_block:
            pl.when(pcol > k)(run)
        else:
            run()

    def store_lower(k):
        @pl.when(pcol == k)
        def _():
            acc[:, pl.ds(0, width)] = low[k]

    barrier = pltpu.get_barrier_semaphore()
    relays_guests = (z == 1) & (z < last)

    def greet(condition, device):
        @pl.when(condition)
        def _():
            pl.semaphore_signal(barrier, inc=1, device_id=device, device_id_type=MESH)

    greet(active, (z - 1, pcol))
    greet(active, partner)
    greet(active & (z < last) & first_chip, (z + 1, pcol))
    greet(active & (chip > 0), (z, core))
    for other in range(1, n_chip):
        greet(relays_guests & first_chip, (z, other * CORES + core))

    for j in range(chunks):
        load(j).start()
    for copy in masks:
        copy.start()

    @pl.when(first_chip & active)
    def _():
        for k in range(2):
            pivot_own(k).start()
        pltpu.make_async_copy(mat.at[own_rows(), pl.ds(0, width)], a.at[core], a_own).start()

    targets = (
        jnp.where(z < last, 1, 0)
        + jnp.where(active, 1, 0)
        + jnp.where(both & first_chip, 1, 0)
        + jnp.where(active & first_chip, n_chip - 1, 0)
        + jnp.where(relays_guests & (chip > 0), 1, 0)
    )
    pl.semaphore_wait(barrier, targets)

    def swap_columns():
        source = mat.at[pl.ds(pl.multiple_of((1 - core) * half, 8), half), pl.ds(0, width)]
        return remote(source, a.at[core], a_send, a_recv, partner)

    def swapped_columns():
        return remote(a.at[1 - core], a.at[1 - core], a_send, a_recv, partner)

    @pl.when(first_chip)
    def _():
        for k in range(2):
            @pl.when(z < last)
            def _():
                pivot_send(k, z + 1, p_send.at[k, z]).start()

            @pl.when(z - 1 > k)
            def _():
                pivot_send(k, z - 1, p_up.at[k]).start()

        @pl.when(active)
        def _():
            swap_columns().start()

    for j in range(chunks):
        load(j).wait()

        @pl.when(z == 0)
        def _():
            originate(0, j * pieces, (j + 1) * pieces)

    for copy in masks:
        copy.wait()

    @pl.when(active)
    def _():
        @pl.when(first_chip)
        def _():
            relay_pivot(0)
            gather_pivot(0)
            pltpu.make_async_copy(mat.at[own_rows(), pl.ds(0, width)], a.at[core], a_own).wait()
            swapped_columns().wait_recv()
            apply_pivot(0, a[0])
            relay_pivot(1)

        ahead = jnp.where(pcol == 0, steps - TAIL, per_block * pieces)
        relay(0, 0, ahead)

        @pl.when(first_chip & both)
        def _():
            top = u.at[0, pl.ds(0, per_block)]
            copy = remote(top, top, t_send, t_recv, partner)

            @pl.when(core == 1)
            def _():
                copy.start()

            gather_pivot(1)

            @pl.when(core == 0)
            def _():
                copy.wait_recv()

            live = col_smem[0, 1].astype(jnp.float32)
            left = split(low[0, own_rows()])
            for q in range(per_block):
                columns = pl.ds(q * chunk, chunk)
                a[1, :, columns] -= live * product(*left, *split(u[0, q]))
            apply_pivot(1, a[1])

            @pl.when(core == 1)
            def _():
                copy.wait_send()

        relay(0, ahead, steps - TAIL)
        take_lower(0)
        for j in range(chunks - 1):
            update(0, j)
            relay(0, steps - TAIL + j, steps - TAIL + j + 1)
        relay(0, steps - TAIL + chunks - 1, steps)

        @pl.when(z == 1)
        def _():
            @pl.when(z < last)
            def _():
                @pl.when(chip > 0)
                def _():
                    for i in range(guests):
                        guest_in(i).start()

                originate(1, 0, guest_start)
                originate(1, guest_end, steps - pieces)

                @pl.when(first_chip)
                def _():
                    pass_guests()

            update(0, chunks - 1)

            @pl.when(z < last)
            def _():
                originate(1, steps - pieces, steps)

            store_lower(0)

        @pl.when(both)
        def _():
            relay(1, 0, pieces)
            update(0, chunks - 1)
            relay(1, pieces, guest_start)
            take_lower(1)
            update(1, 0)
            relay(1, guest_end, guest_end + 4)
            update(1, 1)
            store_lower(0)
            store_lower(1)
            relay(1, guest_end + 4, steps - pieces)

            @pl.when(first_chip)
            def _():
                pass_guests()

            @pl.when(chip > 0)
            def _():
                for i in range(guests):
                    relay_copy(1, guest_start + i).wait_recv()

            for j in range(2, chunks - 1):
                update(1, j)
            for part in range(4):
                begin = steps - pieces + part * (pieces // 4)
                relay(1, begin, begin + pieces // 4)
                update(1, chunks - 1, part, 4)

    @pl.when(z == 0)
    def _():
        finish_sends(0, origin_copy)

    @pl.when(active & first_chip)
    def _():
        @pl.when((z < last) | both)
        def _():
            finish_guests()

    @pl.when((z == 1) & (z < last) & (chip > 0))
    def _():
        for i in range(guests):
            guest_in(i).wait_send()

    @pl.when(active & (z < last))
    def _():
        finish_sends(0, relay_copy)

        @pl.when(z == 1)
        def _():
            finish_sends(1, origin_copy)

        @pl.when(both)
        def _():
            finish_sends(1, relay_copy)

    @pl.when(first_chip)
    def _():
        for k in range(2):
            @pl.when(z < last)
            def _():
                pivot_send(k, z + 1, p_send.at[k, z]).wait_send()

            @pl.when(z - 1 > k)
            def _():
                pivot_send(k, z - 1, p_up.at[k]).wait_send()

            finish_pivot(k)

    @pl.when(first_chip & (z == 1))
    def _():
        pivot_own(1).wait()

    for k in range(2):
        @pl.when(z > k)
        def _():
            lower_pass(k).wait_send()

            @pl.when(first_chip)
            def _():
                for target in range(n_chip - 1, 0, -1):
                    lower_send(k, target).wait_send()
                if k == 0:
                    swap_columns().wait_send()


def dense(n_row, n_col, plan, matrix, pivot_inverse, row_live, col_live):
    rows, columns = matrix.shape
    panels, rows_own, width = pivot_inverse.shape
    chunk = min(CHUNK, width)
    chunks = columns // chunk
    steps = chunks * PIECES
    n_chip = n_col // CORES
    guests = max(1, GUESTS // n_chip)
    f32, bf16, dma = jnp.float32, jnp.bfloat16, pltpu.SemaphoreType.DMA
    return pl.pallas_call(
        functools.partial(kernel, n_row, n_col, chunk),
        out_shape=pltpu.VMEM((rows, columns), f32),
        in_specs=[pl.BlockSpec(memory_space=pltpu.HBM)] * 4,
        out_specs=pl.BlockSpec(memory_space=pltpu.VMEM),
        scratch_shapes=[
            pltpu.SMEM(row_live.shape, jnp.int32),
            pltpu.SMEM(col_live.shape, jnp.int32),
            pltpu.VMEM((panels, chunks, width, chunk), f32),
            pltpu.VMEM((panels, width, width), f32),
            pltpu.VMEM((CORES, width // CORES, width), f32),
            pltpu.VMEM((n_chip, guests, width // PIECES, chunk), f32),
            pltpu.VMEM((panels, width, width), f32),
            pltpu.VMEM((panels, width, width), bf16),
            pltpu.VMEM((panels, width, width), bf16),
            pltpu.VMEM((width, chunk), bf16),
            pltpu.VMEM((width, chunk), bf16),
            dma((chunks,)), dma((2,)),
            dma((panels, steps)), dma((panels, steps)),
            dma((panels, n_row)), dma((panels, n_row)), dma((panels, n_row)), dma((panels, n_row)),
            dma((panels,)), dma, dma, dma, dma, dma,
            dma((panels, n_col // CORES)), dma((panels,)), dma((panels,)), dma((panels,)),
            dma((panels,)), dma((guests,)), dma((n_chip, guests)), dma((n_chip, guests)), dma((n_chip, guests)),
        ],
        compiler_params=pltpu.CompilerParams(
            collective_id=0, has_side_effects=True, vmem_limit_bytes=GRANT - 4 * rows * columns
        ),
    )(row_live, col_live, matrix, pivot_inverse)


def neighbour(chip, bit):
    return chip + bit * (1 - 2 * lax.rem(lax.div(chip, bit), 2))


def live_items(row, col, chip, n_row, n_col, chunks, per_block):
    used = row[1, 2]
    for g in range(3, n_row):
        used = jnp.maximum(used, row[1, g])
    zero, one = [], []
    for j in range(CORES * chunks):
        h = chip * CORES + j % CORES + j // CORES // per_block * n_col
        zero.append(jnp.where(h > 0, col[0, h], 0))
        one.append(jnp.where(h > 1, col[1, h] * used, 0))
    return zero, one


def total(values):
    return functools.reduce(lambda x, y: x + y, values, jnp.int32(0))


def plan_kernel(n_row, n_col, chunks, per_block, row, col, out):
    n_chip, items = n_col // CORES, CORES * chunks
    half, final = items // 2, items - CORES
    lane = lax.broadcasted_iota(jnp.int32, (8, 128), 0) * 128 + lax.broadcasted_iota(jnp.int32, (8, 128), 1)
    lane = lane.astype(jnp.float32)
    digits = []
    rest = lane
    for _ in range(4):
        next_rest = jnp.floor((rest + 0.5) / 5)
        digits.append(rest - 5 * next_rest - 2)
        rest = next_rest
    size = [jnp.abs(f) for f in digits]
    moves = sum(size)
    x_size, y_size = jnp.maximum(size[0], size[1]), jnp.maximum(size[2], size[3])
    needed = items + 1 + jnp.maximum(jnp.maximum(2 * x_size - 1, 2 * y_size), 0)
    longest = jnp.int32(0)
    for quad in range(n_chip // 4):
        worst = needed
        for i in range(4):
            zero, one = live_items(row, col, quad * 4 + i, n_row, n_col, chunks, per_block)
            both = [x * y for x, y in zip(zero, one)]
            early = total(both[:half]).astype(jnp.float32)
            holes = total([(1 - zero[j]) * (1 - one[j]) for j in range(final, items)]).astype(jnp.float32)
            count = total(both).astype(jnp.float32)
            x = digits[i // 2] * (1 - 2 * (i % 2))
            y = digits[2 + i % 2] * (1 - 2 * (i // 2))
            sent = jnp.maximum(x, 0) + jnp.maximum(y, 0)
            load = items + count - x - y - jnp.minimum(holes, early - sent)
            worst = jnp.maximum(worst, jnp.where(sent > early, 99.0, load))
        key = jnp.where(rest > 0.5, 1e7, (worst * 16 + moves) * 1024 + lane)
        best = jnp.min(key).astype(jnp.int32)
        longest = jnp.maximum(longest, lax.div(best, 16384))
        code = lax.rem(best, 1024)
        for e in range(4):
            out[1 + quad * 4 + e] = lax.rem(code, 5) - 2
            code = lax.div(code, 5)
    out[0] = jnp.minimum(jnp.maximum(longest - items - 2, 0), ARMS)


def sparse_kernel(
    slots, n_row, n_col, chunk, row_hbm, col_hbm, plan_hbm, mat, piv, acc,
    row_smem, col_smem, plan, tab, pos, prod, tx, own, out_guest, in_guest, back,
    p, a, low, low_high, low_rest, u_high, u_rest,
    acc_sem, mask_sem, d_send, d_recv, f_send, f_recv, r_send, e_send, e_recv, s_send, s_recv, b_send, b_recv,
    p_send, p_recv, p_pass, p_passed, p_own, a_own, a_send, a_recv, l_send, l_recv, l_pass, l_passed, p_up, turn_sem,
):
    z, pcol = lax.axis_index("prow"), lax.axis_index("pcol")
    core, chip = lax.rem(pcol, CORES), lax.div(pcol, CORES)
    n_chip = n_col // CORES
    partner = (z, pcol + 1 - 2 * core)
    width, half = piv.shape[2], piv.shape[2] // CORES
    rows_own = piv.shape[1]
    rows_half = rows_own // CORES
    chunks = acc.shape[1] // chunk
    per_block = width // chunk
    items = CORES * chunks
    part = chunk // CORES
    piece = width // PARTS
    last = n_row - 1
    lanes = out_guest.shape[0]
    first_chip, active, both = chip == 0, z > 0, z > 1
    mine = pl.ds(pl.multiple_of(core * part, 128), part)

    def remote(src, dst, send, recv, to):
        return pltpu.make_async_remote_copy(
            src_ref=src, dst_ref=dst, send_sem=send, recv_sem=recv, device_id=to, device_id_type=MESH
        )

    masks = [
        pltpu.make_async_copy(row_hbm, row_smem, mask_sem.at[0]),
        pltpu.make_async_copy(col_hbm, col_smem, mask_sem.at[1]),
        pltpu.make_async_copy(plan_hbm, plan, mask_sem.at[2]),
    ]

    def columns_of(j):
        start = j * chunk
        return pl.ds(start if isinstance(j, int) else pl.multiple_of(start, 128), chunk)

    def part_of(j, side):
        return pl.ds(pl.multiple_of(j * chunk + side * part, 128), part)

    def rows_of(r):
        return pl.ds(pl.multiple_of(r * piece, 8), piece)

    def load(j):
        return pltpu.make_async_copy(mat.at[:, columns_of(j)], acc.at[:, columns_of(j)], acc_sem.at[j])

    def pivot_own(k):
        return pltpu.make_async_copy(piv.at[k], p.at[k, pl.ds(z * rows_own, rows_own)], p_own.at[k])

    def pivot_rows(k, source):
        return p.at[k, pl.ds(pl.multiple_of(source * rows_own + core * rows_half, 8), rows_half)]

    def pivot_send(k, target, send):
        return remote(
            piv.at[k, pl.ds(pl.multiple_of(core * rows_half, 8), rows_half)],
            pivot_rows(k, z), send, p_recv.at[k, z], (target, pcol),
        )

    def pivot_relay(k, source, target):
        return remote(pivot_rows(k, source), pivot_rows(k, source), p_send.at[k, source], p_recv.at[k, source], (target, pcol))

    def pivot_landed(k, source):
        return remote(pivot_rows(k, source), pivot_rows(k, source), p_send.at[k, source], p_recv.at[k, source], (z, pcol))

    def pivot_pass(k, source):
        return remote(pivot_rows(k, source), pivot_rows(k, source), p_pass.at[k, source], p_passed.at[k, source], partner)

    def own_rows():
        return pl.ds(pl.multiple_of(core * half, 8), half)

    def lower_send(k, target, q):
        rows = low.at[k, pl.ds(pl.multiple_of(core * half + q * (half // 2), 8), half // 2)]
        return remote(rows, rows, l_send.at[k, target, q], l_recv.at[k, q], (z, target * CORES + core))

    member = lax.rem(chip, 4)
    direct = [t for t in range(1, n_chip) if t % 4 < 3]

    def relay_lower(k):
        for q in range(2):
            @pl.when(member == 1 + q)
            def _():
                lower_send(k, chip, q).wait_recv()
                lower_send(k, chip + 2 - q, q).start()

    def lower_pass(k):
        rows = low.at[k, own_rows()]
        return remote(rows, rows, l_pass.at[k], l_passed.at[k], partner)

    def row_mask(k):
        return row_smem[k, z].astype(jnp.float32)

    def for_sources(k, visit):
        for distance in range(1, n_row):
            @pl.when(z - distance >= 0)
            def _():
                visit(z - distance, z + 1, z < last, z > k)

            @pl.when((z + distance <= last) & (z > k))
            def _():
                visit(z + distance, z - 1, z - 1 > k, z > k)

    def relay_pivot(k):
        def visit(source, target, onward, used):
            pivot_landed(k, source).wait_recv()

            @pl.when(onward)
            def _():
                pivot_relay(k, source, target).start()

            @pl.when(used)
            def _():
                pivot_pass(k, source).start()

        for_sources(k, visit)

    def gather_pivot(k):
        pivot_own(k).wait()
        for source in range(n_row):
            @pl.when(z != source)
            def _():
                pivot_pass(k, source).wait_recv()

    def finish_pivot(k):
        def visit(source, target, onward, used):
            @pl.when(onward)
            def _():
                pivot_relay(k, source, target).wait_send()

            @pl.when(used)
            def _():
                pivot_pass(k, source).wait_send()

        for_sources(k, visit)

    def apply_pivot(k, left):
        left_high, left_low = split(left)

        def visit(q):
            right = split(p[k, :, columns_of(q)])
            low[k, own_rows(), columns_of(q)] = row_mask(k) * product(left_high, left_low, *right)

        loop(0, per_block, visit)
        for turn in range(2):
            for target in direct:
                lower_send(k, target, 1 - turn if target % 4 == 2 else turn).start()
        lower_pass(k).start()

    def take_lower(k):
        @pl.when(chip > 0)
        def _():
            for q in range(2):
                @pl.when(member != 1 + q)
                def _():
                    lower_send(k, 0, q).wait_recv()

            lower_pass(k).start()

        lower_pass(k).wait_recv()

        def visit(r):
            low_high[k, rows_of(r)], low_rest[k, rows_of(r)] = split(low[k, rows_of(r)])

        loop(0, PARTS, visit)

    def store_lower(k):
        @pl.when(pcol == k)
        def _():
            acc[:, pl.ds(0, width)] = low[k]

    def swap_columns():
        source = mat.at[pl.ds(pl.multiple_of((1 - core) * half, 8), half), pl.ds(0, width)]
        return remote(source, a.at[core], a_send, a_recv, partner)

    def swapped_columns():
        return remote(a.at[1 - core], a.at[1 - core], a_send, a_recv, partner)

    def carried(j):
        return jnp.logical_not(first_chip & (lax.rem(j, 2) == 0) & (j < CORES * per_block))

    def upper_send(jj, side, r):
        j = CORES * jj + core
        return remote(
            mat.at[rows_of(r), part_of(jj, side)], pos.at[j, rows_of(r), pl.ds(pl.multiple_of(side * part, 128), part)],
            d_send.at[CORES * jj + side], d_recv.at[j, r], (z + 1, chip * CORES + side),
        )

    def down(source, s, r):
        return remote(source, pos.at[s, rows_of(r), mine], d_send.at[s], d_recv.at[s, r], (z + 1, pcol))

    def down_staged(s, r):
        return down(tx.at[s, rows_of(r)], s, r)

    def down_relay(s, r):
        return down(pos.at[s, rows_of(r), mine], s, r)

    def landed(s, r):
        place = pos.at[s, rows_of(r), mine]
        return remote(place, place, d_send.at[s], d_recv.at[s, r], (z, pcol))

    def give_back(b, r):
        place = pos.at[items + b, rows_of(r), mine]
        target = pos.at[slots + b, rows_of(r), mine]
        to = (z, neighbour(chip, 1 + b % 2) * CORES + core)
        return remote(place, target, r_send.at[b], d_recv.at[slots + b, r], to)

    def slot_sent(s, sem):
        place = pos.at[s, :, mine]
        remote(place, place, sem, d_recv.at[s, 0], partner).wait_send()

    def group_rows(g):
        return pl.ds(pl.multiple_of(g * (width // GROUPS), 8), width // GROUPS)

    def forward(s, g):
        place = pos.at[s, group_rows(g), mine]
        return remote(place, place, f_send.at[s], f_recv.at[s, g], partner)

    def export(b):
        to = (z, neighbour(chip, 1 + b % 2) * CORES + core)
        return remote(out_guest.at[b], in_guest.at[b], e_send.at[b], e_recv.at[b], to)

    def swap_own(jj):
        source = acc.at[:, part_of(jj, 1 - core)]
        return remote(source, own.at[CORES * jj + core], s_send.at[jj], s_recv.at[jj], partner)

    def swapped_own(jj):
        place = own.at[CORES * jj + 1 - core]
        return remote(place, place, s_send.at[jj], s_recv.at[jj], partner)

    def hand_back(jj):
        return remote(own.at[CORES * jj + 1 - core], back.at[jj], b_send.at[jj], b_recv.at[jj], partner)

    def loop(begin, end, visit):
        def body(i, carry):
            visit(i)
            return carry

        lax.fori_loop(begin, end, body, 0)

    barrier = pltpu.get_barrier_semaphore()

    def greet(condition, device):
        @pl.when(condition)
        def _():
            pl.semaphore_signal(barrier, inc=1, device_id=device, device_id_type=MESH)

    greet(active, (z - 1, pcol))
    greet(z == 1, (z - 1, pcol + 1 - 2 * core))
    greet(active | (pcol == 0), partner)
    greet(active & (z < last) & first_chip, (z + 1, pcol))
    greet(active & (chip > 0), (z, core))
    for bit in (1, 2):
        near = neighbour(chip, bit)
        greet(active & (near > 0), (z, near * CORES + core))

    for j in range(chunks):
        load(j).start()
    for copy in masks:
        copy.start()

    @pl.when(first_chip & active)
    def _():
        for k in range(2):
            pivot_own(k).start()
        pltpu.make_async_copy(mat.at[own_rows(), pl.ds(0, width)], a.at[core], a_own).start()

    targets = (
        jnp.where(z < last, 1, 0)
        + jnp.where(z == 0, 1, 0)
        + jnp.where((z == 0) & (pcol == 1), 1, 0)
        + jnp.where(active, 1, 0)
        + jnp.where(both & first_chip, 1, 0)
        + jnp.where(active & first_chip, n_chip - 1, 0)
        + jnp.where(active & (chip > 0), 2, 0)
    )
    pl.semaphore_wait(barrier, targets)

    @pl.when(first_chip)
    def _():
        for k in range(2):
            @pl.when(z < last)
            def _():
                pivot_send(k, z + 1, p_send.at[k, z]).start()

            @pl.when(z - 1 > k)
            def _():
                pivot_send(k, z - 1, p_up.at[k]).start()

        @pl.when(active)
        def _():
            swap_columns().start()

    upper_start = jnp.where(pcol == 0, per_block * PARTS, 0)

    def upper_sent(jj):
        for side in range(CORES):
            slot_sent(0, d_send.at[CORES * jj + side])

    @pl.when(z == 0)
    def _():
        def visit(s):
            for side in range(CORES):
                upper_send(lax.div(s, PARTS), side, lax.rem(s, PARTS)).start()

        @pl.when(first_chip & (core == 0))
        def _():
            pl.semaphore_wait(turn_sem, 1)

        loop(upper_start, chunks * PARTS, visit)

        @pl.when(first_chip & (core == 1))
        def _():
            loop(0, per_block, upper_sent)
            pl.semaphore_signal(turn_sem, inc=1, device_id=partner, device_id_type=MESH)

    for j in range(chunks):
        load(j).wait()

    @pl.when(z == 1)
    def _():
        for jj in range(chunks):
            swap_own(jj).start()

    for copy in masks:
        copy.wait()

    zero, one = live_items(row_smem, col_smem, chip, n_row, n_col, chunks, per_block)
    pair = [x * y for x, y in zip(zero, one)]
    rank, hole, order = [], [], []
    for j in range(items):
        rank.append(total(pair[:j]))
        hole.append((1 - zero[j]) * (1 - one[j]) if j >= items - CORES else jnp.int32(0))
        order.append(total(hole[:j]))
    quad = lax.div(chip, 4)
    flow_x = plan[1 + quad * 4 + lax.div(member, 2)] * (1 - 2 * lax.rem(member, 2))
    flow_y = plan[3 + quad * 4 + lax.rem(member, 2)] * (1 - 2 * lax.div(member, 2))
    x_out, y_out = jnp.maximum(flow_x, 0), jnp.maximum(flow_y, 0)
    x_in, y_in = jnp.maximum(-flow_x, 0), jnp.maximum(-flow_y, 0)
    sent = x_out + y_out
    filled = jnp.minimum(total(hole), total(pair[: items // 2]) - sent)

    def item_of(r):
        return total([jnp.where(rank[j] == r, j * pair[j], 0) for j in range(items)])

    for j in range(items):
        held = (1 - zero[j]) * one[j]
        moved = item_of(sent + order[j]) if j >= items - CORES else j
        tab[0, j] = zero[j]
        tab[1, j] = jnp.where(held > 0, j, jnp.where(order[j] < filled, moved, j))
    imported = [jnp.where((y_in if b % 2 else x_in) > b // 2, 1, 0) for b in range(lanes)]
    imported += [jnp.int32(0)] * (slots - items - lanes)
    place_of = [s - total(imported[:s]) for s in range(slots - items)]
    for s in range(slots - items):
        tab[0, items + s] = 0
        tab[1, items + s] = item_of(sent + filled + place_of[s])
    for b in range(lanes):
        tab[0, slots + b] = 0

    for jj in range(chunks):
        found = []
        for d in range(CORES):
            j = CORES * jj + d
            spare = rank[j] - sent
            fill = total([jnp.where(order[q] == spare, q * hole[q], 0) for q in range(items - CORES, items)])
            index = spare - filled
            late = total([jnp.where(place_of[s] == index, (items + s) * (1 - imported[s]), 0) for s in range(slots - items)])
            away = slots + jnp.where(rank[j] < x_out, 2 * rank[j], 2 * (rank[j] - x_out) + 1)
            place = jnp.where(spare < 0, away, jnp.where(spare < filled, fill, late))
            found.append(jnp.where(pair[j] > 0, place, j))
        tab[2, jj] = jnp.where(core == 0, found[0], found[1])
        tab[3, jj] = jnp.where(core == 0, one[CORES * jj], one[CORES * jj + 1])
        tab[4, jj] = jnp.where(core == 0, zero[CORES * jj], zero[CORES * jj + 1])

    def stage_pair(jj, begin, finish):
        def visit(r):
            for d in range(CORES):
                s = CORES * jj + d

                @pl.when(carried(s))
                def _():
                    landed(s, r).wait_recv()
                    upper = tab[0, s].astype(jnp.float32)
                    rows = rows_of(r)
                    tx[s, rows] = upper * pos[s, rows, mine] + (1 - upper) * own[tab[1, s], rows]

                    @pl.when(z < last)
                    def _():
                        down_staged(s, r).start()

        loop(begin, finish, visit)

    def stage_late(s):
        def visit(r):
            rows = rows_of(r)
            tx[s, rows] = own[tab[1, s], rows]

            @pl.when(z < last)
            def _():
                down_staged(s, r).start()

        loop(0, PARTS, visit)

    def stage_guest(b):
        export(b).wait_recv()
        keep = imported[b].astype(jnp.float32)

        def visit(r):
            rows = rows_of(r)
            tx[items + b, rows] = keep * in_guest[b, rows] + (1 - keep) * own[tab[1, items + b], rows]

            @pl.when(z < last)
            def _():
                down_staged(items + b, r).start()

        loop(0, PARTS, visit)

    def update_pair(jj):
        for d in range(CORES):
            side = pl.ds(d * part, part)
            u_high[:, side], u_rest[:, side] = split(pos[CORES * jj + d, :, mine])

        def visit(t):
            rows = pl.ds(pl.multiple_of(t * half, half), half)
            value = product(low_high[0, rows], low_rest[0, rows], u_high[...], u_rest[...])
            for d in range(CORES):
                s = CORES * jj + d

                @pl.when(carried(s))
                def _():
                    own[s, rows] -= tab[0, s].astype(jnp.float32) * value[:, d * part:(d + 1) * part]

        loop(0, CORES, visit)
        hand_back(jj).start()

    def keep_own(jj):
        acc[:, part_of(jj, core)] = own[CORES * jj + core]

    end = slots - 1
    late_slots = [end] + [slots + b for b in range(lanes) if items + 1 + b == end]
    side_groups = GROUPS // 2
    depth = width // 2

    def multiply(s, side):
        k = 1 - tab[0, s]
        deep = pl.ds(pl.multiple_of(side * depth, depth), depth)
        u_high[deep], u_rest[deep] = split(pos[s, deep])
        for t in range(CORES):
            rows = pl.ds(t * half, half)
            value = product(low_high[k, rows, deep], low_rest[k, rows, deep], u_high[deep], u_rest[deep])
            prod[s, rows] = value + jnp.where(side > 0, prod[s, rows], 0.0)

    def work(w):
        o, side = lax.div(w, 2), lax.rem(w, 2)
        later = o - items - 1
        turn = jnp.where(lax.rem(later, 2) == 0, slots, items + 1) + lax.div(later, 2)
        s = jnp.where(later < 0, o, jnp.where(later < 2 * lanes, turn, o - lanes))

        @pl.when(carried(s))
        def _():
            @pl.when(jnp.logical_not(first_chip & (s < CORES * per_block)))
            def _():
                for i in range(side_groups):
                    forward(s, side * side_groups + i).wait_recv()

            multiply(s, side)

    def arrive(s, g, relays=True):
        for i in range(PARTS // GROUPS):
            r = g * (PARTS // GROUPS) + i
            landed(s, r).wait_recv()
            if relays:
                @pl.when(z < last)
                def _():
                    down_relay(s, r).start()

                for b in range(lanes):
                    @pl.when(s == items + b)
                    def _():
                        give_back(b, r).start()
        forward(s, g).start()

    def arrive_pair(jj, begin=0, finish=GROUPS):
        def visit(g):
            for d in range(CORES):
                s = CORES * jj + d

                @pl.when(carried(s))
                def _():
                    arrive(s, g)

        loop(begin, finish, visit)

    def take_guest(b):
        loop(0, GROUPS, lambda g: arrive(slots + b, g, False))

    units = GROUPS * (slots - items)
    goal, span = 2 * (end + min(slots - items - 2, lanes)), units - GROUPS + 1

    def limit(i):
        s, g = items + lax.div(i, GROUPS), lax.rem(i, GROUPS)
        b = s - items - 1
        guest = jnp.where((b >= 0) & (b < lanes), 2, 0)
        late = jnp.where(g >= side_groups, guest, 0) + jnp.where(g == GROUPS - 1, 1, 0)
        whole = 2 * (s + jnp.minimum(jnp.maximum(b, 0), lanes)) + late
        paced = jnp.where(i < span, jnp.minimum(whole, lax.div((i + 1) * goal, span)), whole)
        return jnp.where(i < units, paced, 2 * (slots + lanes))

    def settle(begin):
        def visit(t):
            jj, rows = lax.div(t, PARTS), rows_of(lax.rem(t, PARTS))
            place = tab[2, jj]
            ready = tab[3, jj] > 0
            for s in late_slots:
                ready = ready & (place != s)
            upper = jnp.where(tab[4, jj] > 0, prod[CORES * jj + core, rows], 0.0)
            acc[rows, columns_of(jj)] -= upper + jnp.where(ready, prod[place, rows], 0.0)

        loop(begin * chunks * PARTS // 2, (begin + 1) * chunks * PARTS // 2, visit)

    def settle_late():
        def visit(t):
            rows = rows_of(t)
            values = [prod[s, rows] for s in late_slots]
            for jj in range(chunks):
                flags = [jnp.where(tab[2, jj] == s, tab[3, jj], 0).astype(jnp.float32) for s in late_slots]
                acc[rows, columns_of(jj)] -= functools.reduce(jnp.add, [f * v for f, v in zip(flags, values)])

        loop(0, PARTS, visit)

    def make_lower():
        gather_pivot(0)
        pltpu.make_async_copy(mat.at[own_rows(), pl.ds(0, width)], a.at[core], a_own).wait()
        swapped_columns().wait_recv()
        apply_pivot(0, a[0])

    @pl.when(active & first_chip)
    def _():
        relay_pivot(0)
        relay_pivot(1)

    @pl.when(z == 1)
    def _():
        for jj in range(chunks):
            own[CORES * jj + core] = acc[:, part_of(jj, core)]
            swapped_own(jj).wait_recv()

        steps = chunks * GROUPS
        updates = [2 * GROUPS + 2, 2 * GROUPS + 3, 3 * GROUPS + 1, steps]

        def visit(t):
            @pl.when(t < steps)
            def _():
                begin = lax.rem(t, GROUPS) * (PARTS // GROUPS)
                stage_pair(lax.div(t, GROUPS), begin, begin + PARTS // GROUPS)

            @pl.when((t == 1) & first_chip)
            def _():
                make_lower()

            @pl.when(t == 2 * GROUPS - 2)
            def _():
                relay_lower(0)

            @pl.when(t == 2 * GROUPS + 1)
            def _():
                take_lower(0)

            @pl.when(t == steps)
            def _():
                stage_guest(0)

            @pl.when(functools.reduce(jnp.logical_or, [t == u for u in updates]))
            def _():
                update_pair(sum(jnp.where(t > u, 1, 0) for u in updates))

            @pl.when(t == updates[1])
            def _():
                for b in range(lanes):
                    out_guest[b] = own[item_of((x_out if b % 2 else 0) + b // 2)]
                    export(b).start()

        loop(0, steps + 1, visit)
        for b in range(1, lanes):
            stage_guest(b)
        loop(items + lanes, slots, stage_late)
        for jj in range(chunks):
            hand_back(jj).wait_recv()
            swap_own(jj).wait_send()
            acc[:, part_of(jj, 1 - core)] = back[jj]
            keep_own(jj)
        store_lower(0)

    @pl.when(both)
    def _():
        pl.when(first_chip)(make_lower)
        loop(0, per_block - 1, arrive_pair)
        arrive_pair(per_block - 1, 0, side_groups)
        relay_lower(0)
        arrive_pair(per_block - 1, side_groups, GROUPS)

        @pl.when(first_chip)
        def _():
            gather_pivot(1)
            live = tab[0, 1].astype(jnp.float32)
            left = split(low[0, own_rows()])

            def visit(q):
                for g in range(GROUPS):
                    forward(CORES * q + 1, g).wait_recv()
                a[1, :, columns_of(q)] -= live * product(*left, *split(pos[CORES * q + 1]))

            loop(0, per_block, visit)
            apply_pivot(1, a[1])

        loop(per_block, chunks - 1, arrive_pair)
        take_lower(0)
        arrive_pair(chunks - 1, 0, 1)
        relay_lower(1)
        arrive_pair(chunks - 1, 1, GROUPS)
        take_lower(1)

        def unit(i):
            @pl.when(i < units)
            def _():
                arrive(items + lax.div(i, GROUPS), lax.rem(i, GROUPS))

            start = jnp.where(i > 0, limit(i - 1), 0)

            b = lax.div(i, GROUPS) - 1

            @pl.when((i < units) & (b >= 0) & (b < lanes) & (lax.rem(i, GROUPS) == side_groups))
            def _():
                take_guest(b)

            loop(start, limit(i), work)
            for half_of in range(2):
                pl.when(i == units - GROUPS + half_of)(functools.partial(settle, half_of))

        loop(0, units + 1, unit)
        settle_late()
        for k in range(2):
            store_lower(k)

    def each_carried(visit):
        def one_slot(s):
            @pl.when(carried(s))
            def _():
                visit(s)

        loop(0, slots, one_slot)

    @pl.when(z == 0)
    def _():
        loop(jnp.where(first_chip, per_block, 0), chunks, upper_sent)

    @pl.when(z == 1)
    def _():
        for jj in range(chunks):
            hand_back(jj).wait_send()
        for b in range(lanes):
            export(b).wait_send()

        @pl.when(z < last)
        def _():
            each_carried(lambda s: slot_sent(s, d_send.at[s]))

    @pl.when(both)
    def _():
        for b in range(lanes):
            slot_sent(slots + b, r_send.at[b])
            slot_sent(slots + b, f_send.at[slots + b])
        each_carried(lambda s: slot_sent(s, f_send.at[s]))

        @pl.when(z < last)
        def _():
            each_carried(lambda s: slot_sent(s, d_send.at[s]))

    @pl.when(first_chip)
    def _():
        for k in range(2):
            @pl.when(z < last)
            def _():
                pivot_send(k, z + 1, p_send.at[k, z]).wait_send()

            @pl.when(z - 1 > k)
            def _():
                pivot_send(k, z - 1, p_up.at[k]).wait_send()

            finish_pivot(k)

    @pl.when(first_chip & (z == 1))
    def _():
        pivot_own(1).wait()

    for k in range(2):
        @pl.when(z > k)
        def _():
            lower_pass(k).wait_send()

            @pl.when(first_chip)
            def _():
                for target in direct:
                    for q in range(2):
                        lower_send(k, target, q).wait_send()
                if k == 0:
                    swap_columns().wait_send()

            for q in range(2):
                @pl.when(member == 1 + q)
                def _():
                    lower_send(k, chip + 2 - q, q).wait_send()


def sparse(arm, n_row, n_col, plan, matrix, pivot_inverse, row_live, col_live):
    rows, columns = matrix.shape
    panels, rows_own, width = pivot_inverse.shape
    chunk = min(CHUNK, width)
    chunks = columns // chunk
    items = CORES * chunks
    slots = items + 2 + arm
    lanes = min(4, slots - items - 1)
    part = chunk // CORES
    n_chip = n_col // CORES
    f32, bf16, dma = jnp.float32, jnp.bfloat16, pltpu.SemaphoreType.DMA
    return pl.pallas_call(
        functools.partial(sparse_kernel, slots, n_row, n_col, chunk),
        out_shape=pltpu.VMEM((rows, columns), f32),
        in_specs=[pl.BlockSpec(memory_space=pltpu.HBM)] * 5,
        out_specs=pl.BlockSpec(memory_space=pltpu.VMEM),
        scratch_shapes=[
            pltpu.SMEM(row_live.shape, jnp.int32),
            pltpu.SMEM(col_live.shape, jnp.int32),
            pltpu.SMEM(plan.shape, jnp.int32),
            pltpu.SMEM((5, slots + lanes), jnp.int32),
            pltpu.VMEM((slots + lanes, width, chunk), f32),
            pltpu.VMEM((slots + lanes, width, chunk), f32),
            pltpu.VMEM((slots, width, part), f32),
            pltpu.VMEM((items, width, part), f32),
            pltpu.VMEM((lanes, width, part), f32),
            pltpu.VMEM((lanes, width, part), f32),
            pltpu.VMEM((chunks, width, part), f32),
            pltpu.VMEM((panels, width, width), f32),
            pltpu.VMEM((CORES, width // CORES, width), f32),
            pltpu.VMEM((panels, width, width), f32),
            pltpu.VMEM((panels, width, width), bf16),
            pltpu.VMEM((panels, width, width), bf16),
            pltpu.VMEM((width, chunk), bf16),
            pltpu.VMEM((width, chunk), bf16),
            dma((chunks,)), dma((3,)),
            dma((slots + lanes,)), dma((slots + lanes, PARTS)),
            dma((slots + lanes,)), dma((slots + lanes, GROUPS)),
            dma((lanes,)), dma((lanes,)), dma((lanes,)),
            dma((chunks,)), dma((chunks,)), dma((chunks,)), dma((chunks,)),
            dma((panels, n_row)), dma((panels, n_row)), dma((panels, n_row)), dma((panels, n_row)),
            dma((panels,)), dma, dma, dma,
            dma((panels, n_chip, 2)), dma((panels, 2)), dma((panels,)), dma((panels,)), dma((panels,)),
            pltpu.SemaphoreType.REGULAR,
        ],
        compiler_params=pltpu.CompilerParams(
            collective_id=1 + arm, has_side_effects=True, vmem_limit_bytes=GRANT - 4 * rows * columns
        ),
    )(row_live, col_live, plan, matrix, pivot_inverse)


def per_device(n_row, n_col, matrix, pivot_inverse, row_live, col_live):
    width = pivot_inverse.shape[2]
    chunk = min(CHUNK, width)
    chunks, per_block = matrix.shape[1] // chunk, width // chunk
    smem = pl.BlockSpec(memory_space=pltpu.SMEM)
    plan = pl.pallas_call(
        functools.partial(plan_kernel, n_row, n_col, chunks, per_block),
        out_shape=jax.ShapeDtypeStruct((1 + 2 * n_col,), jnp.int32),
        in_specs=[smem, smem],
        out_specs=smem,
    )(row_live, col_live)
    arms = [functools.partial(sparse, arm, n_row, n_col) for arm in range(ARMS)]
    arms.append(functools.partial(dense, n_row, n_col))
    return lax.switch(plan[0], arms, plan, matrix, pivot_inverse, row_live, col_live)


def solution(mesh):
    n_row, n_col = mesh.shape["prow"], mesh.shape["pcol"]
    return jax.shard_map(
        functools.partial(per_device, n_row, n_col),
        mesh=mesh,
        in_specs=(P("prow", "pcol"), P(None, "prow", None), P(), P()),
        out_specs=P("prow", "pcol"),
        check_vma=False,
    )
```
